32 devices in a mesh: groups: 2 (over y), seq: 4 (over z), chan: 4 (over x, core).
Axes of the slice: x: 2, y: 2, z: 4, core: 2. Of those that a mesh axis runs over, the one named last changes fastest.
Arguments:
- query_in: bfloat16 [4096, 4096], P(('groups', 'seq'), 'chan'), parts along dimension 0, may hold values from -6 to 6
- key_in: bfloat16 [4096, 4096], P(('groups', 'seq'), 'chan'), parts along dimension 0, may hold values from -6 to 6
- value_in: bfloat16 [4096, 4096], P(('groups', 'seq'), 'chan'), parts along dimension 0, may hold values from -6 to 6
- out_grad: bfloat16 [4096, 4096], P(('groups', 'seq'), 'chan'), parts along dimension 0, may hold values from -6 to 6
- document_rows: int32 [16], P('groups'), parts along dimension 0, may hold values from 1 to 8, 16 in all
- long_filter: float32 [1024, 4096], P(None, 'chan'), may hold values from -0.375 to 0.375
Outputs:
- query_grad: bfloat16 [4096, 4096], P(('groups', 'seq'), 'chan'), parts along dimension 0
- key_grad: bfloat16 [4096, 4096], P(('groups', 'seq'), 'chan'), parts along dimension 0
- value_grad: bfloat16 [4096, 4096], P(('groups', 'seq'), 'chan'), parts along dimension 0
- filter_grad: float32 [2048, 4096], P(('groups', 'seq'), 'chan'), parts along dimension 0
The draws below stay inside these ranges and needn't reach their ends.
There are 2 independent parts, one for each index of `groups`. The reference program is written for one: setup_inputs(seed, part) draws one part's arguments, and reference() takes and returns one part's arrays. A program takes and returns all parts, laid end to end along the dimension named above; an argument that names none is the same for every part. Nothing has to cross between parts.
Inputs may be any that keep to these rules, and one draw needn't show every extreme that they name: `document_rows`: the lengths sum to 16; one of them is exactly 8.
All inputs are finite; a program needn't handle non-finite values.
Results may differ from the reference program's by a relative error of at most 0.001.
Values sent between devices are 32-bit elements; how exact they have to be, the bound alone decides.
No kernel may reach another device: no remote copies, remote signals or barrier semaphores. Data moves between devices by JAX's collectives and lax.ppermute only.
A program may use at most 192 MiB of HBM per device.

```python
import math
import jax
import jax.numpy as jnp
import numpy as np
from jax import lax

D = 4096
ROW = 128
MOST = 8
TOTAL_ROWS = 16
TOKENS = 2048
NDOC = 8
FLEN = 1024


def block_scale(rng, extent, split, least, high):
    factor_of, own = 1.0, jax.random.fold_in(rng, 6)
    for position, blocks in split:
        heights = jnp.exp(jax.random.uniform(jax.random.fold_in(own, position), (blocks,), jnp.float32, least / len(split), high / len(split)))
        factor_of = factor_of * jnp.repeat(heights, extent[position] // blocks).reshape([-1 if axis == position else 1 for axis in range(len(extent))])
    return factor_of


def profile(amount, total, limit, skew):
    loads = [(1 << 20) // math.isqrt(grade ** skew) + 1 for grade in range(2, amount + 1)]
    spare, given = total - limit - (amount - 1), [1] * (amount - 1)
    while spare > 0:
        candidates = [i for i in range(amount - 1) if given[i] < limit]
        mass, budget = sum([loads[i] for i in candidates]), spare
        for i in candidates:
            extra = min(limit - given[i], max(1, budget * loads[i] // mass), spare)
            given[i] = given[i] + extra
            spare = spare - extra
    return np.array([limit] + given)


def ragged_sizes(rng, number_of, total, bound, lean):
    if number_of == 2:
        one = jax.random.randint(rng, (), max(1, total - bound), min(bound, total - 1) + 1)
        return jnp.stack([one, total - one])
    sizes = jnp.asarray(profile(number_of, total, bound, lean), jnp.int32)
    couples = (number_of - 1) // 2
    donor, sink = sizes[1:1 + 2 * couples:2], sizes[2:2 + 2 * couples:2]
    slack = jnp.minimum(donor - 1, bound - sink)
    shifted = jax.random.randint(jax.random.fold_in(rng, 1), (couples,), 0, 1 << 20) % (slack + 1)
    sizes = sizes.at[1:1 + 2 * couples:2].set(donor - shifted).at[2:2 + 2 * couples:2].set(sink + shifted)
    return sizes[jax.random.permutation(jax.random.fold_in(rng, 2), number_of)]


def scatter_about(own_key, shape, spread, most, cuts=(), held_as=jnp.bfloat16):
    drawn = spread * jax.random.normal(own_key, shape, jnp.float32)
    if cuts:
        drawn = drawn * block_scale(own_key, shape, cuts, -0.22, 0.18)
    return jnp.clip(drawn, -most, most).astype(held_as)


def setup_inputs(seed: int = 0, part: int = 0) -> dict:
    seeds = jax.random.split(jax.random.key(seed), 7)
    own_keys = jax.random.split(jax.random.fold_in(seeds[6], part), 7)
    return {
        "query_in": scatter_about(own_keys[0], (TOKENS, D), 1.0, 6.0, ((0, 4), (1, 4))),
        "key_in": scatter_about(own_keys[1], (TOKENS, D), 1.0, 6.0, ((0, 4), (1, 4))),
        "value_in": scatter_about(own_keys[2], (TOKENS, D), 1.0, 6.0, ((0, 4), (1, 4))),
        "out_grad": scatter_about(own_keys[3], (TOKENS, D), 1.0, 6.0, ((0, 4), (1, 4))),
        "document_rows": ragged_sizes(own_keys[4], NDOC, TOTAL_ROWS, MOST, 2).astype(jnp.int32),
        "long_filter": scatter_about(seeds[5], (FLEN, D), (FLEN // 4) ** -0.5, 0.375, ((1, 4),), jnp.float32),
    }


def reference(query_in, key_in, value_in, out_grad, document_rows, long_filter):
    row_count = TOKENS // ROW
    block_width = min(D, 512)
    block_count = D // block_width
    document_ends = jnp.cumsum(document_rows).astype(jnp.int32)
    row_index = jnp.arange(row_count, dtype=jnp.int32)
    document_index = lax.optimization_barrier(jnp.sum((document_ends[None, :] <= row_index[:, None]).astype(jnp.int32), axis=1)).astype(jnp.int32)
    padded_documents = jnp.concatenate([jnp.full((MOST,), -1, jnp.int32), document_index, jnp.full((MOST,), -2, jnp.int32)])
    next_same = jnp.concatenate([document_index[:-1] == document_index[1:], jnp.zeros((1,), bool)])
    prev_same = jnp.concatenate([jnp.zeros((1,), bool), document_index[1:] == document_index[:-1]])

    def split_channels(array):
        return array.reshape(array.shape[0], block_count, block_width).transpose(1, 0, 2)

    def join_channels(array):
        return array.transpose(1, 0, 2).reshape(array.shape[1], D)

    def one_block(pieces):
        query_part, key_part, value_part, grad_part, filter_part = pieces
        mixed = (key_part.astype(jnp.float32) * value_part.astype(jnp.float32)).reshape(row_count, ROW, block_width)
        upstream = (grad_part.astype(jnp.float32) * query_part.astype(jnp.float32)).reshape(row_count, ROW, block_width)
        filter_spec = jnp.fft.rfft(filter_part.reshape(MOST, ROW, block_width), n=2 * ROW, axis=1)
        mixed_spec = jnp.fft.rfft(mixed, n=2 * ROW, axis=1)
        mixed_pad = jnp.concatenate([jnp.zeros((MOST,) + mixed_spec.shape[1:], mixed_spec.dtype), mixed_spec])
        summed = jnp.zeros_like(mixed_spec)
        for offset in range(MOST):
            same_doc = padded_documents[MOST - offset:MOST - offset + row_count] == document_index
            summed = summed + jnp.where(same_doc[:, None, None], mixed_pad[MOST - offset:MOST - offset + row_count] * filter_spec[offset], 0.0)
        wide = jnp.fft.irfft(summed, n=2 * ROW, axis=1)
        spill = jnp.concatenate([jnp.zeros((1, ROW, block_width), wide.dtype), wide[:-1, ROW:]])
        convolved = wide[:, :ROW] + jnp.where(prev_same[:, None, None], spill, 0.0)
        later_rows = jnp.concatenate([upstream[1:], jnp.zeros((1, ROW, block_width), upstream.dtype)])
        grad_in = jnp.concatenate([upstream, jnp.where(next_same[:, None, None], later_rows, 0.0)], axis=1)
        grad_spec = jnp.fft.rfft(grad_in, axis=1)
        grad_pad = jnp.concatenate([grad_spec, jnp.zeros((MOST,) + grad_spec.shape[1:], grad_spec.dtype)])
        backward = jnp.zeros_like(grad_spec)
        filter_terms = []
        for offset in range(MOST):
            same_doc = padded_documents[MOST + offset:MOST + offset + row_count] == document_index
            later = grad_pad[offset:offset + row_count]
            backward = backward + jnp.where(same_doc[:, None, None], later * jnp.conj(filter_spec[offset]), 0.0)
            filter_terms.append(lax.optimization_barrier(jnp.sum(jnp.where(same_doc[:, None, None], later * jnp.conj(mixed_spec), 0.0), axis=0)))
        mixed_grad = jnp.fft.irfft(backward, n=2 * ROW, axis=1)[:, :ROW].reshape(TOKENS, block_width)
        filter_grad = jnp.fft.irfft(jnp.stack(filter_terms), n=2 * ROW, axis=1)[:, :ROW].reshape(FLEN, block_width)
        filter_grad = filter_grad / math.sqrt(TOKENS)
        query_grad = (grad_part.astype(jnp.float32) * convolved.reshape(TOKENS, block_width)).astype(jnp.bfloat16)
        key_grad = (mixed_grad * value_part.astype(jnp.float32)).astype(jnp.bfloat16)
        value_grad = (mixed_grad * key_part.astype(jnp.float32)).astype(jnp.bfloat16)
        return (query_grad, key_grad, value_grad, filter_grad.astype(long_filter.dtype))
    results = lax.map(one_block, (split_channels(query_in), split_channels(key_in), split_channels(value_in), split_channels(out_grad), split_channels(long_filter)))
    return (join_channels(results[0]), join_channels(results[1]), join_channels(results[2]), join_channels(results[3]))
```

```python
import math

import jax
import jax.numpy as jnp
import ml_dtypes
import numpy as np
from jax import lax
from jax.experimental import pallas as pl
from jax.experimental.pallas import tpu as pltpu
from jax.sharding import PartitionSpec as P

ROW = 128
MOST = 8
HALF = ROW // 2
OWN = 4


def split_table(table):
    high = table.astype(ml_dtypes.bfloat16)
    low = (table - high.astype(np.float64)).astype(ml_dtypes.bfloat16)
    return high, low


def dft_tables():
    order = np.concatenate([np.arange(0, ROW, 2), np.arange(1, ROW, 2)])
    phase = np.outer(2 * order + 1, np.arange(ROW)) % (4 * ROW) * (math.pi / (2 * ROW))
    forward = np.concatenate([np.cos(phase), -np.sin(phase)], axis=0)
    high, low = split_table(forward)
    inv_high, inv_low = split_table(forward.T / ROW)
    return (
        np.concatenate([high, high], axis=1),
        low,
        inv_high,
        inv_low,
    )


def halves(value):
    high = value.astype(jnp.bfloat16)
    low = (value - high.astype(jnp.float32)).astype(jnp.bfloat16)
    return high, low


def matmul(one, two):
    return jnp.dot(one, two, preferred_element_type=jnp.float32)


def transform(signal, forward_ref, forward_low_ref):
    high, low = halves(signal)
    return matmul(forward_ref[...], jnp.concatenate([high, low], axis=0)) + matmul(
        forward_low_ref[...], high
    )


def untransform(spectrum, inverse_ref, inverse_low_ref):
    high, low = halves(spectrum)
    return (
        matmul(inverse_ref[...], high)
        + matmul(inverse_ref[...], low)
        + matmul(inverse_low_ref[...], high)
    )


def turned(spectrum, sign):
    real, imag = spectrum[:ROW], spectrum[ROW:]
    plus = lambda part: jnp.concatenate([part[:HALF], -part[HALF:]], axis=0)
    minus = lambda part: jnp.concatenate([-part[:HALF], part[HALF:]], axis=0)
    if sign > 0:
        return jnp.concatenate([minus(imag), plus(real)], axis=0)
    return jnp.concatenate([plus(imag), minus(real)], axis=0)


def filter_kernel(
    table_ref,
    forward_ref,
    forward_low_ref,
    inverse_ref,
    inverse_low_ref,
    behind_ref,
    own_ref,
    grad_ref,
    ahead_ref,
    out_ref,
    mixed_spec,
    grad_spec,
    near,
    back,
    front,
):
    for row in range(OWN):
        rows = pl.ds(row * ROW, ROW)
        mixed_spec[row] = transform(behind_ref[rows, :], forward_ref, forward_low_ref)
        mixed_spec[OWN + row] = transform(own_ref[rows, :], forward_ref, forward_low_ref)
        grad_spec[row] = transform(grad_ref[rows, :], forward_ref, forward_low_ref)
        grad_spec[OWN + row] = transform(ahead_ref[rows, :], forward_ref, forward_low_ref)
    near[...] = jnp.zeros_like(near)
    back[...] = jnp.zeros_like(back)
    front[...] = jnp.zeros_like(front)

    def accumulate(total, source, first, last):
        @pl.loop(first, last)
        def _(offset):
            later = source - OWN + offset
            for part in range(4):
                real = pl.ds(part * 32, 32)
                imag = pl.ds(ROW + part * 32, 32)
                one_re, one_im = mixed_spec[source, real, :], mixed_spec[source, imag, :]
                two_re, two_im = grad_spec[later, real, :], grad_spec[later, imag, :]
                total[offset, real, :] += one_re * two_re + one_im * two_im
                total[offset, imag, :] += one_re * two_im - one_im * two_re

    for source in range(2 * OWN):
        stop = table_ref[2 * OWN + source]
        if source < OWN:
            accumulate(back, source, OWN - source, jnp.minimum(stop, 2 * OWN - source))
            accumulate(near, source, 2 * OWN - source, jnp.minimum(stop, MOST))
        else:
            accumulate(near, source, 0, jnp.minimum(stop, 2 * OWN - source))
            accumulate(
                front, source, 2 * OWN - source, jnp.minimum(stop, min(MOST, 3 * OWN - source))
            )
    for block in range(MOST):
        use_back = table_ref[4 * OWN + block].astype(jnp.float32)
        use_front = table_ref[4 * OWN + MOST + block].astype(jnp.float32)

        def gathered(offset):
            return near[offset] + use_back * back[offset] + use_front * front[offset]

        spectrum = gathered(block)
        if block + 1 < MOST:
            spectrum = spectrum + turned(gathered(block + 1), -1)
        out_ref[pl.ds(block * ROW, ROW), :] = untransform(spectrum, inverse_ref, inverse_low_ref)


def token_kernel(
    table_ref,
    forward_ref,
    forward_low_ref,
    inverse_ref,
    inverse_low_ref,
    far_behind_ref,
    behind_ref,
    own_ref,
    grad_ref,
    ahead_ref,
    far_ahead_ref,
    filter_ref,
    key_ref,
    value_ref,
    out_grad_ref,
    query_grad_ref,
    key_grad_ref,
    value_grad_ref,
    mixed_spec,
    grad_spec,
    filter_spec,
):
    far = MOST - 1 - OWN

    def spectrum_of(ref, row):
        return transform(ref[pl.ds(row * ROW, ROW), :], forward_ref, forward_low_ref)

    for row in range(far):
        mixed_spec[row] = spectrum_of(far_behind_ref, row)
        grad_spec[2 * OWN + row] = spectrum_of(far_ahead_ref, row)
    for row in range(OWN):
        mixed_spec[far + row] = spectrum_of(behind_ref, row)
        mixed_spec[far + OWN + row] = spectrum_of(own_ref, row)
        grad_spec[row] = spectrum_of(grad_ref, row)
        grad_spec[OWN + row] = spectrum_of(ahead_ref, row)
    before = None
    for offset in range(MOST):
        plain = spectrum_of(filter_ref, offset)
        filter_spec[offset] = plain if before is None else plain + turned(before, 1)
        before = plain

    width = own_ref.shape[1]
    for row in range(OWN):
        rows = pl.ds(row * ROW, ROW)
        real_parts, imag_parts, real_back, imag_back = [], [], [], []
        for part in range(4):
            real = pl.ds(part * 32, 32)
            imag = pl.ds(ROW + part * 32, 32)
            nothing = (jnp.zeros((32, width), jnp.float32),) * 2

            def forward_step(offset, totals):
                one = far + OWN + row - offset
                one_re, one_im = mixed_spec[one, real, :], mixed_spec[one, imag, :]
                two_re, two_im = filter_spec[offset, real, :], filter_spec[offset, imag, :]
                return (
                    totals[0] + (one_re * two_re - one_im * two_im),
                    totals[1] + (one_re * two_im + one_im * two_re),
                )

            def backward_step(offset, totals):
                one = row + offset
                one_re, one_im = grad_spec[one, real, :], grad_spec[one, imag, :]
                two_re, two_im = filter_spec[offset, real, :], filter_spec[offset, imag, :]
                return (
                    totals[0] + (two_re * one_re + two_im * one_im),
                    totals[1] + (two_re * one_im - two_im * one_re),
                )

            total = lax.fori_loop(0, jnp.minimum(table_ref[row], MOST), forward_step, nothing)
            real_parts.append(total[0])
            imag_parts.append(total[1])
            total = lax.fori_loop(0, jnp.minimum(table_ref[OWN + row], MOST), backward_step, nothing)
            real_back.append(total[0])
            imag_back.append(total[1])
        convolved = untransform(
            jnp.concatenate(real_parts + imag_parts, axis=0), inverse_ref, inverse_low_ref
        )
        mixed_grad = untransform(
            jnp.concatenate(real_back + imag_back, axis=0), inverse_ref, inverse_low_ref
        )
        query_grad_ref[rows, :] = (
            out_grad_ref[rows, :].astype(jnp.float32) * convolved
        ).astype(jnp.bfloat16)
        key_grad_ref[rows, :] = (
            mixed_grad * value_ref[rows, :].astype(jnp.float32)
        ).astype(jnp.bfloat16)
        value_grad_ref[rows, :] = (
            mixed_grad * key_ref[rows, :].astype(jnp.float32)
        ).astype(jnp.bfloat16)


def scalars(document_rows, first_row, owner_split):
    count = document_rows.shape[0]
    index = jnp.arange(count, dtype=jnp.int32)
    ends = jnp.sum(
        jnp.where(index[None, :] <= index[:, None], document_rows[None, :], 0), axis=1
    )
    row = first_row + jnp.arange(-OWN, OWN, dtype=jnp.int32)
    passed = ends[None, :] <= row[:, None]
    starts = jnp.max(jnp.where(passed, ends[None, :], 0), axis=1)
    stops = jnp.min(jnp.where(passed, jnp.int32(1 << 20), ends[None, :]), axis=1)
    ahead = jnp.where(row >= 0, stops - row, 0)
    behind = row + 1 - starts
    seq = first_row // OWN
    block = jnp.arange(MOST, dtype=jnp.int32)
    if owner_split:
        owner = block * owner_split // MOST
        use_back = (owner >= seq).astype(jnp.int32)
        use_front = (owner <= seq).astype(jnp.int32)
    else:
        use_back = jnp.ones_like(block)
        use_front = jnp.zeros_like(block)
    return jnp.concatenate([behind[OWN:], ahead[OWN:], ahead, use_back, use_front])


def step(rows, by):
    length = lax.axis_size("seq")
    return lax.ppermute(
        rows, "seq", [(i, i + by) for i in range(length) if 0 <= i + by < length]
    )


def reduced(partial, seq_count):
    if seq_count != 4:
        return lax.psum_scatter(partial, "seq", scatter_dimension=0, tiled=True)
    seq = lax.axis_index("seq")
    share = partial.shape[0] // 4
    part = [partial[share * i : share * (i + 1)] for i in range(4)]
    in_a1 = lax.ppermute(part[0], "seq", [(3, 2)])
    in_a2 = lax.ppermute(part[1], "seq", [(3, 2), (0, 1)])
    in_b1 = lax.ppermute(
        jnp.where(seq == 1, part[3], part[0] + in_a1), "seq", [(1, 2), (2, 1)]
    )
    in_b2 = lax.ppermute(
        jnp.where(seq == 1, part[2], part[1] + in_a2), "seq", [(1, 2), (2, 1)]
    )
    in_b3 = lax.ppermute(
        jnp.where(seq == 2, part[3], part[0]) + in_b1, "seq", [(2, 3), (1, 0)]
    )
    own = lax.dynamic_slice_in_dim(partial, seq * share, share, axis=0)
    return own + in_b2 + in_b3 + jnp.where(seq == 1, in_a2, 0.0)


def body(query_in, key_in, value_in, out_grad, document_rows, long_filter):
    seq_count = lax.axis_size("seq")
    tokens, channels = query_in.shape
    total_rows = tokens // ROW * seq_count
    wide = jnp.float32
    mixed = key_in.astype(wide) * value_in.astype(wide)
    upstream = out_grad.astype(wide) * query_in.astype(wide)
    behind = step(mixed, 1)
    ahead = step(upstream, -1)
    far = (MOST - 1 - OWN) * ROW
    far_behind = step(behind[tokens - far :], 1)
    far_ahead = step(ahead[:far], -1)

    first_row = lax.axis_index("seq") * OWN
    table = scalars(document_rows, first_row, 4 if seq_count == 4 else 0)
    tables = dft_tables()

    tile = min(channels, 256)
    smem = pl.BlockSpec(memory_space=pltpu.SMEM)
    fixed = [pl.BlockSpec(t.shape, lambda j: (0, 0)) for t in tables]
    column = lambda rows: pl.BlockSpec((rows, tile), lambda j: (0, j))
    params = pltpu.CompilerParams(vmem_limit_bytes=48 * 1024 * 1024)
    partial = pl.pallas_call(
        filter_kernel,
        grid=(channels // tile,),
        in_specs=[smem] + fixed + [column(tokens)] * 4,
        out_specs=column(MOST * ROW),
        out_shape=jax.ShapeDtypeStruct((MOST * ROW, channels), wide),
        scratch_shapes=[pltpu.VMEM((2 * OWN, 2 * ROW, tile), wide)] * 2
        + [pltpu.VMEM((MOST, 2 * ROW, tile), wide)] * 3,
        compiler_params=params,
        cost_estimate=pl.CostEstimate(
            flops=14_000_000_000, bytes_accessed=13_000_000, transcendentals=0
        ),
        name="filter_terms",
    )(table, *tables, behind, mixed, upstream, ahead)
    filter_grad = reduced(partial, seq_count)

    query_grad, key_grad, value_grad = pl.pallas_call(
        token_kernel,
        grid=(channels // tile,),
        in_specs=[smem]
        + fixed
        + [column(far)]
        + [column(tokens)] * 4
        + [column(far), column(MOST * ROW)]
        + [column(tokens)] * 3,
        out_specs=[column(tokens)] * 3,
        out_shape=[jax.ShapeDtypeStruct((tokens, channels), jnp.bfloat16)] * 3,
        scratch_shapes=[pltpu.VMEM((2 * MOST - 1 - OWN, 2 * ROW, tile), wide)] * 2
        + [pltpu.VMEM((MOST, 2 * ROW, tile), wide)],
        compiler_params=params,
        cost_estimate=pl.CostEstimate(
            flops=25_000_000_000, bytes_accessed=24_000_000, transcendentals=0
        ),
        name="token_grads",
    )(
        table,
        *tables,
        far_behind,
        behind,
        mixed,
        upstream,
        ahead,
        far_ahead,
        long_filter,
        key_in,
        value_in,
        out_grad,
    )
    return query_grad, key_grad, value_grad, filter_grad * (1.0 / math.sqrt(total_rows * ROW))


def solution(mesh):
    tokens = P(("groups", "seq"), "chan")
    return jax.shard_map(
        body,
        mesh=mesh,
        in_specs=(tokens,) * 4 + (P("groups"), P(None, "chan")),
        out_specs=(tokens,) * 4,
        check_vma=False,
    )
```

```python
import math

import jax
import jax.numpy as jnp
import ml_dtypes
import numpy as np
from jax import lax
from jax.experimental import pallas as pl
from jax.experimental.pallas import tpu as pltpu
from jax.sharding import PartitionSpec as P

ROW = 128
MOST = 8
HALF = ROW // 2
OWN = 4
C0, C1, C2, C3 = 20_000_000_000, 10_000_000_000, 20_000_000_000, 1


def split_table(table):
    high = table.astype(ml_dtypes.bfloat16)
    low = (table - high.astype(np.float64)).astype(ml_dtypes.bfloat16)
    return high, low


def dft_tables():
    order = np.concatenate([np.arange(0, ROW, 2), np.arange(1, ROW, 2)])
    phase = np.outer(2 * order + 1, np.arange(ROW)) % (4 * ROW) * (math.pi / (2 * ROW))
    forward = np.concatenate([np.cos(phase), -np.sin(phase)], axis=0)
    high, low = split_table(forward)
    inv_high, inv_low = split_table(forward.T / ROW)
    return (
        np.concatenate([high, high], axis=1),
        low,
        inv_high,
        inv_low,
    )


def halves(value):
    high = value.astype(jnp.bfloat16)
    low = (value - high.astype(jnp.float32)).astype(jnp.bfloat16)
    return high, low


def matmul(one, two):
    return jnp.dot(one, two, preferred_element_type=jnp.float32)


def transform(signal, forward_ref, forward_low_ref):
    high, low = halves(signal)
    return matmul(forward_ref[...], jnp.concatenate([high, low], axis=0)) + matmul(
        forward_low_ref[...], high
    )


def untransform(spectrum, inverse_ref, inverse_low_ref):
    high, low = halves(spectrum)
    return (
        matmul(inverse_ref[...], high)
        + matmul(inverse_ref[...], low)
        + matmul(inverse_low_ref[...], high)
    )


def turned(spectrum, sign):
    real, imag = spectrum[:ROW], spectrum[ROW:]
    plus = lambda part: jnp.concatenate([part[:HALF], -part[HALF:]], axis=0)
    minus = lambda part: jnp.concatenate([-part[:HALF], part[HALF:]], axis=0)
    if sign > 0:
        return jnp.concatenate([minus(imag), plus(real)], axis=0)
    return jnp.concatenate([plus(imag), minus(real)], axis=0)


def multiply_add(total, offset, one_ref, one, two_ref, two):
    for part in range(4):
        real = pl.ds(part * 32, 32)
        imag = pl.ds(ROW + part * 32, 32)
        one_re, one_im = one_ref[one, real, :], one_ref[one, imag, :]
        two_re, two_im = two_ref[two, real, :], two_ref[two, imag, :]
        total[offset, real, :] += one_re * two_re + one_im * two_im
        total[offset, imag, :] += one_re * two_im - one_im * two_re


def own_kernel(
    table_ref,
    forward_ref,
    forward_low_ref,
    inverse_ref,
    inverse_low_ref,
    query_ref,
    key_ref,
    value_ref,
    out_grad_ref,
    filter_ref,
    mixed_spec,
    grad_spec,
    filter_spec,
    first_ref,
    second_ref,
    near,
):
    wide = jnp.float32
    for row in range(OWN):
        rows = pl.ds(row * ROW, ROW)
        mixed_spec[row] = transform(
            key_ref[rows, :].astype(wide) * value_ref[rows, :].astype(wide),
            forward_ref,
            forward_low_ref,
        )
        grad_spec[row] = transform(
            out_grad_ref[rows, :].astype(wide) * query_ref[rows, :].astype(wide),
            forward_ref,
            forward_low_ref,
        )
    near[...] = jnp.zeros_like(near)
    for source in range(OWN):
        stop = jnp.minimum(table_ref[3 * OWN + source], OWN - source)

        @pl.loop(0, stop)
        def _(offset):
            multiply_add(near, offset, mixed_spec, source, grad_spec, source + offset)

    for block in range(OWN):
        spectrum = near[block]
        if block + 1 < OWN:
            spectrum = spectrum + turned(near[block + 1], -1)
        out_ref = (first_ref, second_ref)[block // 2]
        out_ref[pl.ds(block % 2 * ROW, ROW), :] = untransform(
            spectrum, inverse_ref, inverse_low_ref
        )
    before = None
    for offset in range(MOST):
        plain = transform(filter_ref[pl.ds(offset * ROW, ROW), :], forward_ref, forward_low_ref)
        filter_spec[offset] = plain if before is None else plain + turned(before, 1)
        before = plain


def pair_kernel(
    table_ref,
    forward_ref,
    forward_low_ref,
    inverse_ref,
    inverse_low_ref,
    behind_tail_ref,
    behind_head_ref,
    ahead_head_ref,
    ahead_tail_ref,
    mixed_spec,
    grad_spec,
    first_ref,
    second_ref,
    behind_spec,
    ahead_spec,
    out_0,
    out_1,
    out_2,
    out_3,
    middle,
    back,
    front,
):
    def spectrum_of(ref, row):
        return transform(ref[pl.ds(row * ROW, ROW), :], forward_ref, forward_low_ref)

    behind_spec[0] = spectrum_of(behind_head_ref, 0)
    ahead_spec[OWN - 1] = spectrum_of(ahead_tail_ref, 0)
    for row in range(OWN - 1):
        behind_spec[row + 1] = spectrum_of(behind_tail_ref, row)
        ahead_spec[row] = spectrum_of(ahead_head_ref, row)
    middle[...] = jnp.zeros_like(middle)
    back[...] = jnp.zeros_like(back)
    front[...] = jnp.zeros_like(front)
    for source in range(OWN):
        stop = table_ref[2 * OWN + source]

        @pl.loop(OWN - source, jnp.minimum(stop, 2 * OWN - source))
        def _(offset):
            multiply_add(
                back, offset, behind_spec, source, grad_spec, source - OWN + offset
            )

        @pl.loop(2 * OWN - source, jnp.minimum(stop, MOST))
        def _(offset):
            multiply_add(
                middle, offset, behind_spec, source, ahead_spec, source - 2 * OWN + offset
            )

        stop = table_ref[3 * OWN + source]

        @pl.loop(OWN - source, jnp.minimum(stop, min(MOST, 2 * OWN - source)))
        def _(offset):
            multiply_add(
                front, offset, mixed_spec, source, ahead_spec, source - OWN + offset
            )

    outs = (out_0, out_1, out_2, out_3)
    for block in range(MOST):
        use_back = table_ref[4 * OWN + block].astype(jnp.float32)
        use_front = table_ref[4 * OWN + MOST + block].astype(jnp.float32)

        def gathered(offset):
            return middle[offset] + use_back * back[offset] + use_front * front[offset]

        spectrum = gathered(block)
        if block + 1 < MOST:
            spectrum = spectrum + turned(gathered(block + 1), -1)
        rows = pl.ds(block % 2 * ROW, ROW)
        taps = untransform(spectrum, inverse_ref, inverse_low_ref)
        if block < OWN:
            taps = taps + (first_ref, second_ref)[block // 2][rows, :]
        outs[block // 2][rows, :] = taps


def summed(table_ref, place, direction, pieces, filter_spec, width):
    reals, imags = [], []
    count = jnp.minimum(table_ref[place], MOST)
    for part in range(4):
        real = pl.ds(part * 32, 32)
        imag = pl.ds(ROW + part * 32, 32)
        total = (jnp.zeros((32, width), jnp.float32),) * 2
        for ref, first, low, high in pieces:

            def one_step(offset, totals):
                row = first + direction * offset
                one_re, one_im = ref[row, real, :], ref[row, imag, :]
                two_re, two_im = filter_spec[offset, real, :], filter_spec[offset, imag, :]
                if direction < 0:
                    return (
                        totals[0] + (one_re * two_re - one_im * two_im),
                        totals[1] + (one_re * two_im + one_im * two_re),
                    )
                return (
                    totals[0] + (two_re * one_re + two_im * one_im),
                    totals[1] + (two_re * one_im - two_im * one_re),
                )

            total = lax.fori_loop(low, jnp.minimum(count, high), one_step, total)
        reals.append(total[0])
        imags.append(total[1])
    return jnp.concatenate(reals + imags, axis=0)


def query_kernel(
    table_ref,
    forward_ref,
    forward_low_ref,
    inverse_ref,
    inverse_low_ref,
    far_ref,
    behind_spec,
    own_spec,
    filter_spec,
    out_grad_ref,
    query_grad_ref,
    far_spec,
):
    far = MOST - 1 - OWN
    for row in range(far):
        far_spec[row] = transform(
            far_ref[pl.ds(row * ROW, ROW), :], forward_ref, forward_low_ref
        )
    for row in range(OWN):
        rows = pl.ds(row * ROW, ROW)
        pieces = (
            (own_spec, row, 0, row + 1),
            (behind_spec, row + OWN, row + 1, row + 1 + OWN),
            (far_spec, row + OWN + far, row + 1 + OWN, MOST),
        )
        total = summed(table_ref, row, -1, pieces, filter_spec, far_ref.shape[1])
        convolved = untransform(total, inverse_ref, inverse_low_ref)
        query_grad_ref[rows, :] = (
            out_grad_ref[rows, :].astype(jnp.float32) * convolved
        ).astype(jnp.bfloat16)


def key_value_kernel(
    table_ref,
    forward_ref,
    forward_low_ref,
    inverse_ref,
    inverse_low_ref,
    far_ref,
    ahead_spec,
    own_spec,
    filter_spec,
    key_ref,
    value_ref,
    key_grad_ref,
    value_grad_ref,
    far_spec,
):
    far = MOST - 1 - OWN
    for row in range(far):
        far_spec[row] = transform(
            far_ref[pl.ds(row * ROW, ROW), :], forward_ref, forward_low_ref
        )
    for row in range(OWN):
        rows = pl.ds(row * ROW, ROW)
        pieces = (
            (own_spec, row, 0, OWN - row),
            (ahead_spec, row - OWN, OWN - row, 2 * OWN - row),
            (far_spec, row - 2 * OWN, 2 * OWN - row, MOST),
        )
        total = summed(table_ref, OWN + row, 1, pieces, filter_spec, far_ref.shape[1])
        mixed_grad = untransform(total, inverse_ref, inverse_low_ref)
        key_grad_ref[rows, :] = (
            mixed_grad * value_ref[rows, :].astype(jnp.float32)
        ).astype(jnp.bfloat16)
        value_grad_ref[rows, :] = (
            mixed_grad * key_ref[rows, :].astype(jnp.float32)
        ).astype(jnp.bfloat16)


def scalars(document_rows, first_row, owner_split):
    count = document_rows.shape[0]
    index = jnp.arange(count, dtype=jnp.int32)
    ends = jnp.sum(
        jnp.where(index[None, :] <= index[:, None], document_rows[None, :], 0), axis=1
    )
    row = first_row + jnp.arange(-OWN, OWN, dtype=jnp.int32)
    passed = ends[None, :] <= row[:, None]
    starts = jnp.max(jnp.where(passed, ends[None, :], 0), axis=1)
    stops = jnp.min(jnp.where(passed, jnp.int32(1 << 20), ends[None, :]), axis=1)
    ahead = jnp.where(row >= 0, stops - row, 0)
    behind = row + 1 - starts
    seq = first_row // OWN
    block = jnp.arange(MOST, dtype=jnp.int32)
    if owner_split:
        owner = block * owner_split // MOST
        use_back = (owner >= seq).astype(jnp.int32)
        use_front = (owner <= seq).astype(jnp.int32)
    else:
        use_back = jnp.ones_like(block)
        use_front = jnp.zeros_like(block)
    return jnp.concatenate([behind[OWN:], ahead[OWN:], ahead, use_back, use_front])


def step(rows, by):
    length = lax.axis_size("seq")
    return lax.ppermute(
        rows, "seq", [(i, i + by) for i in range(length) if 0 <= i + by < length]
    )


def reduced(early, parts, seq_count):
    if seq_count != 4:
        partial = jnp.concatenate(parts, axis=0)
        return lax.psum_scatter(partial, "seq", scatter_dimension=0, tiled=True)
    seq = lax.axis_index("seq")
    in_a1 = lax.ppermute(early[0], "seq", [(3, 2)])
    in_a2 = lax.ppermute(early[1], "seq", [(3, 2), (0, 1)])
    in_b1 = lax.ppermute(
        jnp.where(seq == 1, parts[3], parts[0] + in_a1), "seq", [(1, 2), (2, 1)]
    )
    in_b2 = lax.ppermute(
        jnp.where(seq == 1, parts[2], parts[1] + in_a2), "seq", [(1, 2), (2, 1)]
    )
    in_b3 = lax.ppermute(
        jnp.where(seq == 2, parts[3], parts[0]) + in_b1, "seq", [(2, 3), (1, 0)]
    )
    own = jnp.where(
        seq < 2,
        jnp.where(seq == 0, parts[0], parts[1] + in_a2),
        jnp.where(seq == 2, parts[2], parts[3]),
    )
    return own + in_b2 + in_b3


def body(query_in, key_in, value_in, out_grad, document_rows, long_filter):
    seq_count = lax.axis_size("seq")
    tokens, channels = query_in.shape
    total_rows = tokens // ROW * seq_count
    wide = jnp.float32
    far = (MOST - 1 - OWN) * ROW

    def mixed(low, high):
        return key_in[low:high].astype(wide) * value_in[low:high].astype(wide)

    def upstream(low, high):
        return out_grad[low:high].astype(wide) * query_in[low:high].astype(wide)

    behind_tail = step(mixed(ROW, tokens), 1)
    ahead_head = step(upstream(0, far), -1)
    behind_head = step(mixed(0, ROW), 1)
    ahead_tail = step(upstream(far, tokens), -1)
    far_behind = step(behind_tail, 1)
    far_ahead = step(ahead_head, -1)

    first_row = lax.axis_index("seq") * OWN
    table = scalars(document_rows, first_row, 4 if seq_count == 4 else 0)
    tables = dft_tables()

    tile = min(channels, 256)
    fixed = [pl.BlockSpec(memory_space=pltpu.SMEM)] + [
        pl.BlockSpec(t.shape, lambda j: (0, 0)) for t in tables
    ]

    def flat(rows, dtype=wide):
        return (
            pl.BlockSpec((rows, tile), lambda j: (0, j)),
            jax.ShapeDtypeStruct((rows, channels), dtype),
            None,
        )

    def spectra(rows):
        return (
            pl.BlockSpec((rows, 2 * ROW, tile), lambda j: (0, 0, j)),
            jax.ShapeDtypeStruct((rows, 2 * ROW, channels), wide),
            pltpu.VMEM((rows, 2 * ROW, tile), wide),
        )

    def call(kernel, cost, ins, outs, scratch, operands):
        return pl.pallas_call(
            kernel,
            grid=(channels // tile,),
            in_specs=fixed + [i[0] for i in ins],
            out_specs=[o[0] for o in outs],
            out_shape=[o[1] for o in outs],
            scratch_shapes=[x[2] for x in scratch],
            compiler_params=pltpu.CompilerParams(vmem_limit_bytes=44 * 1024 * 1024),
            cost_estimate=pl.CostEstimate(
                flops=cost, bytes_accessed=1_000_000, transcendentals=0
            ),
        )(table, *tables, *operands)

    narrow = flat(tokens, jnp.bfloat16)
    share, row, rows = flat(2 * ROW), flat(ROW), flat(far)
    own, every = spectra(OWN), spectra(MOST)
    mixed_spec, grad_spec, filter_spec, first, second = call(
        own_kernel,
        C0,
        [narrow] * 4 + [flat(MOST * ROW)],
        [own, own, every, share, share],
        [own],
        (query_in, key_in, value_in, out_grad, long_filter),
    )
    behind_spec, ahead_spec, *parts = call(
        pair_kernel,
        C1,
        [rows, row, rows, row, own, own, share, share],
        [own, own] + [share] * 4,
        [every] * 3,
        (behind_tail, behind_head, ahead_head, ahead_tail, mixed_spec, grad_spec, first, second),
    )
    second, _ = lax.optimization_barrier((second, ahead_tail[:8, :128]))
    filter_grad = reduced((first, second), parts, seq_count)
    (query_grad,) = call(
        query_kernel,
        C2,
        [rows, own, own, every, narrow],
        [narrow],
        [spectra(MOST - 1 - OWN)],
        (far_behind, behind_spec, mixed_spec, filter_spec, out_grad),
    )
    key_grad, value_grad = call(
        key_value_kernel,
        C3,
        [rows, own, own, every, narrow, narrow],
        [narrow, narrow],
        [spectra(MOST - 1 - OWN)],
        (far_ahead, ahead_spec, grad_spec, filter_spec, key_in, value_in),
    )
    return query_grad, key_grad, value_grad, filter_grad * (1.0 / math.sqrt(total_rows * ROW))


def solution(mesh):
    tokens = P(("groups", "seq"), "chan")
    return jax.shard_map(
        body,
        mesh=mesh,
        in_specs=(tokens,) * 4 + (P("groups"), P(None, "chan")),
        out_specs=(tokens,) * 4,
        check_vma=False,
    )
```

```python
import math

import jax
import jax.numpy as jnp
import ml_dtypes
import numpy as np
from jax import lax
from jax.experimental import pallas as pl
from jax.experimental.pallas import tpu as pltpu
from jax.sharding import PartitionSpec as P

ROW = 128
MOST = 8
HALF = ROW // 2
OWN = 4
FAR = 2
G = 20_000_000_000
CP, C0, C1, C2, C3 = 1, G, G // 2, G // 4, G // 4


def split_table(table):
    high = table.astype(ml_dtypes.bfloat16)
    low = (table - high.astype(np.float64)).astype(ml_dtypes.bfloat16)
    return high, low


def dft_tables():
    order = np.concatenate([np.arange(0, ROW, 2), np.arange(1, ROW, 2)])
    phase = np.outer(2 * order + 1, np.arange(ROW)) % (4 * ROW) * (math.pi / (2 * ROW))
    forward = np.concatenate([np.cos(phase), -np.sin(phase)], axis=0)
    high, low = split_table(forward)
    inv_high, inv_low = split_table(forward.T / ROW)
    return (
        np.concatenate([high, high], axis=1),
        low,
        inv_high,
        inv_low,
    )


def halves(value):
    high = value.astype(jnp.bfloat16)
    low = (value - high.astype(jnp.float32)).astype(jnp.bfloat16)
    return high, low


def matmul(one, two):
    return jnp.dot(one, two, preferred_element_type=jnp.float32)


def transform(signal, forward_ref, forward_low_ref):
    high, low = halves(signal)
    return matmul(forward_ref[...], jnp.concatenate([high, low], axis=0)) + matmul(
        forward_low_ref[...], high
    )


def untransform(spectrum, inverse_ref, inverse_low_ref):
    high, low = halves(spectrum)
    return (
        matmul(inverse_ref[...], high)
        + matmul(inverse_ref[...], low)
        + matmul(inverse_low_ref[...], high)
    )


def turned(spectrum, sign):
    real, imag = spectrum[:ROW], spectrum[ROW:]
    plus = lambda part: jnp.concatenate([part[:HALF], -part[HALF:]], axis=0)
    minus = lambda part: jnp.concatenate([-part[:HALF], part[HALF:]], axis=0)
    if sign > 0:
        return jnp.concatenate([minus(imag), plus(real)], axis=0)
    return jnp.concatenate([plus(imag), minus(real)], axis=0)


def multiply_add(total, offset, one_ref, one, two_ref, two):
    for part in range(4):
        real = pl.ds(part * 32, 32)
        imag = pl.ds(ROW + part * 32, 32)
        one_re, one_im = one_ref[one, real, :], one_ref[one, imag, :]
        two_re, two_im = two_ref[two, real, :], two_ref[two, imag, :]
        total[offset, real, :] += one_re * two_re + one_im * two_im
        total[offset, imag, :] += one_re * two_im - one_im * two_re


def own_kernel(
    table_ref,
    forward_ref,
    forward_low_ref,
    inverse_ref,
    inverse_low_ref,
    query_ref,
    key_ref,
    value_ref,
    out_grad_ref,
    filter_ref,
    mixed_spec,
    grad_spec,
    filter_spec,
    first_ref,
    second_ref,
    near,
):
    wide = jnp.float32
    for row in range(OWN):
        rows = pl.ds(row * ROW, ROW)
        mixed_spec[row] = transform(
            key_ref[rows, :].astype(wide) * value_ref[rows, :].astype(wide),
            forward_ref,
            forward_low_ref,
        )
        grad_spec[row] = transform(
            out_grad_ref[rows, :].astype(wide) * query_ref[rows, :].astype(wide),
            forward_ref,
            forward_low_ref,
        )
    near[...] = jnp.zeros_like(near)
    for source in range(OWN):
        stop = jnp.minimum(table_ref[3 * OWN + source], OWN - source)

        @pl.loop(0, stop)
        def _(offset):
            multiply_add(near, offset, mixed_spec, source, grad_spec, source + offset)

    for block in range(OWN):
        spectrum = near[block]
        if block + 1 < OWN:
            spectrum = spectrum + turned(near[block + 1], -1)
        out_ref = (first_ref, second_ref)[block // 2]
        out_ref[pl.ds(block % 2 * ROW, ROW), :] = untransform(
            spectrum, inverse_ref, inverse_low_ref
        )
    before = None
    for offset in range(MOST):
        plain = transform(filter_ref[pl.ds(offset * ROW, ROW), :], forward_ref, forward_low_ref)
        filter_spec[offset] = plain if before is None else plain + turned(before, 1)
        before = plain


def pair_kernel(
    table_ref,
    forward_ref,
    forward_low_ref,
    inverse_ref,
    inverse_low_ref,
    behind_tail_ref,
    behind_head_ref,
    ahead_head_ref,
    ahead_tail_ref,
    mixed_spec,
    grad_spec,
    first_ref,
    second_ref,
    behind_spec,
    ahead_spec,
    hand_ref,
    turn_ref,
    outward_ref,
    keep_ref,
    middle,
    back,
    front,
):
    def spectrum_of(ref, row):
        return transform(ref[pl.ds(row * ROW, ROW), :], forward_ref, forward_low_ref)

    behind_spec[0] = spectrum_of(behind_head_ref, 0)
    ahead_spec[OWN - 1] = spectrum_of(ahead_tail_ref, 0)
    for row in range(OWN - 1):
        behind_spec[row + 1] = spectrum_of(behind_tail_ref, row)
        ahead_spec[row] = spectrum_of(ahead_head_ref, row)
    middle[...] = jnp.zeros_like(middle)
    back[...] = jnp.zeros_like(back)
    front[...] = jnp.zeros_like(front)
    for source in range(OWN):
        stop = table_ref[2 * OWN + source]

        @pl.loop(OWN - source, jnp.minimum(stop, 2 * OWN - source))
        def _(offset):
            multiply_add(
                back, offset, behind_spec, source, grad_spec, source - OWN + offset
            )

        @pl.loop(2 * OWN - source, jnp.minimum(stop, MOST))
        def _(offset):
            multiply_add(
                middle, offset, behind_spec, source, ahead_spec, source - 2 * OWN + offset
            )

        stop = table_ref[3 * OWN + source]

        @pl.loop(OWN - source, jnp.minimum(stop, min(MOST, 2 * OWN - source)))
        def _(offset):
            multiply_add(
                front, offset, mixed_spec, source, ahead_spec, source - OWN + offset
            )

    for block in range(MOST):
        use_back = table_ref[4 * OWN + block].astype(jnp.float32)
        use_front = table_ref[4 * OWN + MOST + block].astype(jnp.float32)

        def gathered(offset):
            return middle[offset] + use_back * back[offset] + use_front * front[offset]

        spectrum = gathered(block)
        if block + 1 < MOST:
            spectrum = spectrum + turned(gathered(block + 1), -1)
        rows = pl.ds(block % 2 * ROW, ROW)
        taps = untransform(spectrum, inverse_ref, inverse_low_ref)
        if block < OWN:
            taps = taps + (first_ref, second_ref)[block // 2][rows, :]
        role = table_ref[4 * OWN + 2 * MOST + 1 + block // 2]
        for place, out_ref in enumerate((hand_ref, turn_ref, outward_ref, keep_ref)):

            @pl.when(role == place)
            def _():
                out_ref[rows, :] = taps


def forward_kernel(
    table_ref,
    forward_ref,
    forward_low_ref,
    inverse_ref,
    inverse_low_ref,
    behind_ref,
    ahead_ref,
    filter_spec,
    right_ref,
    left_ref,
):
    right_ref[...] = behind_ref[pl.ds(ROW, 2 * ROW), :]
    left_ref[...] = ahead_ref[pl.ds(0, 2 * ROW), :]

    def parts(spectrum):
        return spectrum[:ROW], spectrum[ROW:]

    @pl.when(table_ref[4 * OWN + 2 * MOST] == MOST)
    def _():
        total_re, total_im = 0.0, 0.0
        for row in range(3):
            signal = behind_ref[pl.ds(row * ROW, ROW), :]
            one_re, one_im = parts(transform(signal, forward_ref, forward_low_ref))
            two_re, two_im = parts(filter_spec[3 - row])
            total_re = total_re + (one_re * two_re - one_im * two_im)
            total_im = total_im + (one_re * two_im + one_im * two_re)
        right_ref[pl.ds(0, ROW), :] = untransform(
            jnp.concatenate([total_re, total_im], axis=0), inverse_ref, inverse_low_ref
        )

    @pl.when(table_ref[3 * OWN - 1] == MOST)
    def _():
        total_re, total_im = 0.0, 0.0
        for row in range(3):
            signal = ahead_ref[pl.ds(row * ROW, ROW), :]
            one_re, one_im = parts(transform(signal, forward_ref, forward_low_ref))
            two_re, two_im = parts(filter_spec[1 + row])
            total_re = total_re + (two_re * one_re + two_im * one_im)
            total_im = total_im + (two_re * one_im - two_im * one_re)
        left_ref[pl.ds(0, ROW), :] = untransform(
            jnp.concatenate([total_re, total_im], axis=0), inverse_ref, inverse_low_ref
        )


def summed(counts, direction, pieces, filter_spec, width):
    reals, imags = [], []
    for part in range(4):
        real = pl.ds(part * 32, 32)
        imag = pl.ds(ROW + part * 32, 32)
        total = (jnp.zeros((32, width), jnp.float32),) * 2
        for count, (ref, first, low, high) in zip(counts, pieces):

            def one_step(offset, totals):
                row = first + direction * offset
                one_re, one_im = ref[row, real, :], ref[row, imag, :]
                two_re, two_im = filter_spec[offset, real, :], filter_spec[offset, imag, :]
                if direction < 0:
                    return (
                        totals[0] + (one_re * two_re - one_im * two_im),
                        totals[1] + (one_re * two_im + one_im * two_re),
                    )
                return (
                    totals[0] + (two_re * one_re + two_im * one_im),
                    totals[1] + (two_re * one_im - two_im * one_re),
                )

            total = lax.fori_loop(low, jnp.minimum(count, high), one_step, total)
        reals.append(total[0])
        imags.append(total[1])
    return jnp.concatenate(reals + imags, axis=0)


def query_kernel(
    table_ref,
    forward_ref,
    forward_low_ref,
    inverse_ref,
    inverse_low_ref,
    far_ref,
    behind_spec,
    own_spec,
    filter_spec,
    out_grad_ref,
    query_grad_ref,
    far_spec,
):
    for row in range(FAR):
        far_spec[row] = transform(
            far_ref[pl.ds(row * ROW, ROW), :], forward_ref, forward_low_ref
        )
    for row in range(OWN):
        rows = pl.ds(row * ROW, ROW)
        pieces = (
            (own_spec, row, 0, row + 1),
            (behind_spec, row + OWN, row + 1, row + 1 + OWN),
            (far_spec, row + OWN + FAR, row + 1 + OWN, min(MOST, row + 1 + OWN + FAR)),
        )
        count = jnp.minimum(table_ref[row], MOST)
        whole = count == MOST
        counts = (count, count, jnp.where(whole, 0, count) if row == 0 else count)
        total = summed(counts, -1, pieces, filter_spec, far_ref.shape[1])
        convolved = untransform(total, inverse_ref, inverse_low_ref)
        if row == 0:
            convolved = convolved + jnp.where(whole, far_ref[pl.ds(0, ROW), :], 0.0)
        query_grad_ref[rows, :] = (
            out_grad_ref[rows, :].astype(jnp.float32) * convolved
        ).astype(jnp.bfloat16)


def key_value_kernel(
    table_ref,
    forward_ref,
    forward_low_ref,
    inverse_ref,
    inverse_low_ref,
    far_ref,
    ahead_spec,
    own_spec,
    filter_spec,
    key_ref,
    value_ref,
    key_grad_ref,
    value_grad_ref,
    far_spec,
):
    for row in range(FAR):
        far_spec[row] = transform(
            far_ref[pl.ds(row * ROW, ROW), :], forward_ref, forward_low_ref
        )
    for row in range(OWN):
        rows = pl.ds(row * ROW, ROW)
        pieces = (
            (own_spec, row, 0, OWN - row),
            (ahead_spec, row - OWN, OWN - row, 2 * OWN - row),
            (far_spec, row - 2 * OWN, 2 * OWN - row, min(MOST, 2 * OWN + FAR - row)),
        )
        count = jnp.minimum(table_ref[OWN + row], MOST)
        last = row == OWN - 1
        whole = count == MOST
        counts = (count, count, jnp.where(whole, 0, count) if last else count)
        total = summed(counts, 1, pieces, filter_spec, far_ref.shape[1])
        mixed_grad = untransform(total, inverse_ref, inverse_low_ref)
        if last:
            mixed_grad = mixed_grad + jnp.where(whole, far_ref[pl.ds(0, ROW), :], 0.0)
        key_grad_ref[rows, :] = (
            mixed_grad * value_ref[rows, :].astype(jnp.float32)
        ).astype(jnp.bfloat16)
        value_grad_ref[rows, :] = (
            mixed_grad * key_ref[rows, :].astype(jnp.float32)
        ).astype(jnp.bfloat16)


ROLES = np.array([[3, 0, 1, 2], [2, 3, 1, 0], [0, 1, 3, 2], [0, 1, 2, 3]], np.int32)


def scalars(document_rows, first_row, owner_split):
    count = document_rows.shape[0]
    index = jnp.arange(count, dtype=jnp.int32)
    ends = jnp.sum(
        jnp.where(index[None, :] <= index[:, None], document_rows[None, :], 0), axis=1
    )
    row = first_row + jnp.arange(-OWN, OWN + 1, dtype=jnp.int32)
    passed = ends[None, :] <= row[:, None]
    starts = jnp.max(jnp.where(passed, ends[None, :], 0), axis=1)
    stops = jnp.min(jnp.where(passed, jnp.int32(1 << 20), ends[None, :]), axis=1)
    ahead = jnp.where(row >= 0, stops - row, 0)
    behind = row + 1 - starts
    seq = first_row // OWN
    block = jnp.arange(MOST, dtype=jnp.int32)
    index4 = jnp.arange(4, dtype=jnp.int32)
    if owner_split:
        owner = block * owner_split // MOST
        use_back = (owner >= seq).astype(jnp.int32)
        use_front = (owner <= seq).astype(jnp.int32)
        roles = jnp.sum(jnp.where(index4[:, None] == seq, ROLES, 0), axis=0)
    else:
        use_back = jnp.ones_like(block)
        use_front = jnp.zeros_like(block)
        roles = index4
    ahead = ahead[: 2 * OWN]
    return jnp.concatenate(
        [behind[OWN : 2 * OWN], ahead[OWN:], ahead, use_back, use_front, behind[2 * OWN :], roles]
    )


def add_kernel(one_ref, two_ref, out_ref):
    out_ref[...] = one_ref[...] + two_ref[...]


def step(rows, by, first=0):
    length = lax.axis_size("seq")
    pairs = [(i, i + 1) for i in range(first, length - 1)]
    if by < 0:
        pairs = [(length - 1 - i, length - 1 - j) for i, j in pairs]
    return lax.ppermute(rows, "seq", pairs)


def first_sums(early, roles, rows_far):
    hand, turn, outward, keep = roles
    in_first = lax.ppermute(early[0], "seq", [(3, 2)])
    in_second = lax.ppermute(early[1], "seq", [(3, 2)])
    in_end = lax.ppermute(early[1], "seq", [(0, 1)])
    in_side = lax.ppermute(outward, "seq", [(2, 3), (1, 0)])
    kept = keep + in_side + in_end
    hand, turn, rows_far = lax.optimization_barrier((hand + in_first, turn, rows_far))
    in_far = lax.ppermute(hand, "seq", [(1, 3), (2, 0)])
    return (kept, in_far, turn, in_second), rows_far


def last_sums(pending):
    kept, in_far, turn, in_second = pending
    block = pl.BlockSpec((ROW, turn.shape[1]), lambda j: (j, 0))
    turn = pl.pallas_call(
        add_kernel,
        grid=(turn.shape[0] // ROW,),
        in_specs=[block] * 2,
        out_specs=block,
        out_shape=jax.ShapeDtypeStruct(turn.shape, turn.dtype),
        compiler_params=pltpu.CompilerParams(vmem_limit_bytes=8 * 1024 * 1024),
        cost_estimate=pl.CostEstimate(flops=1, bytes_accessed=1, transcendentals=0),
        name="add_terms",
    )(turn, in_second)
    return kept + in_far + lax.ppermute(turn, "seq", [(1, 2), (2, 1)])


def body(query_in, key_in, value_in, out_grad, document_rows, long_filter):
    seq_count = lax.axis_size("seq")
    tokens, channels = query_in.shape
    total_rows = tokens // ROW * seq_count
    wide = jnp.float32
    far = (MOST - 1 - OWN) * ROW

    def mixed(low, high):
        return key_in[low:high].astype(wide) * value_in[low:high].astype(wide)

    def upstream(low, high):
        return out_grad[low:high].astype(wide) * query_in[low:high].astype(wide)

    behind_tail = step(mixed(ROW, tokens), 1)
    ahead_head = step(upstream(0, far), -1)
    behind_head = step(mixed(0, ROW), 1)
    ahead_tail = step(upstream(far, tokens), -1)
    first_row = lax.axis_index("seq") * OWN
    table = scalars(document_rows, first_row, 4 if seq_count == 4 else 0)
    tables = dft_tables()

    tile = min(channels, 256)
    fixed = [pl.BlockSpec(memory_space=pltpu.SMEM)] + [
        pl.BlockSpec(t.shape, lambda j: (0, 0)) for t in tables
    ]

    def flat(rows, dtype=wide):
        return (
            pl.BlockSpec((rows, tile), lambda j: (0, j)),
            jax.ShapeDtypeStruct((rows, channels), dtype),
            None,
        )

    def spectra(rows):
        return (
            pl.BlockSpec((rows, 2 * ROW, tile), lambda j: (0, 0, j)),
            jax.ShapeDtypeStruct((rows, 2 * ROW, channels), wide),
            pltpu.VMEM((rows, 2 * ROW, tile), wide),
        )

    def call(kernel, cost, ins, outs, scratch, operands):
        return pl.pallas_call(
            kernel,
            grid=(channels // tile,),
            in_specs=fixed + [i[0] for i in ins],
            out_specs=[o[0] for o in outs],
            out_shape=[o[1] for o in outs],
            scratch_shapes=[x[2] for x in scratch],
            compiler_params=pltpu.CompilerParams(vmem_limit_bytes=44 * 1024 * 1024),
            cost_estimate=pl.CostEstimate(
                flops=cost, bytes_accessed=1_000_000, transcendentals=0
            ),
        )(table, *tables, *operands)

    narrow = flat(tokens, jnp.bfloat16)
    share, row, rows = flat(2 * ROW), flat(ROW), flat(far)
    own, every = spectra(OWN), spectra(MOST)
    mixed_spec, grad_spec, filter_spec, first, second = call(
        own_kernel,
        C0,
        [narrow] * 4 + [flat(MOST * ROW)],
        [own, own, every, share, share],
        [own],
        (query_in, key_in, value_in, out_grad, long_filter),
    )
    half = flat(2 * ROW)
    upper = (
        pl.BlockSpec((OWN, 2 * ROW, tile), lambda j: (1, 0, j)),
        every[1],
        None,
    )
    right, left = call(
        forward_kernel,
        CP,
        [rows, rows, upper],
        [half, half],
        [],
        (behind_tail, ahead_head, filter_spec),
    )
    far_behind = step(right, 1, first=1)
    far_ahead = step(left, -1, first=1)
    behind_spec, ahead_spec, *roles = call(
        pair_kernel,
        C1,
        [rows, row, rows, row, own, own, share, share],
        [own, own, share, share, share, share],
        [every] * 3,
        (behind_tail, behind_head, ahead_head, ahead_tail, mixed_spec, grad_spec, first, second),
    )
    if seq_count == 4:
        pending, (far_behind, far_ahead) = first_sums(
            (first, second), roles, (far_behind, far_ahead)
        )
    (query_grad,) = call(
        query_kernel,
        C2,
        [half, own, own, every, narrow],
        [narrow],
        [spectra(FAR)],
        (far_behind, behind_spec, mixed_spec, filter_spec, out_grad),
    )
    if seq_count == 4:
        kept, in_far, turn, in_second = pending
        turn, query_grad = lax.optimization_barrier((turn, query_grad))
        in_far, far_ahead = lax.optimization_barrier((in_far, far_ahead))
        filter_grad = last_sums((kept, in_far, turn, in_second))
    else:
        filter_grad = lax.psum_scatter(
            jnp.concatenate(roles, axis=0), "seq", scatter_dimension=0, tiled=True
        )
    key_grad, value_grad = call(
        key_value_kernel,
        C3,
        [half, own, own, every, narrow, narrow],
        [narrow, narrow],
        [spectra(FAR)],
        (far_ahead, ahead_spec, grad_spec, filter_spec, key_in, value_in),
    )
    return query_grad, key_grad, value_grad, filter_grad * (1.0 / math.sqrt(total_rows * ROW))


def solution(mesh):
    tokens = P(("groups", "seq"), "chan")
    return jax.shard_map(
        body,
        mesh=mesh,
        in_specs=(tokens,) * 4 + (P("groups"), P(None, "chan")),
        out_specs=(tokens,) * 4,
        check_vma=False,
    )
```

```python
import math

import jax
import jax.numpy as jnp
import ml_dtypes
import numpy as np
from jax import lax
from jax.experimental import pallas as pl
from jax.experimental.pallas import tpu as pltpu
from jax.sharding import PartitionSpec as P

ROW = 128
MOST = 8
HALF = ROW // 2
OWN = 4
FAR = 2
G = 20_000_000_000
CP, C0, C1, C2, C3 = 1, G, G // 2, G // 4, G // 4


def split_table(table):
    high = table.astype(ml_dtypes.bfloat16)
    low = (table - high.astype(np.float64)).astype(ml_dtypes.bfloat16)
    return high, low


def dft_tables():
    order = np.concatenate([np.arange(0, ROW, 2), np.arange(1, ROW, 2)])
    phase = np.outer(2 * order + 1, np.arange(ROW)) % (4 * ROW) * (math.pi / (2 * ROW))
    forward = np.concatenate([np.cos(phase), -np.sin(phase)], axis=0)
    high, low = split_table(forward)
    inv_high, inv_low = split_table(forward.T / ROW)
    return (
        np.concatenate([high, high], axis=1),
        low,
        inv_high,
        inv_low,
    )


def halves(value):
    high = value.astype(jnp.bfloat16)
    low = (value - high.astype(jnp.float32)).astype(jnp.bfloat16)
    return high, low


def matmul(one, two):
    return jnp.dot(one, two, preferred_element_type=jnp.float32)


def transform(signal, forward_ref, forward_low_ref):
    high, low = halves(signal)
    return matmul(forward_ref[...], jnp.concatenate([high, low], axis=0)) + matmul(
        forward_low_ref[...], high
    )


def untransform(spectrum, inverse_ref, inverse_low_ref):
    high, low = halves(spectrum)
    return (
        matmul(inverse_ref[...], high)
        + matmul(inverse_ref[...], low)
        + matmul(inverse_low_ref[...], high)
    )


def turned(spectrum, sign):
    real, imag = spectrum[:ROW], spectrum[ROW:]
    plus = lambda part: jnp.concatenate([part[:HALF], -part[HALF:]], axis=0)
    minus = lambda part: jnp.concatenate([-part[:HALF], part[HALF:]], axis=0)
    if sign > 0:
        return jnp.concatenate([minus(imag), plus(real)], axis=0)
    return jnp.concatenate([plus(imag), minus(real)], axis=0)


def multiply_add(total, offset, one_ref, one, two_ref, two):
    for part in range(4):
        real = pl.ds(part * 32, 32)
        imag = pl.ds(ROW + part * 32, 32)
        one_re, one_im = one_ref[one, real, :], one_ref[one, imag, :]
        two_re, two_im = two_ref[two, real, :], two_ref[two, imag, :]
        total[offset, real, :] += one_re * two_re + one_im * two_im
        total[offset, imag, :] += one_re * two_im - one_im * two_re


def own_kernel(
    table_ref,
    forward_ref,
    forward_low_ref,
    inverse_ref,
    inverse_low_ref,
    query_ref,
    key_ref,
    value_ref,
    out_grad_ref,
    filter_ref,
    mixed_spec,
    grad_spec,
    filter_spec,
    first_ref,
    second_ref,
    near,
):
    wide = jnp.float32
    for row in range(OWN):
        rows = pl.ds(row * ROW, ROW)
        mixed_spec[row] = transform(
            key_ref[rows, :].astype(wide) * value_ref[rows, :].astype(wide),
            forward_ref,
            forward_low_ref,
        )
        grad_spec[row] = transform(
            out_grad_ref[rows, :].astype(wide) * query_ref[rows, :].astype(wide),
            forward_ref,
            forward_low_ref,
        )
    near[...] = jnp.zeros_like(near)
    for source in range(OWN):
        stop = jnp.minimum(table_ref[3 * OWN + source], OWN - source)

        @pl.loop(0, stop)
        def _(offset):
            multiply_add(near, offset, mixed_spec, source, grad_spec, source + offset)

    for block in range(OWN):
        spectrum = near[block]
        if block + 1 < OWN:
            spectrum = spectrum + turned(near[block + 1], -1)
        out_ref = (first_ref, second_ref)[block // 2]
        out_ref[pl.ds(block % 2 * ROW, ROW), :] = untransform(
            spectrum, inverse_ref, inverse_low_ref
        )
    before = None
    for offset in range(MOST):
        plain = transform(filter_ref[pl.ds(offset * ROW, ROW), :], forward_ref, forward_low_ref)
        filter_spec[offset] = plain if before is None else plain + turned(before, 1)
        before = plain


def pair_kernel(
    table_ref,
    forward_ref,
    forward_low_ref,
    inverse_ref,
    inverse_low_ref,
    behind_tail_ref,
    behind_head_ref,
    ahead_head_ref,
    ahead_tail_ref,
    mixed_spec,
    grad_spec,
    first_ref,
    second_ref,
    behind_spec,
    ahead_spec,
    hand_ref,
    turn_ref,
    outward_ref,
    keep_ref,
    spectrum,
):
    before_own = jnp.minimum(table_ref[0] - 1, OWN)
    from_own = table_ref[3 * OWN - 1] - 1
    before_next = jnp.minimum(table_ref[4 * OWN + 2 * MOST] - 1, OWN)
    from_next = jnp.minimum(table_ref[2 * OWN - 1] - 1, OWN)

    def fill(spec_ref, row, used, ref, place):
        @pl.when(used)
        def _():
            spec_ref[row] = transform(
                ref[pl.ds(place * ROW, ROW), :], forward_ref, forward_low_ref
            )

    fill(behind_spec, 0, before_own >= OWN, behind_head_ref, 0)
    fill(ahead_spec, OWN - 1, from_next >= OWN, ahead_tail_ref, 0)
    for row in range(OWN - 1):
        fill(behind_spec, row + 1, before_own >= OWN - 1 - row, behind_tail_ref, row)
        fill(ahead_spec, row, from_next > row, ahead_head_ref, row)

    width = keep_ref.shape[1]
    zeros = (jnp.zeros((HALF, width), jnp.float32),) * 2
    for owner in range(MOST // 2):
        use_back = table_ref[4 * OWN + 2 * owner] > 0
        use_front = table_ref[4 * OWN + MOST + 2 * owner] > 0
        ranges = {}
        for offset in range(max(1, 2 * owner), min(MOST, 2 * owner + 3)):
            low = jnp.maximum(-before_own, -offset)
            high = jnp.minimum(0, jnp.minimum(from_own, OWN) - offset)
            kinds = [(behind_spec, OWN, grad_spec, 0, low, jnp.where(use_back, high, low))]
            if offset > OWN:
                low = jnp.maximum(-before_own, OWN - offset)
                high = jnp.minimum(0, jnp.minimum(from_own, 2 * OWN) - offset)
                kinds.append((behind_spec, OWN, ahead_spec, -OWN, low, high))
            low = jnp.maximum(OWN - before_next, OWN - offset)
            high = jnp.minimum(OWN, OWN + from_next - offset)
            kinds.append(
                (mixed_spec, 0, ahead_spec, -OWN, low, jnp.where(use_front, high, low))
            )
            ranges[offset] = kinds
        for part in range(2):
            real = pl.ds(part * HALF, HALF)
            imag = pl.ds(ROW + part * HALF, HALF)

            def gathered(offset):
                total = zeros
                for one_ref, one, two_ref, two, low, high in ranges.get(offset, ()):

                    def one_step(row, totals):
                        one_re = one_ref[row + one, real, :]
                        one_im = one_ref[row + one, imag, :]
                        two_re = two_ref[row + offset + two, real, :]
                        two_im = two_ref[row + offset + two, imag, :]
                        return (
                            totals[0] + (one_re * two_re + one_im * two_im),
                            totals[1] + (one_re * two_im - one_im * two_re),
                        )

                    total = lax.fori_loop(low, high, one_step, total)
                return total

            sign = 1.0 - 2.0 * part
            now_re, now_im = gathered(2 * owner)
            for place in range(2):
                next_re, next_im = gathered(2 * owner + place + 1)
                spectrum[place, real, :] = now_re + sign * next_im
                spectrum[place, imag, :] = now_im - sign * next_re
                now_re, now_im = next_re, next_im
        role = table_ref[4 * OWN + 2 * MOST + 1 + owner]
        for place in range(2):
            rows = pl.ds(place * ROW, ROW)
            taps = untransform(spectrum[place], inverse_ref, inverse_low_ref)
            if owner < 2:
                taps = taps + (first_ref, second_ref)[owner][rows, :]
            for kind, out_ref in enumerate((hand_ref, turn_ref, outward_ref, keep_ref)):

                @pl.when(role == kind)
                def _():
                    out_ref[rows, :] = taps


def forward_kernel(
    table_ref,
    forward_ref,
    forward_low_ref,
    inverse_ref,
    inverse_low_ref,
    behind_ref,
    ahead_ref,
    filter_spec,
    right_ref,
    left_ref,
):
    right_ref[...] = behind_ref[pl.ds(ROW, 2 * ROW), :]
    left_ref[...] = ahead_ref[pl.ds(0, 2 * ROW), :]

    def parts(spectrum):
        return spectrum[:ROW], spectrum[ROW:]

    @pl.when(table_ref[4 * OWN + 2 * MOST] == MOST)
    def _():
        total_re, total_im = 0.0, 0.0
        for row in range(3):
            signal = behind_ref[pl.ds(row * ROW, ROW), :]
            one_re, one_im = parts(transform(signal, forward_ref, forward_low_ref))
            two_re, two_im = parts(filter_spec[3 - row])
            total_re = total_re + (one_re * two_re - one_im * two_im)
            total_im = total_im + (one_re * two_im + one_im * two_re)
        right_ref[pl.ds(0, ROW), :] = untransform(
            jnp.concatenate([total_re, total_im], axis=0), inverse_ref, inverse_low_ref
        )

    @pl.when(table_ref[3 * OWN - 1] == MOST)
    def _():
        total_re, total_im = 0.0, 0.0
        for row in range(3):
            signal = ahead_ref[pl.ds(row * ROW, ROW), :]
            one_re, one_im = parts(transform(signal, forward_ref, forward_low_ref))
            two_re, two_im = parts(filter_spec[1 + row])
            total_re = total_re + (two_re * one_re + two_im * one_im)
            total_im = total_im + (two_re * one_im - two_im * one_re)
        left_ref[pl.ds(0, ROW), :] = untransform(
            jnp.concatenate([total_re, total_im], axis=0), inverse_ref, inverse_low_ref
        )


def summed(counts, direction, pieces, filter_spec, width):
    reals, imags = [], []
    for part in range(4):
        real = pl.ds(part * 32, 32)
        imag = pl.ds(ROW + part * 32, 32)
        total = (jnp.zeros((32, width), jnp.float32),) * 2
        for count, (ref, first, low, high) in zip(counts, pieces):

            def one_step(offset, totals):
                row = first + direction * offset
                one_re, one_im = ref[row, real, :], ref[row, imag, :]
                two_re, two_im = filter_spec[offset, real, :], filter_spec[offset, imag, :]
                if direction < 0:
                    return (
                        totals[0] + (one_re * two_re - one_im * two_im),
                        totals[1] + (one_re * two_im + one_im * two_re),
                    )
                return (
                    totals[0] + (two_re * one_re + two_im * one_im),
                    totals[1] + (two_re * one_im - two_im * one_re),
                )

            total = lax.fori_loop(low, jnp.minimum(count, high), one_step, total)
        reals.append(total[0])
        imags.append(total[1])
    return jnp.concatenate(reals + imags, axis=0)


def query_kernel(
    table_ref,
    forward_ref,
    forward_low_ref,
    inverse_ref,
    inverse_low_ref,
    far_ref,
    behind_spec,
    own_spec,
    filter_spec,
    out_grad_ref,
    query_grad_ref,
    far_spec,
):
    for row in range(FAR):
        reach = table_ref[0] - 1

        @pl.when(jnp.logical_and(reach >= OWN + FAR - row, reach < MOST - 1))
        def _():
            far_spec[row] = transform(
                far_ref[pl.ds(row * ROW, ROW), :], forward_ref, forward_low_ref
            )

    for row in range(OWN):
        rows = pl.ds(row * ROW, ROW)
        pieces = (
            (own_spec, row, 0, row + 1),
            (behind_spec, row + OWN, row + 1, row + 1 + OWN),
            (far_spec, row + OWN + FAR, row + 1 + OWN, min(MOST, row + 1 + OWN + FAR)),
        )
        count = jnp.minimum(table_ref[row], MOST)
        whole = count == MOST
        counts = (count, count, jnp.where(whole, 0, count) if row == 0 else count)
        total = summed(counts, -1, pieces, filter_spec, far_ref.shape[1])
        convolved = untransform(total, inverse_ref, inverse_low_ref)
        if row == 0:
            convolved = convolved + jnp.where(whole, far_ref[pl.ds(0, ROW), :], 0.0)
        query_grad_ref[rows, :] = (
            out_grad_ref[rows, :].astype(jnp.float32) * convolved
        ).astype(jnp.bfloat16)


def key_value_kernel(
    table_ref,
    forward_ref,
    forward_low_ref,
    inverse_ref,
    inverse_low_ref,
    far_ref,
    ahead_spec,
    own_spec,
    filter_spec,
    key_ref,
    value_ref,
    key_grad_ref,
    value_grad_ref,
    far_spec,
):
    for row in range(FAR):
        reach = table_ref[2 * OWN - 1] - 1

        @pl.when(jnp.logical_and(reach > OWN + row, reach < MOST - 1))
        def _():
            far_spec[row] = transform(
                far_ref[pl.ds(row * ROW, ROW), :], forward_ref, forward_low_ref
            )

    for row in range(OWN):
        rows = pl.ds(row * ROW, ROW)
        pieces = (
            (own_spec, row, 0, OWN - row),
            (ahead_spec, row - OWN, OWN - row, 2 * OWN - row),
            (far_spec, row - 2 * OWN, 2 * OWN - row, min(MOST, 2 * OWN + FAR - row)),
        )
        count = jnp.minimum(table_ref[OWN + row], MOST)
        last = row == OWN - 1
        whole = count == MOST
        counts = (count, count, jnp.where(whole, 0, count) if last else count)
        total = summed(counts, 1, pieces, filter_spec, far_ref.shape[1])
        mixed_grad = untransform(total, inverse_ref, inverse_low_ref)
        if last:
            mixed_grad = mixed_grad + jnp.where(whole, far_ref[pl.ds(0, ROW), :], 0.0)
        key_grad_ref[rows, :] = (
            mixed_grad * value_ref[rows, :].astype(jnp.float32)
        ).astype(jnp.bfloat16)
        value_grad_ref[rows, :] = (
            mixed_grad * key_ref[rows, :].astype(jnp.float32)
        ).astype(jnp.bfloat16)


ROLES = np.array([[3, 0, 1, 2], [2, 3, 1, 0], [0, 1, 3, 2], [0, 1, 2, 3]], np.int32)


def scalars(document_rows, first_row, owner_split):
    count = document_rows.shape[0]
    index = jnp.arange(count, dtype=jnp.int32)
    ends = jnp.sum(
        jnp.where(index[None, :] <= index[:, None], document_rows[None, :], 0), axis=1
    )
    row = first_row + jnp.arange(-OWN, OWN + 1, dtype=jnp.int32)
    passed = ends[None, :] <= row[:, None]
    starts = jnp.max(jnp.where(passed, ends[None, :], 0), axis=1)
    stops = jnp.min(jnp.where(passed, jnp.int32(1 << 20), ends[None, :]), axis=1)
    ahead = jnp.where(row >= 0, stops - row, 0)
    behind = row + 1 - starts
    seq = first_row // OWN
    block = jnp.arange(MOST, dtype=jnp.int32)
    index4 = jnp.arange(4, dtype=jnp.int32)
    if owner_split:
        owner = block * owner_split // MOST
        use_back = (owner >= seq).astype(jnp.int32)
        use_front = (owner <= seq).astype(jnp.int32)
        roles = jnp.sum(jnp.where(index4[:, None] == seq, ROLES, 0), axis=0)
    else:
        use_back = jnp.ones_like(block)
        use_front = jnp.zeros_like(block)
        roles = index4
    ahead = ahead[: 2 * OWN]
    return jnp.concatenate(
        [behind[OWN : 2 * OWN], ahead[OWN:], ahead, use_back, use_front, behind[2 * OWN :], roles]
    )


def add_kernel(one_ref, two_ref, out_ref):
    out_ref[...] = one_ref[...] + two_ref[...]


def step(rows, by, first=0):
    length = lax.axis_size("seq")
    pairs = [(i, i + 1) for i in range(first, length - 1)]
    if by < 0:
        pairs = [(length - 1 - i, length - 1 - j) for i, j in pairs]
    return lax.ppermute(rows, "seq", pairs)


def first_sums(early, roles, rows_far):
    hand, turn, outward, keep = roles
    in_first = lax.ppermute(early[0], "seq", [(3, 2)])
    in_second = lax.ppermute(early[1], "seq", [(3, 2)])
    in_end = lax.ppermute(early[1], "seq", [(0, 1)])
    hand, turn, rows_far = lax.optimization_barrier((hand + in_first, turn, rows_far))
    in_far = lax.ppermute(hand, "seq", [(1, 3), (2, 0)])
    return (keep + in_end, in_far, turn, outward, in_second), rows_far


def last_sums(pending):
    kept, in_far, turn, outward, in_second = pending
    in_side = lax.ppermute(outward, "seq", [(2, 3), (1, 0)])
    block = pl.BlockSpec((ROW, turn.shape[1]), lambda j: (j, 0))
    turn = pl.pallas_call(
        add_kernel,
        grid=(turn.shape[0] // ROW,),
        in_specs=[block] * 2,
        out_specs=block,
        out_shape=jax.ShapeDtypeStruct(turn.shape, turn.dtype),
        compiler_params=pltpu.CompilerParams(vmem_limit_bytes=8 * 1024 * 1024),
        cost_estimate=pl.CostEstimate(flops=1, bytes_accessed=1, transcendentals=0),
        name="add_terms",
    )(turn, in_second)
    return kept + in_side + in_far + lax.ppermute(turn, "seq", [(1, 2), (2, 1)])


def body(query_in, key_in, value_in, out_grad, document_rows, long_filter):
    seq_count = lax.axis_size("seq")
    tokens, channels = query_in.shape
    total_rows = tokens // ROW * seq_count
    wide = jnp.float32
    far = (MOST - 1 - OWN) * ROW

    def mixed(low, high):
        return key_in[low:high].astype(wide) * value_in[low:high].astype(wide)

    def upstream(low, high):
        return out_grad[low:high].astype(wide) * query_in[low:high].astype(wide)

    behind_tail = step(mixed(ROW, tokens), 1)
    ahead_head = step(upstream(0, far), -1)
    behind_head = step(mixed(0, ROW), 1)
    ahead_tail = step(upstream(far, tokens), -1)
    first_row = lax.axis_index("seq") * OWN
    table = scalars(document_rows, first_row, 4 if seq_count == 4 else 0)
    tables = dft_tables()

    tile = min(channels, 256)
    fixed = [pl.BlockSpec(memory_space=pltpu.SMEM)] + [
        pl.BlockSpec(t.shape, lambda j: (0, 0)) for t in tables
    ]

    def flat(rows, dtype=wide):
        return (
            pl.BlockSpec((rows, tile), lambda j: (0, j)),
            jax.ShapeDtypeStruct((rows, channels), dtype),
            None,
        )

    def spectra(rows):
        return (
            pl.BlockSpec((rows, 2 * ROW, tile), lambda j: (0, 0, j)),
            jax.ShapeDtypeStruct((rows, 2 * ROW, channels), wide),
            pltpu.VMEM((rows, 2 * ROW, tile), wide),
        )

    def call(kernel, cost, ins, outs, scratch, operands):
        return pl.pallas_call(
            kernel,
            grid=(channels // tile,),
            in_specs=fixed + [i[0] for i in ins],
            out_specs=[o[0] for o in outs],
            out_shape=[o[1] for o in outs],
            scratch_shapes=[x[2] for x in scratch],
            compiler_params=pltpu.CompilerParams(vmem_limit_bytes=44 * 1024 * 1024),
            cost_estimate=pl.CostEstimate(
                flops=cost, bytes_accessed=1_000_000, transcendentals=0
            ),
        )(table, *tables, *operands)

    narrow = flat(tokens, jnp.bfloat16)
    share, row, rows = flat(2 * ROW), flat(ROW), flat(far)
    own, every = spectra(OWN), spectra(MOST)
    mixed_spec, grad_spec, filter_spec, first, second = call(
        own_kernel,
        C0,
        [narrow] * 4 + [flat(MOST * ROW)],
        [own, own, every, share, share],
        [own],
        (query_in, key_in, value_in, out_grad, long_filter),
    )
    half = flat(2 * ROW)
    upper = (
        pl.BlockSpec((OWN, 2 * ROW, tile), lambda j: (1, 0, j)),
        every[1],
        None,
    )
    right, left = call(
        forward_kernel,
        CP,
        [rows, rows, upper],
        [half, half],
        [],
        (behind_tail, ahead_head, filter_spec),
    )
    far_behind = step(right, 1, first=1)
    far_ahead = step(left, -1, first=1)
    behind_spec, ahead_spec, *roles = call(
        pair_kernel,
        C1,
        [rows, row, rows, row, own, own, share, share],
        [own, own, share, share, share, share],
        [spectra(2)],
        (behind_tail, behind_head, ahead_head, ahead_tail, mixed_spec, grad_spec, first, second),
    )
    if seq_count == 4:
        pending, (far_behind, far_ahead) = first_sums(
            (first, second), roles, (far_behind, far_ahead)
        )
    (query_grad,) = call(
        query_kernel,
        C2,
        [half, own, own, every, narrow],
        [narrow],
        [spectra(FAR)],
        (far_behind, behind_spec, mixed_spec, filter_spec, out_grad),
    )
    if seq_count == 4:
        kept, in_far, turn, outward, in_second = pending
        turn, outward, query_grad = lax.optimization_barrier((turn, outward, query_grad))
        in_far, far_ahead = lax.optimization_barrier((in_far, far_ahead))
        filter_grad = last_sums((kept, in_far, turn, outward, in_second))
    else:
        filter_grad = lax.psum_scatter(
            jnp.concatenate(roles, axis=0), "seq", scatter_dimension=0, tiled=True
        )
    key_grad, value_grad = call(
        key_value_kernel,
        C3,
        [half, own, own, every, narrow, narrow],
        [narrow, narrow],
        [spectra(FAR)],
        (far_ahead, ahead_spec, grad_spec, filter_spec, key_in, value_in),
    )
    return query_grad, key_grad, value_grad, filter_grad * (1.0 / math.sqrt(total_rows * ROW))


def solution(mesh):
    tokens = P(("groups", "seq"), "chan")
    return jax.shard_map(
        body,
        mesh=mesh,
        in_specs=(tokens,) * 4 + (P("groups"), P(None, "chan")),
        out_specs=(tokens,) * 4,
        check_vma=False,
    )
```

```python
import math

import jax
import jax.numpy as jnp
import ml_dtypes
import numpy as np
from jax import lax
from jax.experimental import pallas as pl
from jax.experimental.pallas import tpu as pltpu
from jax.sharding import PartitionSpec as P

ROW = 128
MOST = 8
HALF = ROW // 2
OWN = 4
FAR = 2
G = 20_000_000_000
CP, C0, C1, C2, C3 = 1, G, G // 2, G // 4, G // 4


def split_table(table):
    high = table.astype(ml_dtypes.bfloat16)
    low = (table - high.astype(np.float64)).astype(ml_dtypes.bfloat16)
    return high, low


def dft_tables():
    order = np.concatenate([np.arange(0, ROW, 2), np.arange(1, ROW, 2)])
    phase = np.outer(2 * order + 1, np.arange(ROW)) % (4 * ROW) * (math.pi / (2 * ROW))
    forward = np.concatenate([np.cos(phase), -np.sin(phase)], axis=0)
    high, low = split_table(forward)
    inv_high, inv_low = split_table(forward.T / ROW)
    return (
        np.concatenate([high, high], axis=1),
        low,
        inv_high,
        inv_low,
    )


def halves(value):
    high = value.astype(jnp.bfloat16)
    low = (value - high.astype(jnp.float32)).astype(jnp.bfloat16)
    return high, low


def matmul(one, two):
    return jnp.dot(one, two, preferred_element_type=jnp.float32)


def transform(signal, forward_ref, forward_low_ref):
    high, low = halves(signal)
    return matmul(forward_ref[...], jnp.concatenate([high, low], axis=0)) + matmul(
        forward_low_ref[...], high
    )


def untransform(spectrum, inverse_ref, inverse_low_ref):
    high, low = halves(spectrum)
    return (
        matmul(inverse_ref[...], high)
        + matmul(inverse_ref[...], low)
        + matmul(inverse_low_ref[...], high)
    )


def turned(spectrum, sign):
    real, imag = spectrum[:ROW], spectrum[ROW:]
    plus = lambda part: jnp.concatenate([part[:HALF], -part[HALF:]], axis=0)
    minus = lambda part: jnp.concatenate([-part[:HALF], part[HALF:]], axis=0)
    if sign > 0:
        return jnp.concatenate([minus(imag), plus(real)], axis=0)
    return jnp.concatenate([plus(imag), minus(real)], axis=0)


def multiply_add(total, offset, one_ref, one, two_ref, two):
    for part in range(4):
        real = pl.ds(part * 32, 32)
        imag = pl.ds(ROW + part * 32, 32)
        one_re, one_im = one_ref[one, real, :], one_ref[one, imag, :]
        two_re, two_im = two_ref[two, real, :], two_ref[two, imag, :]
        total[offset, real, :] += one_re * two_re + one_im * two_im
        total[offset, imag, :] += one_re * two_im - one_im * two_re


def own_kernel(
    table_ref,
    forward_ref,
    forward_low_ref,
    inverse_ref,
    inverse_low_ref,
    query_ref,
    key_ref,
    value_ref,
    out_grad_ref,
    filter_ref,
    mixed_spec,
    grad_spec,
    filter_spec,
    first_ref,
    second_ref,
    near,
):
    wide = jnp.float32
    for row in range(OWN):
        rows = pl.ds(row * ROW, ROW)
        mixed_spec[row] = transform(
            key_ref[rows, :].astype(wide) * value_ref[rows, :].astype(wide),
            forward_ref,
            forward_low_ref,
        )
        grad_spec[row] = transform(
            out_grad_ref[rows, :].astype(wide) * query_ref[rows, :].astype(wide),
            forward_ref,
            forward_low_ref,
        )
    near[...] = jnp.zeros_like(near)
    for source in range(OWN):
        stop = jnp.minimum(table_ref[3 * OWN + source], OWN - source)

        @pl.loop(0, stop)
        def _(offset):
            multiply_add(near, offset, mixed_spec, source, grad_spec, source + offset)

    for block in range(OWN):
        spectrum = near[block]
        if block + 1 < OWN:
            spectrum = spectrum + turned(near[block + 1], -1)
        out_ref = (first_ref, second_ref)[block // 2]
        out_ref[pl.ds(block % 2 * ROW, ROW), :] = untransform(
            spectrum, inverse_ref, inverse_low_ref
        )
    before = None
    for offset in range(MOST):
        plain = transform(filter_ref[pl.ds(offset * ROW, ROW), :], forward_ref, forward_low_ref)
        filter_spec[offset] = plain if before is None else plain + turned(before, 1)
        before = plain


def fill(spec_ref, row, used, refs, place, tables):
    @pl.when(used)
    def _():
        rows = pl.ds(place * ROW, ROW)
        signal = refs[0][rows, :].astype(jnp.float32)
        for ref in refs[1:]:
            signal = signal * ref[rows, :].astype(jnp.float32)
        spec_ref[row] = transform(signal, *tables)


def fill_behind(spec_ref, count, head_ref, tail_ref, tables):
    fill(spec_ref, 0, count >= OWN, (head_ref,), 0, tables)
    for row in range(1, OWN):
        fill(spec_ref, row, count >= OWN - row, (tail_ref,), row - 1, tables)


def fill_ahead(spec_ref, count, head_ref, tail_ref, tables):
    for row in range(OWN - 1):
        fill(spec_ref, row, count > row, (head_ref,), row, tables)
    fill(spec_ref, OWN - 1, count >= OWN, (tail_ref,), 0, tables)


def pair_kernel(
    table_ref,
    forward_ref,
    forward_low_ref,
    inverse_ref,
    inverse_low_ref,
    behind_tail_ref,
    behind_head_ref,
    ahead_head_ref,
    ahead_tail_ref,
    query_ref,
    key_ref,
    value_ref,
    out_grad_ref,
    first_ref,
    second_ref,
    hand_ref,
    turn_ref,
    outward_ref,
    keep_ref,
    behind_spec,
    mixed_spec,
    grad_spec,
    ahead_spec,
    spectrum,
):
    before_own = jnp.minimum(table_ref[0] - 1, OWN)
    from_own = table_ref[3 * OWN - 1] - 1
    before_next = jnp.minimum(table_ref[4 * OWN + 2 * MOST] - 1, OWN)
    from_next = jnp.minimum(table_ref[2 * OWN - 1] - 1, OWN)

    tables = (forward_ref, forward_low_ref)
    fill_behind(behind_spec, before_own, behind_head_ref, behind_tail_ref, tables)
    fill_ahead(ahead_spec, from_next, ahead_head_ref, ahead_tail_ref, tables)
    for row in range(OWN):
        fill(mixed_spec, row, before_next >= OWN - row, (key_ref, value_ref), row, tables)
        fill(grad_spec, row, from_own > row, (out_grad_ref, query_ref), row, tables)

    width = keep_ref.shape[1]
    zeros = (jnp.zeros((HALF, width), jnp.float32),) * 2
    for owner in range(MOST // 2):
        use_back = table_ref[4 * OWN + 2 * owner] > 0
        use_front = table_ref[4 * OWN + MOST + 2 * owner] > 0
        ranges = {}
        for offset in range(max(1, 2 * owner), min(MOST, 2 * owner + 3)):
            low = jnp.maximum(-before_own, -offset)
            high = jnp.minimum(0, jnp.minimum(from_own, OWN) - offset)
            kinds = [(behind_spec, OWN, grad_spec, 0, low, jnp.where(use_back, high, low))]
            if offset > OWN:
                low = jnp.maximum(-before_own, OWN - offset)
                high = jnp.minimum(0, jnp.minimum(from_own, 2 * OWN) - offset)
                kinds.append((behind_spec, OWN, ahead_spec, -OWN, low, high))
            low = jnp.maximum(OWN - before_next, OWN - offset)
            high = jnp.minimum(OWN, OWN + from_next - offset)
            kinds.append(
                (mixed_spec, 0, ahead_spec, -OWN, low, jnp.where(use_front, high, low))
            )
            ranges[offset] = kinds
        for part in range(2):
            real = pl.ds(part * HALF, HALF)
            imag = pl.ds(ROW + part * HALF, HALF)

            def gathered(offset):
                total = zeros
                for one_ref, one, two_ref, two, low, high in ranges.get(offset, ()):

                    def one_step(row, totals):
                        one_re = one_ref[row + one, real, :]
                        one_im = one_ref[row + one, imag, :]
                        two_re = two_ref[row + offset + two, real, :]
                        two_im = two_ref[row + offset + two, imag, :]
                        return (
                            totals[0] + (one_re * two_re + one_im * two_im),
                            totals[1] + (one_re * two_im - one_im * two_re),
                        )

                    total = lax.fori_loop(low, high, one_step, total)
                return total

            sign = 1.0 - 2.0 * part
            now_re, now_im = gathered(2 * owner)
            for place in range(2):
                next_re, next_im = gathered(2 * owner + place + 1)
                spectrum[place, real, :] = now_re + sign * next_im
                spectrum[place, imag, :] = now_im - sign * next_re
                now_re, now_im = next_re, next_im
        role = table_ref[4 * OWN + 2 * MOST + 1 + owner]
        for place in range(2):
            rows = pl.ds(place * ROW, ROW)
            taps = untransform(spectrum[place], inverse_ref, inverse_low_ref)
            if owner < 2:
                taps = taps + (first_ref, second_ref)[owner][rows, :]
            for kind, out_ref in enumerate((hand_ref, turn_ref, outward_ref, keep_ref)):

                @pl.when(role == kind)
                def _():
                    out_ref[rows, :] = taps


def forward_kernel(
    table_ref,
    forward_ref,
    forward_low_ref,
    inverse_ref,
    inverse_low_ref,
    behind_ref,
    ahead_ref,
    filter_spec,
    right_ref,
    left_ref,
):
    right_ref[...] = behind_ref[pl.ds(ROW, 2 * ROW), :]
    left_ref[...] = ahead_ref[pl.ds(0, 2 * ROW), :]

    def parts(spectrum):
        return spectrum[:ROW], spectrum[ROW:]

    @pl.when(table_ref[4 * OWN + 2 * MOST] == MOST)
    def _():
        total_re, total_im = 0.0, 0.0
        for row in range(3):
            signal = behind_ref[pl.ds(row * ROW, ROW), :]
            one_re, one_im = parts(transform(signal, forward_ref, forward_low_ref))
            two_re, two_im = parts(filter_spec[3 - row])
            total_re = total_re + (one_re * two_re - one_im * two_im)
            total_im = total_im + (one_re * two_im + one_im * two_re)
        right_ref[pl.ds(0, ROW), :] = untransform(
            jnp.concatenate([total_re, total_im], axis=0), inverse_ref, inverse_low_ref
        )

    @pl.when(table_ref[3 * OWN - 1] == MOST)
    def _():
        total_re, total_im = 0.0, 0.0
        for row in range(3):
            signal = ahead_ref[pl.ds(row * ROW, ROW), :]
            one_re, one_im = parts(transform(signal, forward_ref, forward_low_ref))
            two_re, two_im = parts(filter_spec[1 + row])
            total_re = total_re + (two_re * one_re + two_im * one_im)
            total_im = total_im + (two_re * one_im - two_im * one_re)
        left_ref[pl.ds(0, ROW), :] = untransform(
            jnp.concatenate([total_re, total_im], axis=0), inverse_ref, inverse_low_ref
        )


def summed(counts, direction, pieces, filter_spec, width):
    reals, imags = [], []
    for part in range(4):
        real = pl.ds(part * 32, 32)
        imag = pl.ds(ROW + part * 32, 32)
        total = (jnp.zeros((32, width), jnp.float32),) * 2
        for count, (ref, first, low, high) in zip(counts, pieces):

            def one_step(offset, totals):
                row = first + direction * offset
                one_re, one_im = ref[row, real, :], ref[row, imag, :]
                two_re, two_im = filter_spec[offset, real, :], filter_spec[offset, imag, :]
                if direction < 0:
                    return (
                        totals[0] + (one_re * two_re - one_im * two_im),
                        totals[1] + (one_re * two_im + one_im * two_re),
                    )
                return (
                    totals[0] + (two_re * one_re + two_im * one_im),
                    totals[1] + (two_re * one_im - two_im * one_re),
                )

            total = lax.fori_loop(low, jnp.minimum(count, high), one_step, total)
        reals.append(total[0])
        imags.append(total[1])
    return jnp.concatenate(reals + imags, axis=0)


def query_kernel(
    table_ref,
    forward_ref,
    forward_low_ref,
    inverse_ref,
    inverse_low_ref,
    far_ref,
    head_ref,
    tail_ref,
    own_spec,
    filter_spec,
    out_grad_ref,
    query_grad_ref,
    far_spec,
    behind_spec,
):
    reach = table_ref[0] - 1
    tables = (forward_ref, forward_low_ref)
    fill_behind(behind_spec, reach, head_ref, tail_ref, tables)
    for row in range(FAR):
        used = jnp.logical_and(reach >= OWN + FAR - row, reach < MOST - 1)
        fill(far_spec, row, used, (far_ref,), row, tables)

    for row in range(OWN):
        rows = pl.ds(row * ROW, ROW)
        pieces = (
            (own_spec, row, 0, row + 1),
            (behind_spec, row + OWN, row + 1, row + 1 + OWN),
            (far_spec, row + OWN + FAR, row + 1 + OWN, min(MOST, row + 1 + OWN + FAR)),
        )
        count = jnp.minimum(table_ref[row], MOST)
        whole = count == MOST
        counts = (count, count, jnp.where(whole, 0, count) if row == 0 else count)
        total = summed(counts, -1, pieces, filter_spec, far_ref.shape[1])
        convolved = untransform(total, inverse_ref, inverse_low_ref)
        if row == 0:
            convolved = convolved + jnp.where(whole, far_ref[pl.ds(0, ROW), :], 0.0)
        query_grad_ref[rows, :] = (
            out_grad_ref[rows, :].astype(jnp.float32) * convolved
        ).astype(jnp.bfloat16)


def key_value_kernel(
    table_ref,
    forward_ref,
    forward_low_ref,
    inverse_ref,
    inverse_low_ref,
    far_ref,
    head_ref,
    tail_ref,
    own_spec,
    filter_spec,
    key_ref,
    value_ref,
    key_grad_ref,
    value_grad_ref,
    far_spec,
    ahead_spec,
):
    reach = table_ref[2 * OWN - 1] - 1
    tables = (forward_ref, forward_low_ref)
    fill_ahead(ahead_spec, reach, head_ref, tail_ref, tables)
    for row in range(FAR):
        used = jnp.logical_and(reach > OWN + row, reach < MOST - 1)
        fill(far_spec, row, used, (far_ref,), row, tables)

    for row in range(OWN):
        rows = pl.ds(row * ROW, ROW)
        pieces = (
            (own_spec, row, 0, OWN - row),
            (ahead_spec, row - OWN, OWN - row, 2 * OWN - row),
            (far_spec, row - 2 * OWN, 2 * OWN - row, min(MOST, 2 * OWN + FAR - row)),
        )
        count = jnp.minimum(table_ref[OWN + row], MOST)
        last = row == OWN - 1
        whole = count == MOST
        counts = (count, count, jnp.where(whole, 0, count) if last else count)
        total = summed(counts, 1, pieces, filter_spec, far_ref.shape[1])
        mixed_grad = untransform(total, inverse_ref, inverse_low_ref)
        if last:
            mixed_grad = mixed_grad + jnp.where(whole, far_ref[pl.ds(0, ROW), :], 0.0)
        key_grad_ref[rows, :] = (
            mixed_grad * value_ref[rows, :].astype(jnp.float32)
        ).astype(jnp.bfloat16)
        value_grad_ref[rows, :] = (
            mixed_grad * key_ref[rows, :].astype(jnp.float32)
        ).astype(jnp.bfloat16)


ROLES = np.array([[3, 0, 1, 2], [2, 3, 1, 0], [0, 1, 3, 2], [0, 1, 2, 3]], np.int32)


def scalars(document_rows, first_row, owner_split):
    count = document_rows.shape[0]
    index = jnp.arange(count, dtype=jnp.int32)
    ends = jnp.sum(
        jnp.where(index[None, :] <= index[:, None], document_rows[None, :], 0), axis=1
    )
    row = first_row + jnp.arange(-OWN, OWN + 1, dtype=jnp.int32)
    passed = ends[None, :] <= row[:, None]
    starts = jnp.max(jnp.where(passed, ends[None, :], 0), axis=1)
    stops = jnp.min(jnp.where(passed, jnp.int32(1 << 20), ends[None, :]), axis=1)
    ahead = jnp.where(row >= 0, stops - row, 0)
    behind = row + 1 - starts
    seq = first_row // OWN
    block = jnp.arange(MOST, dtype=jnp.int32)
    index4 = jnp.arange(4, dtype=jnp.int32)
    if owner_split:
        owner = block * owner_split // MOST
        use_back = (owner >= seq).astype(jnp.int32)
        use_front = (owner <= seq).astype(jnp.int32)
        roles = jnp.sum(jnp.where(index4[:, None] == seq, ROLES, 0), axis=0)
    else:
        use_back = jnp.ones_like(block)
        use_front = jnp.zeros_like(block)
        roles = index4
    ahead = ahead[: 2 * OWN]
    return jnp.concatenate(
        [behind[OWN : 2 * OWN], ahead[OWN:], ahead, use_back, use_front, behind[2 * OWN :], roles]
    )


def add_kernel(one_ref, two_ref, out_ref):
    out_ref[...] = one_ref[...] + two_ref[...]


def step(rows, by, first=0):
    length = lax.axis_size("seq")
    pairs = [(i, i + 1) for i in range(first, length - 1)]
    if by < 0:
        pairs = [(length - 1 - i, length - 1 - j) for i, j in pairs]
    return lax.ppermute(rows, "seq", pairs)


def first_sums(early, roles, rows_far):
    hand, turn, outward, keep = roles
    in_first = lax.ppermute(early[0], "seq", [(3, 2)])
    in_second = lax.ppermute(early[1], "seq", [(3, 2)])
    in_end = lax.ppermute(early[1], "seq", [(0, 1)])
    hand, turn, rows_far = lax.optimization_barrier((hand + in_first, turn, rows_far))
    in_far = lax.ppermute(hand, "seq", [(1, 3), (2, 0)])
    return (keep + in_end, in_far, turn, outward, in_second), rows_far


def last_sums(pending):
    kept, in_far, turn, outward, in_second = pending
    in_side = lax.ppermute(outward, "seq", [(2, 3), (1, 0)])
    block = pl.BlockSpec((ROW, turn.shape[1]), lambda j: (j, 0))
    turn = pl.pallas_call(
        add_kernel,
        grid=(turn.shape[0] // ROW,),
        in_specs=[block] * 2,
        out_specs=block,
        out_shape=jax.ShapeDtypeStruct(turn.shape, turn.dtype),
        compiler_params=pltpu.CompilerParams(vmem_limit_bytes=8 * 1024 * 1024),
        cost_estimate=pl.CostEstimate(flops=1, bytes_accessed=1, transcendentals=0),
        name="add_terms",
    )(turn, in_second)
    return kept + in_side + in_far + lax.ppermute(turn, "seq", [(1, 2), (2, 1)])


def body(query_in, key_in, value_in, out_grad, document_rows, long_filter):
    seq_count = lax.axis_size("seq")
    tokens, channels = query_in.shape
    total_rows = tokens // ROW * seq_count
    wide = jnp.float32
    far = (MOST - 1 - OWN) * ROW

    def mixed(low, high):
        return key_in[low:high].astype(wide) * value_in[low:high].astype(wide)

    def upstream(low, high):
        return out_grad[low:high].astype(wide) * query_in[low:high].astype(wide)

    behind_tail = step(mixed(ROW, tokens), 1)
    ahead_head = step(upstream(0, far), -1)
    behind_head = step(mixed(0, ROW), 1)
    ahead_tail = step(upstream(far, tokens), -1)
    first_row = lax.axis_index("seq") * OWN
    table = scalars(document_rows, first_row, 4 if seq_count == 4 else 0)
    tables = dft_tables()

    tile = min(channels, 256)
    fixed = [pl.BlockSpec(memory_space=pltpu.SMEM)] + [
        pl.BlockSpec(t.shape, lambda j: (0, 0)) for t in tables
    ]

    def flat(rows, dtype=wide):
        return (
            pl.BlockSpec((rows, tile), lambda j: (0, j)),
            jax.ShapeDtypeStruct((rows, channels), dtype),
            None,
        )

    def spectra(rows):
        return (
            pl.BlockSpec((rows, 2 * ROW, tile), lambda j: (0, 0, j)),
            jax.ShapeDtypeStruct((rows, 2 * ROW, channels), wide),
            pltpu.VMEM((rows, 2 * ROW, tile), wide),
        )

    def call(kernel, cost, ins, outs, scratch, operands):
        return pl.pallas_call(
            kernel,
            grid=(channels // tile,),
            in_specs=fixed + [i[0] for i in ins],
            out_specs=[o[0] for o in outs],
            out_shape=[o[1] for o in outs],
            scratch_shapes=[x[2] for x in scratch],
            compiler_params=pltpu.CompilerParams(vmem_limit_bytes=44 * 1024 * 1024),
            cost_estimate=pl.CostEstimate(
                flops=cost, bytes_accessed=1_000_000, transcendentals=0
            ),
        )(table, *tables, *operands)

    narrow = flat(tokens, jnp.bfloat16)
    share, row, rows = flat(2 * ROW), flat(ROW), flat(far)
    own, every = spectra(OWN), spectra(MOST)
    mixed_spec, grad_spec, filter_spec, first, second = call(
        own_kernel,
        C0,
        [narrow] * 4 + [flat(MOST * ROW)],
        [own, own, every, share, share],
        [own],
        (query_in, key_in, value_in, out_grad, long_filter),
    )
    half = flat(2 * ROW)
    upper = (
        pl.BlockSpec((OWN, 2 * ROW, tile), lambda j: (1, 0, j)),
        every[1],
        None,
    )
    right, left = call(
        forward_kernel,
        CP,
        [rows, rows, upper],
        [half, half],
        [],
        (behind_tail, ahead_head, filter_spec),
    )
    far_behind = step(right, 1, first=1)
    far_ahead = step(left, -1, first=1)
    roles = call(
        pair_kernel,
        C1,
        [rows, row, rows, row] + [narrow] * 4 + [share, share],
        [share] * 4,
        [own] * 4 + [spectra(2)],
        (behind_tail, behind_head, ahead_head, ahead_tail)
        + (query_in, key_in, value_in, out_grad, first, second),
    )
    if seq_count == 4:
        pending, (far_behind, far_ahead) = first_sums(
            (first, second), roles, (far_behind, far_ahead)
        )
    (query_grad,) = call(
        query_kernel,
        C2,
        [half, row, rows, own, every, narrow],
        [narrow],
        [spectra(FAR), own],
        (far_behind, behind_head, behind_tail, mixed_spec, filter_spec, out_grad),
    )
    if seq_count == 4:
        kept, in_far, turn, outward, in_second = pending
        turn, outward, query_grad = lax.optimization_barrier((turn, outward, query_grad))
        in_far, far_ahead = lax.optimization_barrier((in_far, far_ahead))
        filter_grad = last_sums((kept, in_far, turn, outward, in_second))
    else:
        filter_grad = lax.psum_scatter(
            jnp.concatenate(roles, axis=0), "seq", scatter_dimension=0, tiled=True
        )
    key_grad, value_grad = call(
        key_value_kernel,
        C3,
        [half, rows, row, own, every, narrow, narrow],
        [narrow, narrow],
        [spectra(FAR), own],
        (far_ahead, ahead_head, ahead_tail, grad_spec, filter_spec, key_in, value_in),
    )
    return query_grad, key_grad, value_grad, filter_grad * (1.0 / math.sqrt(total_rows * ROW))


def solution(mesh):
    tokens = P(("groups", "seq"), "chan")
    return jax.shard_map(
        body,
        mesh=mesh,
        in_specs=(tokens,) * 4 + (P("groups"), P(None, "chan")),
        out_specs=(tokens,) * 4,
        check_vma=False,
    )
```

```python
import functools
import math

import jax
import jax.numpy as jnp
import ml_dtypes
import numpy as np
from jax import lax
from jax.experimental import pallas as pl
from jax.experimental.pallas import tpu as pltpu
from jax.sharding import PartitionSpec as P

ROW = 128
MOST = 8
HALF = ROW // 2
OWN = 4
FAR = 2
CHUNK = 32
G = 20_000_000_000
CP, C0, C1, C2, C3 = 1, G, G // 2, G // 4, G // 4


def split_table(table):
    high = table.astype(ml_dtypes.bfloat16)
    low = (table - high.astype(np.float64)).astype(ml_dtypes.bfloat16)
    return high, low


def dft_tables():
    order = np.concatenate([np.arange(0, ROW, 2), np.arange(1, ROW, 2)])
    phase = np.outer(2 * order + 1, np.arange(ROW)) % (4 * ROW) * (math.pi / (2 * ROW))
    forward = np.concatenate([np.cos(phase), -np.sin(phase)], axis=0)
    high, low = split_table(forward)
    inv_high, inv_low = split_table(forward.T / ROW)
    return (
        np.concatenate([high, high], axis=1),
        low,
        np.concatenate([inv_high, inv_low], axis=0),
    )


def halves(value):
    high = value.astype(jnp.bfloat16)
    low = (value - high.astype(jnp.float32)).astype(jnp.bfloat16)
    return high, low


def matmul(one, two):
    return jnp.dot(one, two, preferred_element_type=jnp.float32)


def transform(signal, forward_ref, forward_low_ref):
    high, low = halves(signal)
    return matmul(forward_ref[...], jnp.concatenate([high, low], axis=0)) + matmul(
        forward_low_ref[...], high
    )


def untransform(spectrum, inverse_ref):
    high, low = halves(spectrum)
    both = matmul(inverse_ref[...], high)
    return both[:ROW] + (both[ROW:] + matmul(inverse_ref[pl.ds(0, ROW), :], low))


def turned(spectrum, sign):
    real, imag = spectrum[:ROW], spectrum[ROW:]
    plus = lambda part: jnp.concatenate([part[:HALF], -part[HALF:]], axis=0)
    minus = lambda part: jnp.concatenate([-part[:HALF], part[HALF:]], axis=0)
    if sign > 0:
        return jnp.concatenate([minus(imag), plus(real)], axis=0)
    return jnp.concatenate([plus(imag), minus(real)], axis=0)


def multiply_add(total, offset, one_ref, one, two_ref, two):
    for part in range(4):
        real = pl.ds(part * 32, 32)
        imag = pl.ds(ROW + part * 32, 32)
        one_re, one_im = one_ref[one, real, :], one_ref[one, imag, :]
        two_re, two_im = two_ref[two, real, :], two_ref[two, imag, :]
        total[offset, real, :] += one_re * two_re + one_im * two_im
        total[offset, imag, :] += one_re * two_im - one_im * two_re


def own_kernel(
    table_ref,
    forward_ref,
    forward_low_ref,
    inverse_ref,
    query_ref,
    key_ref,
    value_ref,
    out_grad_ref,
    filter_ref,
    mixed_spec,
    grad_spec,
    filter_spec,
    first_ref,
    second_ref,
    near,
):
    wide = jnp.float32
    for row in range(OWN):
        rows = pl.ds(row * ROW, ROW)
        mixed_spec[row] = transform(
            key_ref[rows, :].astype(wide) * value_ref[rows, :].astype(wide),
            forward_ref,
            forward_low_ref,
        )
        grad_spec[row] = transform(
            out_grad_ref[rows, :].astype(wide) * query_ref[rows, :].astype(wide),
            forward_ref,
            forward_low_ref,
        )
    near[...] = jnp.zeros_like(near)
    for source in range(OWN):
        stop = jnp.minimum(table_ref[3 * OWN + source], OWN - source)

        @pl.loop(0, stop)
        def _(offset):
            multiply_add(near, offset, mixed_spec, source, grad_spec, source + offset)

    for block in range(OWN):
        spectrum = near[block]
        if block + 1 < OWN:
            spectrum = spectrum + turned(near[block + 1], -1)
        out_ref = (first_ref, second_ref)[block // 2]
        out_ref[pl.ds(block % 2 * ROW, ROW), :] = untransform(
            spectrum, inverse_ref
        )
    before = None
    for offset in range(MOST):
        plain = transform(filter_ref[pl.ds(offset * ROW, ROW), :], forward_ref, forward_low_ref)
        filter_spec[offset] = plain if before is None else plain + turned(before, 1)
        before = plain


def fill(spec_ref, used, pieces, tables):
    @pl.when(used)
    def _():
        for row, (refs, place) in enumerate(pieces):
            rows = pl.ds(place * ROW, ROW)
            signal = refs[0][rows, :].astype(jnp.float32)
            for ref in refs[1:]:
                signal = signal * ref[rows, :].astype(jnp.float32)
            spec_ref[row] = transform(signal, *tables)


def behind_pieces(head_ref, tail_ref):
    return [((head_ref,), 0)] + [((tail_ref,), row) for row in range(OWN - 1)]


def ahead_pieces(head_ref, tail_ref):
    return [((head_ref,), row) for row in range(OWN - 1)] + [((tail_ref,), 0)]


def pair_sums(ranges, owner, mixed_spec, grad_spec, spectrum):
    width = spectrum.shape[2]
    zeros = (jnp.zeros((CHUNK, width), jnp.float32),) * 2

    def gathered(offset, real, imag):
        def one_step(row, totals):
            one_re = mixed_spec[row + OWN, real, :]
            one_im = mixed_spec[row + OWN, imag, :]
            two_re = grad_spec[row + offset, real, :]
            two_im = grad_spec[row + offset, imag, :]
            return (
                totals[0] + (one_re * two_re + one_im * two_im),
                totals[1] + (one_re * two_im - one_im * two_re),
            )

        total = zeros
        for low, high in ranges.get(offset, ()):
            total = lax.fori_loop(low, high, one_step, total)
        return total

    for part in range(ROW // CHUNK):
        real = pl.ds(part * CHUNK, CHUNK)
        imag = pl.ds(ROW + part * CHUNK, CHUNK)
        sign = 1.0 if part * CHUNK < HALF else -1.0
        now_re, now_im = gathered(2 * owner, real, imag)
        for place in range(2):
            next_re, next_im = gathered(2 * owner + place + 1, real, imag)
            spectrum[place, real, :] = now_re + sign * next_im
            spectrum[place, imag, :] = now_im - sign * next_re
            now_re, now_im = next_re, next_im


def pair_kernel(
    table_ref,
    forward_ref,
    forward_low_ref,
    inverse_ref,
    behind_tail_ref,
    behind_head_ref,
    ahead_head_ref,
    ahead_tail_ref,
    query_ref,
    key_ref,
    value_ref,
    out_grad_ref,
    first_ref,
    second_ref,
    hand_ref,
    turn_ref,
    outward_ref,
    keep_ref,
    mixed_spec,
    grad_spec,
    spectrum,
):
    before_own = jnp.minimum(table_ref[0] - 1, OWN)
    from_own = table_ref[3 * OWN - 1] - 1
    before_next = jnp.minimum(table_ref[4 * OWN + 2 * MOST] - 1, OWN)
    from_next = jnp.minimum(table_ref[2 * OWN - 1] - 1, OWN)

    tables = (forward_ref, forward_low_ref)
    own_mixed = [((key_ref, value_ref), row) for row in range(OWN)]
    own_grad = [((out_grad_ref, query_ref), row) for row in range(OWN)]
    behind = behind_pieces(behind_head_ref, behind_tail_ref)
    ahead = ahead_pieces(ahead_head_ref, ahead_tail_ref)
    own_part, ahead_part = pl.ds(OWN, OWN), pl.ds(OWN, OWN)
    fill(mixed_spec, before_own > 0, behind, tables)
    fill(grad_spec, before_own > 0, own_grad, tables)
    fill(mixed_spec.at[own_part], before_next > 0, own_mixed, tables)
    fill(grad_spec.at[ahead_part], before_next > 0, ahead, tables)

    for owner in range(MOST // 2):
        use_back = table_ref[4 * OWN + 2 * owner] > 0
        use_front = table_ref[4 * OWN + MOST + 2 * owner] > 0
        ranges = {}
        for offset in range(max(1, 2 * owner), min(MOST, 2 * owner + 3)):
            low = jnp.maximum(-before_own, jnp.where(use_back, -offset, OWN - offset))
            high = jnp.minimum(0, jnp.minimum(from_own, 2 * OWN) - offset)
            next_low = jnp.maximum(OWN - before_next, OWN - offset)
            next_high = jnp.where(use_front, jnp.minimum(OWN, OWN + from_next - offset), 0)
            ranges[offset] = ((low, high), (next_low, next_high))
        busy = functools.reduce(
            jnp.logical_or, [high > low for both in ranges.values() for low, high in both]
        )
        role = table_ref[4 * OWN + 2 * MOST + 1 + owner]
        outs = (hand_ref, turn_ref, outward_ref, keep_ref)
        own_ref = (first_ref, second_ref)[owner] if owner < 2 else None
        for kind, out_ref in enumerate(outs):

            @pl.when(jnp.logical_and(role == kind, jnp.logical_not(busy)))
            def _():
                out_ref[...] = jnp.zeros_like(out_ref) if own_ref is None else own_ref[...]

        @pl.when(busy)
        def _():
            pair_sums(ranges, owner, mixed_spec, grad_spec, spectrum)
            for place in range(2):
                rows = pl.ds(place * ROW, ROW)
                taps = untransform(spectrum[place], inverse_ref)
                if own_ref is not None:
                    taps = taps + own_ref[rows, :]
                for kind, out_ref in enumerate(outs):

                    @pl.when(role == kind)
                    def _():
                        out_ref[rows, :] = taps


def forward_kernel(
    table_ref,
    forward_ref,
    forward_low_ref,
    inverse_ref,
    behind_ref,
    ahead_ref,
    filter_spec,
    right_ref,
    left_ref,
):
    right_ref[...] = behind_ref[pl.ds(ROW, 2 * ROW), :]
    left_ref[...] = ahead_ref[pl.ds(0, 2 * ROW), :]

    def parts(spectrum):
        return spectrum[:ROW], spectrum[ROW:]

    @pl.when(table_ref[4 * OWN + 2 * MOST] == MOST)
    def _():
        total_re, total_im = 0.0, 0.0
        for row in range(3):
            signal = behind_ref[pl.ds(row * ROW, ROW), :]
            one_re, one_im = parts(transform(signal, forward_ref, forward_low_ref))
            two_re, two_im = parts(filter_spec[3 - row])
            total_re = total_re + (one_re * two_re - one_im * two_im)
            total_im = total_im + (one_re * two_im + one_im * two_re)
        right_ref[pl.ds(0, ROW), :] = untransform(
            jnp.concatenate([total_re, total_im], axis=0), inverse_ref
        )

    @pl.when(table_ref[3 * OWN - 1] == MOST)
    def _():
        total_re, total_im = 0.0, 0.0
        for row in range(3):
            signal = ahead_ref[pl.ds(row * ROW, ROW), :]
            one_re, one_im = parts(transform(signal, forward_ref, forward_low_ref))
            two_re, two_im = parts(filter_spec[1 + row])
            total_re = total_re + (two_re * one_re + two_im * one_im)
            total_im = total_im + (two_re * one_im - two_im * one_re)
        left_ref[pl.ds(0, ROW), :] = untransform(
            jnp.concatenate([total_re, total_im], axis=0), inverse_ref
        )


def summed(counts, direction, pieces, filter_spec, width):
    reals, imags = [], []
    for part in range(4):
        real = pl.ds(part * 32, 32)
        imag = pl.ds(ROW + part * 32, 32)
        total = (jnp.zeros((32, width), jnp.float32),) * 2
        for count, (ref, first, low, high) in zip(counts, pieces):

            def one_step(offset, totals):
                row = first + direction * offset
                one_re, one_im = ref[row, real, :], ref[row, imag, :]
                two_re, two_im = filter_spec[offset, real, :], filter_spec[offset, imag, :]
                if direction < 0:
                    return (
                        totals[0] + (one_re * two_re - one_im * two_im),
                        totals[1] + (one_re * two_im + one_im * two_re),
                    )
                return (
                    totals[0] + (two_re * one_re + two_im * one_im),
                    totals[1] + (two_re * one_im - two_im * one_re),
                )

            total = lax.fori_loop(low, jnp.minimum(count, high), one_step, total)
        reals.append(total[0])
        imags.append(total[1])
    return jnp.concatenate(reals + imags, axis=0)


def query_kernel(
    table_ref,
    forward_ref,
    forward_low_ref,
    inverse_ref,
    far_ref,
    head_ref,
    tail_ref,
    own_spec,
    filter_spec,
    out_grad_ref,
    query_grad_ref,
    far_spec,
    behind_spec,
):
    reach = table_ref[0] - 1
    tables = (forward_ref, forward_low_ref)
    fill(behind_spec, reach > 0, behind_pieces(head_ref, tail_ref), tables)
    used = jnp.logical_and(reach > OWN, reach < MOST - 1)
    fill(far_spec, used, [((far_ref,), row) for row in range(FAR)], tables)

    for row in range(OWN):
        rows = pl.ds(row * ROW, ROW)
        pieces = (
            (own_spec, row, 0, row + 1),
            (behind_spec, row + OWN, row + 1, row + 1 + OWN),
            (far_spec, row + OWN + FAR, row + 1 + OWN, min(MOST, row + 1 + OWN + FAR)),
        )
        count = jnp.minimum(table_ref[row], MOST)
        whole = count == MOST
        counts = (count, count, jnp.where(whole, 0, count) if row == 0 else count)
        total = summed(counts, -1, pieces, filter_spec, far_ref.shape[1])
        convolved = untransform(total, inverse_ref)
        if row == 0:
            convolved = convolved + jnp.where(whole, far_ref[pl.ds(0, ROW), :], 0.0)
        query_grad_ref[rows, :] = (
            out_grad_ref[rows, :].astype(jnp.float32) * convolved
        ).astype(jnp.bfloat16)


def key_value_kernel(
    table_ref,
    forward_ref,
    forward_low_ref,
    inverse_ref,
    far_ref,
    head_ref,
    tail_ref,
    own_spec,
    filter_spec,
    key_ref,
    value_ref,
    key_grad_ref,
    value_grad_ref,
    far_spec,
    ahead_spec,
):
    reach = table_ref[2 * OWN - 1] - 1
    tables = (forward_ref, forward_low_ref)
    fill(ahead_spec, reach > 0, ahead_pieces(head_ref, tail_ref), tables)
    used = jnp.logical_and(reach > OWN, reach < MOST - 1)
    fill(far_spec, used, [((far_ref,), row) for row in range(FAR)], tables)

    for row in range(OWN):
        rows = pl.ds(row * ROW, ROW)
        pieces = (
            (own_spec, row, 0, OWN - row),
            (ahead_spec, row - OWN, OWN - row, 2 * OWN - row),
            (far_spec, row - 2 * OWN, 2 * OWN - row, min(MOST, 2 * OWN + FAR - row)),
        )
        count = jnp.minimum(table_ref[OWN + row], MOST)
        last = row == OWN - 1
        whole = count == MOST
        counts = (count, count, jnp.where(whole, 0, count) if last else count)
        total = summed(counts, 1, pieces, filter_spec, far_ref.shape[1])
        mixed_grad = untransform(total, inverse_ref)
        if last:
            mixed_grad = mixed_grad + jnp.where(whole, far_ref[pl.ds(0, ROW), :], 0.0)
        key_grad_ref[rows, :] = (
            mixed_grad * value_ref[rows, :].astype(jnp.float32)
        ).astype(jnp.bfloat16)
        value_grad_ref[rows, :] = (
            mixed_grad * key_ref[rows, :].astype(jnp.float32)
        ).astype(jnp.bfloat16)


ROLES = np.array([[3, 0, 1, 2], [2, 3, 1, 0], [0, 1, 3, 2], [0, 1, 2, 3]], np.int32)


def scalars(document_rows, first_row, owner_split):
    count = document_rows.shape[0]
    index = jnp.arange(count, dtype=jnp.int32)
    ends = jnp.sum(
        jnp.where(index[None, :] <= index[:, None], document_rows[None, :], 0), axis=1
    )
    row = first_row + jnp.arange(-OWN, OWN + 1, dtype=jnp.int32)
    passed = ends[None, :] <= row[:, None]
    starts = jnp.max(jnp.where(passed, ends[None, :], 0), axis=1)
    stops = jnp.min(jnp.where(passed, jnp.int32(1 << 20), ends[None, :]), axis=1)
    ahead = jnp.where(row >= 0, stops - row, 0)
    behind = row + 1 - starts
    seq = first_row // OWN
    block = jnp.arange(MOST, dtype=jnp.int32)
    index4 = jnp.arange(4, dtype=jnp.int32)
    if owner_split:
        owner = block * owner_split // MOST
        use_back = (owner >= seq).astype(jnp.int32)
        use_front = (owner <= seq).astype(jnp.int32)
        roles = jnp.sum(jnp.where(index4[:, None] == seq, ROLES, 0), axis=0)
    else:
        use_back = jnp.ones_like(block)
        use_front = jnp.zeros_like(block)
        roles = index4
    ahead = ahead[: 2 * OWN]
    return jnp.concatenate(
        [behind[OWN : 2 * OWN], ahead[OWN:], ahead, use_back, use_front, behind[2 * OWN :], roles]
    )


def add_kernel(one_ref, two_ref, out_ref):
    out_ref[...] = one_ref[...] + two_ref[...]


def step(rows, by, first=0):
    length = lax.axis_size("seq")
    pairs = [(i, i + 1) for i in range(first, length - 1)]
    if by < 0:
        pairs = [(length - 1 - i, length - 1 - j) for i, j in pairs]
    return lax.ppermute(rows, "seq", pairs)


def first_sums(early, roles, rows_far):
    hand, turn, outward, keep = roles
    in_first = lax.ppermute(early[0], "seq", [(3, 2)])
    in_second = lax.ppermute(early[1], "seq", [(3, 2)])
    in_end = lax.ppermute(early[1], "seq", [(0, 1)])
    hand, turn, rows_far = lax.optimization_barrier((hand + in_first, turn, rows_far))
    in_far = lax.ppermute(hand, "seq", [(1, 3), (2, 0)])
    return (keep + in_end, in_far, turn, outward, in_second), rows_far


def last_sums(pending):
    kept, in_far, turn, outward, in_second = pending
    in_side = lax.ppermute(outward, "seq", [(2, 3), (1, 0)])
    block = pl.BlockSpec((ROW, turn.shape[1]), lambda j: (j, 0))
    turn = pl.pallas_call(
        add_kernel,
        grid=(turn.shape[0] // ROW,),
        in_specs=[block] * 2,
        out_specs=block,
        out_shape=jax.ShapeDtypeStruct(turn.shape, turn.dtype),
        compiler_params=pltpu.CompilerParams(vmem_limit_bytes=8 * 1024 * 1024),
        cost_estimate=pl.CostEstimate(flops=1, bytes_accessed=1, transcendentals=0),
        name="add_terms",
    )(turn, in_second)
    return kept + in_side + in_far + lax.ppermute(turn, "seq", [(1, 2), (2, 1)])


def body(query_in, key_in, value_in, out_grad, document_rows, long_filter):
    seq_count = lax.axis_size("seq")
    tokens, channels = query_in.shape
    total_rows = tokens // ROW * seq_count
    wide = jnp.float32
    far = (MOST - 1 - OWN) * ROW

    def mixed(low, high):
        return key_in[low:high].astype(wide) * value_in[low:high].astype(wide)

    def upstream(low, high):
        return out_grad[low:high].astype(wide) * query_in[low:high].astype(wide)

    behind_tail = step(mixed(ROW, tokens), 1)
    ahead_head = step(upstream(0, far), -1)
    behind_head = step(mixed(0, ROW), 1)
    ahead_tail = step(upstream(far, tokens), -1)
    first_row = lax.axis_index("seq") * OWN
    table = scalars(document_rows, first_row, 4 if seq_count == 4 else 0)
    tables = dft_tables()

    narrow_tile, wide_tile = min(channels, 256), min(channels, 512)
    fixed = [pl.BlockSpec(memory_space=pltpu.SMEM)] + [
        pl.BlockSpec(t.shape, lambda j: (0, 0)) for t in tables
    ]

    def flat(rows, dtype=wide):
        return (
            lambda tile: pl.BlockSpec((rows, tile), lambda j: (0, j)),
            jax.ShapeDtypeStruct((rows, channels), dtype),
            None,
        )

    def spectra(rows):
        return (
            lambda tile: pl.BlockSpec((rows, 2 * ROW, tile), lambda j: (0, 0, j)),
            jax.ShapeDtypeStruct((rows, 2 * ROW, channels), wide),
            lambda tile: pltpu.VMEM((rows, 2 * ROW, tile), wide),
        )

    def call(kernel, cost, ins, outs, scratch, operands, tile=narrow_tile):
        return pl.pallas_call(
            kernel,
            grid=(channels // tile,),
            in_specs=fixed + [i[0](tile) for i in ins],
            out_specs=[o[0](tile) for o in outs],
            out_shape=[o[1] for o in outs],
            scratch_shapes=[x[2](tile) for x in scratch],
            compiler_params=pltpu.CompilerParams(vmem_limit_bytes=(44 if tile == narrow_tile else 52) * 1024 * 1024),
            cost_estimate=pl.CostEstimate(
                flops=cost, bytes_accessed=1_000_000, transcendentals=0
            ),
        )(table, *tables, *operands)

    narrow = flat(tokens, jnp.bfloat16)
    share, row, rows = flat(2 * ROW), flat(ROW), flat(far)
    own, every = spectra(OWN), spectra(MOST)
    mixed_spec, grad_spec, filter_spec, first, second = call(
        own_kernel,
        C0,
        [narrow] * 4 + [flat(MOST * ROW)],
        [own, own, every, share, share],
        [own],
        (query_in, key_in, value_in, out_grad, long_filter),
    )
    half = flat(2 * ROW)
    upper = (
        lambda tile: pl.BlockSpec((OWN, 2 * ROW, tile), lambda j: (1, 0, j)),
        every[1],
        None,
    )
    right, left = call(
        forward_kernel,
        CP,
        [rows, rows, upper],
        [half, half],
        [],
        (behind_tail, ahead_head, filter_spec),
    )
    far_behind = step(right, 1, first=1)
    far_ahead = step(left, -1, first=1)
    roles = call(
        pair_kernel,
        C1,
        [rows, row, rows, row] + [narrow] * 4 + [share, share],
        [share] * 4,
        [every] * 2 + [spectra(2)],
        (behind_tail, behind_head, ahead_head, ahead_tail)
        + (query_in, key_in, value_in, out_grad, first, second),
        wide_tile,
    )
    if seq_count == 4:
        pending, (far_behind, far_ahead) = first_sums(
            (first, second), roles, (far_behind, far_ahead)
        )
    (query_grad,) = call(
        query_kernel,
        C2,
        [half, row, rows, own, every, narrow],
        [narrow],
        [spectra(FAR), own],
        (far_behind, behind_head, behind_tail, mixed_spec, filter_spec, out_grad),
    )
    if seq_count == 4:
        kept, in_far, turn, outward, in_second = pending
        turn, outward, query_grad = lax.optimization_barrier((turn, outward, query_grad))
        in_far, far_ahead = lax.optimization_barrier((in_far, far_ahead))
        filter_grad = last_sums((kept, in_far, turn, outward, in_second))
    else:
        filter_grad = lax.psum_scatter(
            jnp.concatenate(roles, axis=0), "seq", scatter_dimension=0, tiled=True
        )
    key_grad, value_grad = call(
        key_value_kernel,
        C3,
        [half, rows, row, own, every, narrow, narrow],
        [narrow, narrow],
        [spectra(FAR), own],
        (far_ahead, ahead_head, ahead_tail, grad_spec, filter_spec, key_in, value_in),
    )
    return query_grad, key_grad, value_grad, filter_grad * (1.0 / math.sqrt(total_rows * ROW))


def solution(mesh):
    tokens = P(("groups", "seq"), "chan")
    return jax.shard_map(
        body,
        mesh=mesh,
        in_specs=(tokens,) * 4 + (P("groups"), P(None, "chan")),
        out_specs=(tokens,) * 4,
        check_vma=False,
    )
```

```python
import functools
import math

import jax
import jax.numpy as jnp
import ml_dtypes
import numpy as np
from jax import lax
from jax.experimental import pallas as pl
from jax.experimental.pallas import tpu as pltpu
from jax.sharding import PartitionSpec as P

ROW = 128
MOST = 8
HALF = ROW // 2
OWN = 4
FAR = 2
CHUNK = 32
G = 20_000_000_000
CP, C0, C1, C2, C3 = 1, G, G // 2, G // 4, G // 4


def split_table(table):
    high = table.astype(ml_dtypes.bfloat16)
    low = (table - high.astype(np.float64)).astype(ml_dtypes.bfloat16)
    return high, low


def dft_tables():
    order = np.concatenate([np.arange(0, ROW, 2), np.arange(1, ROW, 2)])
    phase = np.outer(2 * order + 1, np.arange(ROW)) % (4 * ROW) * (math.pi / (2 * ROW))
    forward = np.concatenate([np.cos(phase), -np.sin(phase)], axis=0)
    high, low = split_table(forward)
    inv_high, inv_low = split_table(forward.T / ROW)
    return (
        np.concatenate([high, high], axis=1),
        low,
        np.concatenate([inv_high, inv_low], axis=0),
    )


def halves(value):
    high = value.astype(jnp.bfloat16)
    low = (value - high.astype(jnp.float32)).astype(jnp.bfloat16)
    return high, low


def matmul(one, two):
    return jnp.dot(one, two, preferred_element_type=jnp.float32)


def transform(signal, forward_ref, forward_low_ref):
    high, low = halves(signal)
    return matmul(forward_ref[...], jnp.concatenate([high, low], axis=0)) + matmul(
        forward_low_ref[...], high
    )


def untransform(spectrum, inverse_ref):
    high, low = halves(spectrum)
    both = matmul(inverse_ref[...], high)
    return both[:ROW] + (both[ROW:] + matmul(inverse_ref[pl.ds(0, ROW), :], low))


def turned(spectrum, sign):
    real, imag = spectrum[:ROW], spectrum[ROW:]
    plus = lambda part: jnp.concatenate([part[:HALF], -part[HALF:]], axis=0)
    minus = lambda part: jnp.concatenate([-part[:HALF], part[HALF:]], axis=0)
    if sign > 0:
        return jnp.concatenate([minus(imag), plus(real)], axis=0)
    return jnp.concatenate([plus(imag), minus(real)], axis=0)


def multiply_add(total, offset, one_ref, one, two_ref, two):
    for part in range(4):
        real = pl.ds(part * 32, 32)
        imag = pl.ds(ROW + part * 32, 32)
        one_re, one_im = one_ref[one, real, :], one_ref[one, imag, :]
        two_re, two_im = two_ref[two, real, :], two_ref[two, imag, :]
        total[offset, real, :] += one_re * two_re + one_im * two_im
        total[offset, imag, :] += one_re * two_im - one_im * two_re


def own_kernel(
    table_ref,
    forward_ref,
    forward_low_ref,
    inverse_ref,
    query_ref,
    key_ref,
    value_ref,
    out_grad_ref,
    filter_ref,
    mixed_spec,
    grad_spec,
    filter_spec,
    first_ref,
    second_ref,
    near,
):
    wide = jnp.float32
    for row in range(OWN):
        rows = pl.ds(row * ROW, ROW)
        mixed_spec[row] = transform(
            key_ref[rows, :].astype(wide) * value_ref[rows, :].astype(wide),
            forward_ref,
            forward_low_ref,
        )
        grad_spec[row] = transform(
            out_grad_ref[rows, :].astype(wide) * query_ref[rows, :].astype(wide),
            forward_ref,
            forward_low_ref,
        )
    near[...] = jnp.zeros_like(near)
    for source in range(OWN):
        stop = jnp.minimum(table_ref[3 * OWN + source], OWN - source)

        @pl.loop(0, stop)
        def _(offset):
            multiply_add(near, offset, mixed_spec, source, grad_spec, source + offset)

    for block in range(OWN):
        spectrum = near[block]
        if block + 1 < OWN:
            spectrum = spectrum + turned(near[block + 1], -1)
        out_ref = (first_ref, second_ref)[block // 2]
        out_ref[pl.ds(block % 2 * ROW, ROW), :] = untransform(
            spectrum, inverse_ref
        )
    before = None
    for offset in range(MOST):
        plain = transform(filter_ref[pl.ds(offset * ROW, ROW), :], forward_ref, forward_low_ref)
        filter_spec[offset] = plain if before is None else plain + turned(before, 1)
        before = plain


def fill(spec_ref, used, pieces, tables):
    @pl.when(used)
    def _():
        for row, (refs, place) in enumerate(pieces):
            rows = pl.ds(place * ROW, ROW)
            signal = refs[0][rows, :].astype(jnp.float32)
            for ref in refs[1:]:
                signal = signal * ref[rows, :].astype(jnp.float32)
            spec_ref[row] = transform(signal, *tables)


def behind_pieces(head_ref, tail_ref):
    return [((head_ref,), 0)] + [((tail_ref,), row) for row in range(OWN - 1)]


def ahead_pieces(head_ref, tail_ref):
    return [((head_ref,), row) for row in range(OWN - 1)] + [((tail_ref,), 0)]


def pair_sums(ranges, owner, mixed_spec, grad_spec, spectrum):
    width = spectrum.shape[2]
    zeros = (jnp.zeros((CHUNK, width), jnp.float32),) * 2

    def gathered(offset, real, imag):
        def one_step(row, totals):
            one_re = mixed_spec[row + OWN, real, :]
            one_im = mixed_spec[row + OWN, imag, :]
            two_re = grad_spec[row + offset, real, :]
            two_im = grad_spec[row + offset, imag, :]
            return (
                totals[0] + (one_re * two_re + one_im * two_im),
                totals[1] + (one_re * two_im - one_im * two_re),
            )

        total = zeros
        for low, high in ranges.get(offset, ()):
            total = lax.fori_loop(low, high, one_step, total)
        return total

    for part in range(ROW // CHUNK):
        real = pl.ds(part * CHUNK, CHUNK)
        imag = pl.ds(ROW + part * CHUNK, CHUNK)
        sign = 1.0 if part * CHUNK < HALF else -1.0
        now_re, now_im = gathered(2 * owner, real, imag)
        for place in range(2):
            next_re, next_im = gathered(2 * owner + place + 1, real, imag)
            spectrum[place, real, :] = now_re + sign * next_im
            spectrum[place, imag, :] = now_im - sign * next_re
            now_re, now_im = next_re, next_im


def pair_kernel(
    table_ref,
    forward_ref,
    forward_low_ref,
    inverse_ref,
    behind_tail_ref,
    behind_head_ref,
    ahead_head_ref,
    ahead_tail_ref,
    query_ref,
    key_ref,
    value_ref,
    out_grad_ref,
    first_ref,
    second_ref,
    hand_ref,
    turn_ref,
    outward_ref,
    keep_ref,
    mixed_spec,
    grad_spec,
    spectrum,
):
    before_own = jnp.minimum(table_ref[0] - 1, OWN)
    from_own = table_ref[3 * OWN - 1] - 1
    before_next = jnp.minimum(table_ref[4 * OWN + 2 * MOST] - 1, OWN)
    from_next = jnp.minimum(table_ref[2 * OWN - 1] - 1, OWN)

    tables = (forward_ref, forward_low_ref)
    own_mixed = [((key_ref, value_ref), row) for row in range(OWN)]
    own_grad = [((out_grad_ref, query_ref), row) for row in range(OWN)]
    behind = behind_pieces(behind_head_ref, behind_tail_ref)
    ahead = ahead_pieces(ahead_head_ref, ahead_tail_ref)
    own_part, ahead_part = pl.ds(OWN, OWN), pl.ds(OWN, OWN)
    fill(mixed_spec, before_own > 0, behind, tables)
    fill(grad_spec, before_own > 0, own_grad, tables)
    fill(mixed_spec.at[own_part], before_next > 0, own_mixed, tables)
    fill(grad_spec.at[ahead_part], before_next > 0, ahead, tables)

    for owner in range(MOST // 2):
        use_back = table_ref[4 * OWN + 2 * owner] > 0
        use_front = table_ref[4 * OWN + MOST + 2 * owner] > 0
        ranges = {}
        for offset in range(max(1, 2 * owner), min(MOST, 2 * owner + 3)):
            low = jnp.maximum(-before_own, jnp.where(use_back, -offset, OWN - offset))
            high = jnp.minimum(0, jnp.minimum(from_own, 2 * OWN) - offset)
            next_low = jnp.maximum(OWN - before_next, OWN - offset)
            next_high = jnp.where(use_front, jnp.minimum(OWN, OWN + from_next - offset), 0)
            ranges[offset] = ((low, high), (next_low, next_high))
        busy = functools.reduce(
            jnp.logical_or, [high > low for both in ranges.values() for low, high in both]
        )
        role = table_ref[4 * OWN + 2 * MOST + 1 + owner]
        outs = (hand_ref, turn_ref, outward_ref, keep_ref)
        own_ref = (first_ref, second_ref)[owner] if owner < 2 else None
        for kind, out_ref in enumerate(outs):

            @pl.when(jnp.logical_and(role == kind, jnp.logical_not(busy)))
            def _():
                out_ref[...] = jnp.zeros_like(out_ref) if own_ref is None else own_ref[...]

        @pl.when(busy)
        def _():
            pair_sums(ranges, owner, mixed_spec, grad_spec, spectrum)
            for place in range(2):
                rows = pl.ds(place * ROW, ROW)
                taps = untransform(spectrum[place], inverse_ref)
                if own_ref is not None:
                    taps = taps + own_ref[rows, :]
                for kind, out_ref in enumerate(outs):

                    @pl.when(role == kind)
                    def _():
                        out_ref[rows, :] = taps


def forward_kernel(
    table_ref,
    forward_ref,
    forward_low_ref,
    inverse_ref,
    behind_ref,
    ahead_ref,
    filter_spec,
    right_ref,
    left_ref,
):
    right_ref[...] = behind_ref[pl.ds(ROW, 2 * ROW), :]
    left_ref[...] = ahead_ref[pl.ds(0, 2 * ROW), :]

    def parts(spectrum):
        return spectrum[:ROW], spectrum[ROW:]

    @pl.when(table_ref[4 * OWN + 2 * MOST] == MOST)
    def _():
        total_re, total_im = 0.0, 0.0
        for row in range(3):
            signal = behind_ref[pl.ds(row * ROW, ROW), :]
            one_re, one_im = parts(transform(signal, forward_ref, forward_low_ref))
            two_re, two_im = parts(filter_spec[3 - row])
            total_re = total_re + (one_re * two_re - one_im * two_im)
            total_im = total_im + (one_re * two_im + one_im * two_re)
        right_ref[pl.ds(0, ROW), :] = untransform(
            jnp.concatenate([total_re, total_im], axis=0), inverse_ref
        )

    @pl.when(table_ref[3 * OWN - 1] == MOST)
    def _():
        total_re, total_im = 0.0, 0.0
        for row in range(3):
            signal = ahead_ref[pl.ds(row * ROW, ROW), :]
            one_re, one_im = parts(transform(signal, forward_ref, forward_low_ref))
            two_re, two_im = parts(filter_spec[1 + row])
            total_re = total_re + (two_re * one_re + two_im * one_im)
            total_im = total_im + (two_re * one_im - two_im * one_re)
        left_ref[pl.ds(0, ROW), :] = untransform(
            jnp.concatenate([total_re, total_im], axis=0), inverse_ref
        )


def summed(counts, direction, pieces, filter_spec, width):
    reals, imags = [], []
    for part in range(4):
        real = pl.ds(part * 32, 32)
        imag = pl.ds(ROW + part * 32, 32)
        total = (jnp.zeros((32, width), jnp.float32),) * 2
        for count, (ref, first, low, high) in zip(counts, pieces):

            def one_step(offset, totals):
                row = first + direction * offset
                one_re, one_im = ref[row, real, :], ref[row, imag, :]
                two_re, two_im = filter_spec[offset, real, :], filter_spec[offset, imag, :]
                if direction < 0:
                    return (
                        totals[0] + (one_re * two_re - one_im * two_im),
                        totals[1] + (one_re * two_im + one_im * two_re),
                    )
                return (
                    totals[0] + (two_re * one_re + two_im * one_im),
                    totals[1] + (two_re * one_im - two_im * one_re),
                )

            total = lax.fori_loop(low, jnp.minimum(count, high), one_step, total)
        reals.append(total[0])
        imags.append(total[1])
    return jnp.concatenate(reals + imags, axis=0)


def query_kernel(
    table_ref,
    forward_ref,
    forward_low_ref,
    inverse_ref,
    far_ref,
    head_ref,
    tail_ref,
    own_spec,
    filter_spec,
    out_grad_ref,
    query_grad_ref,
    far_spec,
    behind_spec,
):
    reach = table_ref[0] - 1
    tables = (forward_ref, forward_low_ref)
    fill(behind_spec, reach > 0, behind_pieces(head_ref, tail_ref), tables)
    used = jnp.logical_and(reach > OWN, reach < MOST - 1)
    fill(far_spec, used, [((far_ref,), row) for row in range(FAR)], tables)

    for row in range(OWN):
        rows = pl.ds(row * ROW, ROW)
        pieces = (
            (own_spec, row, 0, row + 1),
            (behind_spec, row + OWN, row + 1, row + 1 + OWN),
            (far_spec, row + OWN + FAR, row + 1 + OWN, min(MOST, row + 1 + OWN + FAR)),
        )
        count = jnp.minimum(table_ref[row], MOST)
        whole = count == MOST
        counts = (count, count, jnp.where(whole, 0, count) if row == 0 else count)
        total = summed(counts, -1, pieces, filter_spec, far_ref.shape[1])
        convolved = untransform(total, inverse_ref)
        if row == 0:
            convolved = convolved + jnp.where(whole, far_ref[pl.ds(0, ROW), :], 0.0)
        query_grad_ref[rows, :] = (
            out_grad_ref[rows, :].astype(jnp.float32) * convolved
        ).astype(jnp.bfloat16)


def key_value_kernel(
    table_ref,
    forward_ref,
    forward_low_ref,
    inverse_ref,
    far_ref,
    head_ref,
    tail_ref,
    own_spec,
    filter_spec,
    key_ref,
    value_ref,
    key_grad_ref,
    value_grad_ref,
    far_spec,
    ahead_spec,
):
    reach = table_ref[2 * OWN - 1] - 1
    tables = (forward_ref, forward_low_ref)
    fill(ahead_spec, reach > 0, ahead_pieces(head_ref, tail_ref), tables)
    used = jnp.logical_and(reach > OWN, reach < MOST - 1)
    fill(far_spec, used, [((far_ref,), row) for row in range(FAR)], tables)

    for row in range(OWN):
        rows = pl.ds(row * ROW, ROW)
        pieces = (
            (own_spec, row, 0, OWN - row),
            (ahead_spec, row - OWN, OWN - row, 2 * OWN - row),
            (far_spec, row - 2 * OWN, 2 * OWN - row, min(MOST, 2 * OWN + FAR - row)),
        )
        count = jnp.minimum(table_ref[OWN + row], MOST)
        last = row == OWN - 1
        whole = count == MOST
        counts = (count, count, jnp.where(whole, 0, count) if last else count)
        total = summed(counts, 1, pieces, filter_spec, far_ref.shape[1])
        mixed_grad = untransform(total, inverse_ref)
        if last:
            mixed_grad = mixed_grad + jnp.where(whole, far_ref[pl.ds(0, ROW), :], 0.0)
        key_grad_ref[rows, :] = (
            mixed_grad * value_ref[rows, :].astype(jnp.float32)
        ).astype(jnp.bfloat16)
        value_grad_ref[rows, :] = (
            mixed_grad * key_ref[rows, :].astype(jnp.float32)
        ).astype(jnp.bfloat16)


ROLES = np.array([[3, 0, 1, 2], [2, 3, 1, 0], [0, 1, 3, 2], [0, 1, 2, 3]], np.int32)


def scalars(document_rows, first_row, owner_split):
    count = document_rows.shape[0]
    index = jnp.arange(count, dtype=jnp.int32)
    ends = jnp.sum(
        jnp.where(index[None, :] <= index[:, None], document_rows[None, :], 0), axis=1
    )
    row = first_row + jnp.arange(-OWN, OWN + 1, dtype=jnp.int32)
    passed = ends[None, :] <= row[:, None]
    starts = jnp.max(jnp.where(passed, ends[None, :], 0), axis=1)
    stops = jnp.min(jnp.where(passed, jnp.int32(1 << 20), ends[None, :]), axis=1)
    ahead = jnp.where(row >= 0, stops - row, 0)
    behind = row + 1 - starts
    seq = first_row // OWN
    block = jnp.arange(MOST, dtype=jnp.int32)
    index4 = jnp.arange(4, dtype=jnp.int32)
    if owner_split:
        owner = block * owner_split // MOST
        use_back = (owner >= seq).astype(jnp.int32)
        use_front = (owner <= seq).astype(jnp.int32)
        roles = jnp.sum(jnp.where(index4[:, None] == seq, ROLES, 0), axis=0)
    else:
        use_back = jnp.ones_like(block)
        use_front = jnp.zeros_like(block)
        roles = index4
    ahead = ahead[: 2 * OWN]
    return jnp.concatenate(
        [behind[OWN : 2 * OWN], ahead[OWN:], ahead, use_back, use_front, behind[2 * OWN :], roles]
    )


def add_kernel(one_ref, two_ref, out_ref):
    out_ref[...] = one_ref[...] + two_ref[...]


def step(rows, by, first=0):
    length = lax.axis_size("seq")
    pairs = [(i, i + 1) for i in range(first, length - 1)]
    if by < 0:
        pairs = [(length - 1 - i, length - 1 - j) for i, j in pairs]
    return lax.ppermute(rows, "seq", pairs)


def first_sums(early, roles, rows_far):
    hand, turn, outward, keep = roles
    in_first = lax.ppermute(early[0], "seq", [(3, 2)])
    in_second = lax.ppermute(early[1], "seq", [(3, 2)])
    in_end = lax.ppermute(early[1], "seq", [(0, 1)])
    hand, turn, outward, rows_far = lax.optimization_barrier(
        (hand + in_first, turn, outward, rows_far)
    )
    in_far = lax.ppermute(hand, "seq", [(1, 3), (2, 0)])
    in_side = lax.ppermute(outward, "seq", [(2, 3), (1, 0)])
    return (keep + in_end + in_far, in_side, turn, in_second), rows_far


def last_sums(pending):
    kept, in_side, turn, in_second = pending
    block = pl.BlockSpec((ROW, turn.shape[1]), lambda j: (j, 0))
    turn = pl.pallas_call(
        add_kernel,
        grid=(turn.shape[0] // ROW,),
        in_specs=[block] * 2,
        out_specs=block,
        out_shape=jax.ShapeDtypeStruct(turn.shape, turn.dtype),
        compiler_params=pltpu.CompilerParams(vmem_limit_bytes=8 * 1024 * 1024),
        cost_estimate=pl.CostEstimate(flops=1, bytes_accessed=1, transcendentals=0),
        name="add_terms",
    )(turn, in_second)
    return kept + in_side + lax.ppermute(turn, "seq", [(1, 2), (2, 1)])


def body(query_in, key_in, value_in, out_grad, document_rows, long_filter):
    seq_count = lax.axis_size("seq")
    tokens, channels = query_in.shape
    total_rows = tokens // ROW * seq_count
    wide = jnp.float32
    far = (MOST - 1 - OWN) * ROW

    def mixed(low, high):
        return key_in[low:high].astype(wide) * value_in[low:high].astype(wide)

    def upstream(low, high):
        return out_grad[low:high].astype(wide) * query_in[low:high].astype(wide)

    behind_tail = step(mixed(ROW, tokens), 1)
    ahead_head = step(upstream(0, far), -1)
    behind_head = step(mixed(0, ROW), 1)
    ahead_tail = step(upstream(far, tokens), -1)
    first_row = lax.axis_index("seq") * OWN
    table = scalars(document_rows, first_row, 4 if seq_count == 4 else 0)
    tables = dft_tables()

    narrow_tile, wide_tile = min(channels, 256), min(channels, 512)
    fixed = [pl.BlockSpec(memory_space=pltpu.SMEM)] + [
        pl.BlockSpec(t.shape, lambda j: (0, 0)) for t in tables
    ]

    def flat(rows, dtype=wide):
        return (
            lambda tile: pl.BlockSpec((rows, tile), lambda j: (0, j)),
            jax.ShapeDtypeStruct((rows, channels), dtype),
            None,
        )

    def spectra(rows):
        return (
            lambda tile: pl.BlockSpec((rows, 2 * ROW, tile), lambda j: (0, 0, j)),
            jax.ShapeDtypeStruct((rows, 2 * ROW, channels), wide),
            lambda tile: pltpu.VMEM((rows, 2 * ROW, tile), wide),
        )

    def call(kernel, cost, ins, outs, scratch, operands, tile=narrow_tile):
        return pl.pallas_call(
            kernel,
            grid=(channels // tile,),
            in_specs=fixed + [i[0](tile) for i in ins],
            out_specs=[o[0](tile) for o in outs],
            out_shape=[o[1] for o in outs],
            scratch_shapes=[x[2](tile) for x in scratch],
            compiler_params=pltpu.CompilerParams(vmem_limit_bytes=52 * 1024 * 1024),
            cost_estimate=pl.CostEstimate(
                flops=cost, bytes_accessed=1_000_000, transcendentals=0
            ),
        )(table, *tables, *operands)

    narrow = flat(tokens, jnp.bfloat16)
    share, row, rows = flat(2 * ROW), flat(ROW), flat(far)
    own, every = spectra(OWN), spectra(MOST)
    mixed_spec, grad_spec, filter_spec, first, second = call(
        own_kernel,
        C0,
        [narrow] * 4 + [flat(MOST * ROW)],
        [own, own, every, share, share],
        [own],
        (query_in, key_in, value_in, out_grad, long_filter),
    )
    half = flat(2 * ROW)
    upper = (
        lambda tile: pl.BlockSpec((OWN, 2 * ROW, tile), lambda j: (1, 0, j)),
        every[1],
        None,
    )
    right, left = call(
        forward_kernel,
        CP,
        [rows, rows, upper],
        [half, half],
        [],
        (behind_tail, ahead_head, filter_spec),
    )
    far_behind = step(right, 1, first=1)
    far_ahead = step(left, -1, first=1)
    roles = call(
        pair_kernel,
        C1,
        [rows, row, rows, row] + [narrow] * 4 + [share, share],
        [share] * 4,
        [every] * 2 + [spectra(2)],
        (behind_tail, behind_head, ahead_head, ahead_tail)
        + (query_in, key_in, value_in, out_grad, first, second),
        wide_tile,
    )
    if seq_count == 4:
        pending, (far_behind, far_ahead) = first_sums(
            (first, second), roles, (far_behind, far_ahead)
        )
    (query_grad,) = call(
        query_kernel,
        C2,
        [half, row, rows, own, every, narrow],
        [narrow],
        [spectra(FAR), own],
        (far_behind, behind_head, behind_tail, mixed_spec, filter_spec, out_grad),
    )
    if seq_count == 4:
        kept, in_side, turn, in_second = pending
        turn, query_grad = lax.optimization_barrier((turn, query_grad))
        kept, far_ahead = lax.optimization_barrier((kept, far_ahead))
        filter_grad = last_sums((kept, in_side, turn, in_second))
    else:
        filter_grad = lax.psum_scatter(
            jnp.concatenate(roles, axis=0), "seq", scatter_dimension=0, tiled=True
        )
    key_grad, value_grad = call(
        key_value_kernel,
        C3,
        [half, rows, row, own, every, narrow, narrow],
        [narrow, narrow],
        [spectra(FAR), own],
        (far_ahead, ahead_head, ahead_tail, grad_spec, filter_spec, key_in, value_in),
    )
    return query_grad, key_grad, value_grad, filter_grad * (1.0 / math.sqrt(total_rows * ROW))


def solution(mesh):
    tokens = P(("groups", "seq"), "chan")
    return jax.shard_map(
        body,
        mesh=mesh,
        in_specs=(tokens,) * 4 + (P("groups"), P(None, "chan")),
        out_specs=(tokens,) * 4,
        check_vma=False,
    )
```

```python
import functools
import math

import jax
import jax.numpy as jnp
import ml_dtypes
import numpy as np
from jax import lax
from jax.experimental import pallas as pl
from jax.experimental.pallas import tpu as pltpu
from jax.sharding import PartitionSpec as P

ROW = 128
MOST = 8
HALF = ROW // 2
OWN = 4
FAR = 2
CHUNK = 32
G = 20_000_000_000
CP, C0, C1, C2, C3 = 1, G, G // 2, G // 4, G // 4


def split_table(table):
    high = table.astype(ml_dtypes.bfloat16)
    low = (table - high.astype(np.float64)).astype(ml_dtypes.bfloat16)
    return high, low


def dft_tables():
    order = np.concatenate([np.arange(0, ROW, 2), np.arange(1, ROW, 2)])
    phase = np.outer(2 * order + 1, np.arange(ROW)) % (4 * ROW) * (math.pi / (2 * ROW))
    forward = np.concatenate([np.cos(phase), -np.sin(phase)], axis=0)
    high, low = split_table(forward)
    inv_high, inv_low = split_table(forward.T / ROW)
    return (
        np.concatenate([high, high], axis=1),
        low,
        np.concatenate([inv_high, inv_low], axis=0),
    )


def halves(value):
    high = value.astype(jnp.bfloat16)
    low = (value - high.astype(jnp.float32)).astype(jnp.bfloat16)
    return high, low


def matmul(one, two):
    return jnp.dot(one, two, preferred_element_type=jnp.float32)


def transform(signal, forward_ref, forward_low_ref):
    high, low = halves(signal)
    return matmul(forward_ref[...], jnp.concatenate([high, low], axis=0)) + matmul(
        forward_low_ref[...], high
    )


def untransform(spectrum, inverse_ref):
    high, low = halves(spectrum)
    both = matmul(inverse_ref[...], high)
    return both[:ROW] + (both[ROW:] + matmul(inverse_ref[pl.ds(0, ROW), :], low))


def turned(spectrum, sign):
    real, imag = spectrum[:ROW], spectrum[ROW:]
    plus = lambda part: jnp.concatenate([part[:HALF], -part[HALF:]], axis=0)
    minus = lambda part: jnp.concatenate([-part[:HALF], part[HALF:]], axis=0)
    if sign > 0:
        return jnp.concatenate([minus(imag), plus(real)], axis=0)
    return jnp.concatenate([plus(imag), minus(real)], axis=0)


def multiply_add(total, offset, one_ref, one, two_ref, two):
    for part in range(4):
        real = pl.ds(part * 32, 32)
        imag = pl.ds(ROW + part * 32, 32)
        one_re, one_im = one_ref[one, real, :], one_ref[one, imag, :]
        two_re, two_im = two_ref[two, real, :], two_ref[two, imag, :]
        total[offset, real, :] += one_re * two_re + one_im * two_im
        total[offset, imag, :] += one_re * two_im - one_im * two_re


def own_kernel(
    table_ref,
    forward_ref,
    forward_low_ref,
    inverse_ref,
    query_ref,
    key_ref,
    value_ref,
    out_grad_ref,
    filter_ref,
    mixed_spec,
    grad_spec,
    filter_spec,
    first_ref,
    second_ref,
    near,
):
    wide = jnp.float32
    for row in range(OWN):
        rows = pl.ds(row * ROW, ROW)
        mixed_spec[row] = transform(
            key_ref[rows, :].astype(wide) * value_ref[rows, :].astype(wide),
            forward_ref,
            forward_low_ref,
        )
        grad_spec[row] = transform(
            out_grad_ref[rows, :].astype(wide) * query_ref[rows, :].astype(wide),
            forward_ref,
            forward_low_ref,
        )
    near[...] = jnp.zeros_like(near)
    for source in range(OWN):
        stop = jnp.minimum(table_ref[3 * OWN + source], OWN - source)

        @pl.loop(0, stop)
        def _(offset):
            multiply_add(near, offset, mixed_spec, source, grad_spec, source + offset)

    for block in range(OWN):
        spectrum = near[block]
        if block + 1 < OWN:
            spectrum = spectrum + turned(near[block + 1], -1)
        out_ref = (first_ref, second_ref)[block // 2]
        out_ref[pl.ds(block % 2 * ROW, ROW), :] = untransform(
            spectrum, inverse_ref
        )
    before = None
    for offset in range(MOST):
        plain = transform(filter_ref[pl.ds(offset * ROW, ROW), :], forward_ref, forward_low_ref)
        filter_spec[offset] = plain if before is None else plain + turned(before, 1)
        before = plain


def fill(spec_ref, used, pieces, tables):
    @pl.when(used)
    def _():
        for row, (refs, place) in enumerate(pieces):
            rows = pl.ds(place * ROW, ROW)
            signal = refs[0][rows, :].astype(jnp.float32)
            for ref in refs[1:]:
                signal = signal * ref[rows, :].astype(jnp.float32)
            spec_ref[row] = transform(signal, *tables)


def behind_pieces(head_ref, tail_ref):
    return [((head_ref,), 0)] + [((tail_ref,), row) for row in range(OWN - 1)]


def ahead_pieces(head_ref, tail_ref):
    return [((head_ref,), row) for row in range(OWN - 1)] + [((tail_ref,), 0)]


def pair_sums(ranges, owner, mixed_spec, grad_spec, spectrum):
    width = spectrum.shape[2]
    zeros = (jnp.zeros((CHUNK, width), jnp.float32),) * 2

    def gathered(offset, real, imag):
        def one_step(row, totals):
            one_re = mixed_spec[row + OWN, real, :]
            one_im = mixed_spec[row + OWN, imag, :]
            two_re = grad_spec[row + offset, real, :]
            two_im = grad_spec[row + offset, imag, :]
            return (
                totals[0] + (one_re * two_re + one_im * two_im),
                totals[1] + (one_re * two_im - one_im * two_re),
            )

        total = zeros
        for low, high in ranges.get(offset, ()):
            total = lax.fori_loop(low, high, one_step, total)
        return total

    for part in range(ROW // CHUNK):
        real = pl.ds(part * CHUNK, CHUNK)
        imag = pl.ds(ROW + part * CHUNK, CHUNK)
        sign = 1.0 if part * CHUNK < HALF else -1.0
        now_re, now_im = gathered(2 * owner, real, imag)
        for place in range(2):
            next_re, next_im = gathered(2 * owner + place + 1, real, imag)
            spectrum[place, real, :] = now_re + sign * next_im
            spectrum[place, imag, :] = now_im - sign * next_re
            now_re, now_im = next_re, next_im


def pair_kernel(
    table_ref,
    forward_ref,
    forward_low_ref,
    inverse_ref,
    behind_tail_ref,
    behind_head_ref,
    ahead_head_ref,
    ahead_tail_ref,
    query_ref,
    key_ref,
    value_ref,
    out_grad_ref,
    first_ref,
    second_ref,
    hand_ref,
    turn_ref,
    outward_ref,
    keep_ref,
    mixed_spec,
    grad_spec,
    spectrum,
):
    before_own = jnp.minimum(table_ref[0] - 1, OWN)
    from_own = table_ref[3 * OWN - 1] - 1
    before_next = jnp.minimum(table_ref[4 * OWN + 2 * MOST] - 1, OWN)
    from_next = jnp.minimum(table_ref[2 * OWN - 1] - 1, OWN)

    tables = (forward_ref, forward_low_ref)
    own_mixed = [((key_ref, value_ref), row) for row in range(OWN)]
    own_grad = [((out_grad_ref, query_ref), row) for row in range(OWN)]
    behind = behind_pieces(behind_head_ref, behind_tail_ref)
    ahead = ahead_pieces(ahead_head_ref, ahead_tail_ref)
    own_part, ahead_part = pl.ds(OWN, OWN), pl.ds(OWN, OWN)
    fill(mixed_spec, before_own > 0, behind, tables)
    fill(grad_spec, before_own > 0, own_grad, tables)
    fill(mixed_spec.at[own_part], before_next > 0, own_mixed, tables)
    fill(grad_spec.at[ahead_part], before_next > 0, ahead, tables)

    for owner in range(MOST // 2):
        use_back = table_ref[4 * OWN + 2 * owner] > 0
        use_front = table_ref[4 * OWN + MOST + 2 * owner] > 0
        ranges = {}
        for offset in range(max(1, 2 * owner), min(MOST, 2 * owner + 3)):
            low = jnp.maximum(-before_own, jnp.where(use_back, -offset, OWN - offset))
            high = jnp.minimum(0, jnp.minimum(from_own, 2 * OWN) - offset)
            next_low = jnp.maximum(OWN - before_next, OWN - offset)
            next_high = jnp.where(use_front, jnp.minimum(OWN, OWN + from_next - offset), 0)
            ranges[offset] = ((low, high), (next_low, next_high))
        busy = functools.reduce(
            jnp.logical_or, [high > low for both in ranges.values() for low, high in both]
        )
        role = table_ref[4 * OWN + 2 * MOST + 1 + owner]
        outs = (hand_ref, turn_ref, outward_ref, keep_ref)
        own_ref = (first_ref, second_ref)[owner] if owner < 2 else None
        for kind, out_ref in enumerate(outs):

            @pl.when(jnp.logical_and(role == kind, jnp.logical_not(busy)))
            def _():
                out_ref[...] = jnp.zeros_like(out_ref) if own_ref is None else own_ref[...]

        @pl.when(busy)
        def _():
            pair_sums(ranges, owner, mixed_spec, grad_spec, spectrum)
            for place in range(2):
                rows = pl.ds(place * ROW, ROW)
                taps = untransform(spectrum[place], inverse_ref)
                if own_ref is not None:
                    taps = taps + own_ref[rows, :]
                for kind, out_ref in enumerate(outs):

                    @pl.when(role == kind)
                    def _():
                        out_ref[rows, :] = taps


def forward_kernel(
    table_ref,
    forward_ref,
    forward_low_ref,
    inverse_ref,
    behind_ref,
    ahead_ref,
    filter_spec,
    right_ref,
    left_ref,
):
    right_ref[...] = behind_ref[pl.ds(ROW, 2 * ROW), :]
    left_ref[...] = ahead_ref[pl.ds(0, 2 * ROW), :]

    def parts(spectrum):
        return spectrum[:ROW], spectrum[ROW:]

    @pl.when(table_ref[4 * OWN + 2 * MOST] == MOST)
    def _():
        total_re, total_im = 0.0, 0.0
        for row in range(3):
            signal = behind_ref[pl.ds(row * ROW, ROW), :]
            one_re, one_im = parts(transform(signal, forward_ref, forward_low_ref))
            two_re, two_im = parts(filter_spec[3 - row])
            total_re = total_re + (one_re * two_re - one_im * two_im)
            total_im = total_im + (one_re * two_im + one_im * two_re)
        right_ref[pl.ds(0, ROW), :] = untransform(
            jnp.concatenate([total_re, total_im], axis=0), inverse_ref
        )

    @pl.when(table_ref[3 * OWN - 1] == MOST)
    def _():
        total_re, total_im = 0.0, 0.0
        for row in range(3):
            signal = ahead_ref[pl.ds(row * ROW, ROW), :]
            one_re, one_im = parts(transform(signal, forward_ref, forward_low_ref))
            two_re, two_im = parts(filter_spec[1 + row])
            total_re = total_re + (two_re * one_re + two_im * one_im)
            total_im = total_im + (two_re * one_im - two_im * one_re)
        left_ref[pl.ds(0, ROW), :] = untransform(
            jnp.concatenate([total_re, total_im], axis=0), inverse_ref
        )


def summed(counts, direction, pieces, filter_spec, width):
    reals, imags = [], []
    for part in range(4):
        real = pl.ds(part * 32, 32)
        imag = pl.ds(ROW + part * 32, 32)
        total = (jnp.zeros((32, width), jnp.float32),) * 2
        for count, (ref, first, low, high) in zip(counts, pieces):

            def one_step(offset, totals):
                row = first + direction * offset
                one_re, one_im = ref[row, real, :], ref[row, imag, :]
                two_re, two_im = filter_spec[offset, real, :], filter_spec[offset, imag, :]
                if direction < 0:
                    return (
                        totals[0] + (one_re * two_re - one_im * two_im),
                        totals[1] + (one_re * two_im + one_im * two_re),
                    )
                return (
                    totals[0] + (two_re * one_re + two_im * one_im),
                    totals[1] + (two_re * one_im - two_im * one_re),
                )

            total = lax.fori_loop(low, jnp.minimum(count, high), one_step, total)
        reals.append(total[0])
        imags.append(total[1])
    return jnp.concatenate(reals + imags, axis=0)


def query_kernel(
    table_ref,
    forward_ref,
    forward_low_ref,
    inverse_ref,
    far_ref,
    head_ref,
    tail_ref,
    own_spec,
    filter_spec,
    out_grad_ref,
    query_grad_ref,
    far_spec,
    behind_spec,
):
    reach = table_ref[0] - 1
    tables = (forward_ref, forward_low_ref)
    fill(behind_spec, reach > 0, behind_pieces(head_ref, tail_ref), tables)
    used = jnp.logical_and(reach > OWN, reach < MOST - 1)
    fill(far_spec, used, [((far_ref,), row) for row in range(FAR)], tables)

    for row in range(OWN):
        rows = pl.ds(row * ROW, ROW)
        pieces = (
            (own_spec, row, 0, row + 1),
            (behind_spec, row + OWN, row + 1, row + 1 + OWN),
            (far_spec, row + OWN + FAR, row + 1 + OWN, min(MOST, row + 1 + OWN + FAR)),
        )
        count = jnp.minimum(table_ref[row], MOST)
        whole = count == MOST
        counts = (count, count, jnp.where(whole, 0, count) if row == 0 else count)
        total = summed(counts, -1, pieces, filter_spec, far_ref.shape[1])
        convolved = untransform(total, inverse_ref)
        if row == 0:
            convolved = convolved + jnp.where(whole, far_ref[pl.ds(0, ROW), :], 0.0)
        query_grad_ref[rows, :] = (
            out_grad_ref[rows, :].astype(jnp.float32) * convolved
        ).astype(jnp.bfloat16)


def key_value_kernel(
    table_ref,
    forward_ref,
    forward_low_ref,
    inverse_ref,
    far_ref,
    head_ref,
    tail_ref,
    own_spec,
    filter_spec,
    key_ref,
    value_ref,
    key_grad_ref,
    value_grad_ref,
    far_spec,
    ahead_spec,
):
    reach = table_ref[2 * OWN - 1] - 1
    tables = (forward_ref, forward_low_ref)
    fill(ahead_spec, reach > 0, ahead_pieces(head_ref, tail_ref), tables)
    used = jnp.logical_and(reach > OWN, reach < MOST - 1)
    fill(far_spec, used, [((far_ref,), row) for row in range(FAR)], tables)

    for row in range(OWN):
        rows = pl.ds(row * ROW, ROW)
        pieces = (
            (own_spec, row, 0, OWN - row),
            (ahead_spec, row - OWN, OWN - row, 2 * OWN - row),
            (far_spec, row - 2 * OWN, 2 * OWN - row, min(MOST, 2 * OWN + FAR - row)),
        )
        count = jnp.minimum(table_ref[OWN + row], MOST)
        last = row == OWN - 1
        whole = count == MOST
        counts = (count, count, jnp.where(whole, 0, count) if last else count)
        total = summed(counts, 1, pieces, filter_spec, far_ref.shape[1])
        mixed_grad = untransform(total, inverse_ref)
        if last:
            mixed_grad = mixed_grad + jnp.where(whole, far_ref[pl.ds(0, ROW), :], 0.0)
        key_grad_ref[rows, :] = (
            mixed_grad * value_ref[rows, :].astype(jnp.float32)
        ).astype(jnp.bfloat16)
        value_grad_ref[rows, :] = (
            mixed_grad * key_ref[rows, :].astype(jnp.float32)
        ).astype(jnp.bfloat16)


ROLES = np.array([[3, 0, 1, 2], [2, 3, 1, 0], [0, 1, 3, 2], [0, 1, 2, 3]], np.int32)


def scalars(document_rows, first_row, owner_split):
    count = document_rows.shape[0]
    index = jnp.arange(count, dtype=jnp.int32)
    ends = jnp.sum(
        jnp.where(index[None, :] <= index[:, None], document_rows[None, :], 0), axis=1
    )
    row = first_row + jnp.arange(-OWN, OWN + 1, dtype=jnp.int32)
    passed = ends[None, :] <= row[:, None]
    starts = jnp.max(jnp.where(passed, ends[None, :], 0), axis=1)
    stops = jnp.min(jnp.where(passed, jnp.int32(1 << 20), ends[None, :]), axis=1)
    ahead = jnp.where(row >= 0, stops - row, 0)
    behind = row + 1 - starts
    seq = first_row // OWN
    block = jnp.arange(MOST, dtype=jnp.int32)
    index4 = jnp.arange(4, dtype=jnp.int32)
    if owner_split:
        owner = block * owner_split // MOST
        use_back = (owner >= seq).astype(jnp.int32)
        use_front = (owner <= seq).astype(jnp.int32)
        roles = jnp.sum(jnp.where(index4[:, None] == seq, ROLES, 0), axis=0)
    else:
        use_back = jnp.ones_like(block)
        use_front = jnp.zeros_like(block)
        roles = index4
    ahead = ahead[: 2 * OWN]
    return jnp.concatenate(
        [behind[OWN : 2 * OWN], ahead[OWN:], ahead, use_back, use_front, behind[2 * OWN :], roles]
    )


def add_kernel(one_ref, two_ref, out_ref):
    out_ref[...] = one_ref[...] + two_ref[...]


def step(rows, by, first=0):
    length = lax.axis_size("seq")
    pairs = [(i, i + 1) for i in range(first, length - 1)]
    if by < 0:
        pairs = [(length - 1 - i, length - 1 - j) for i, j in pairs]
    return lax.ppermute(rows, "seq", pairs)


def first_sums(early, roles, rows_far):
    hand, turn, outward, keep = roles
    in_first = lax.ppermute(early[0], "seq", [(3, 2)])
    in_second = lax.ppermute(early[1], "seq", [(3, 2)])
    in_end = lax.ppermute(early[1], "seq", [(0, 1)])
    hand, turn, rows_far = lax.optimization_barrier((hand + in_first, turn, rows_far))
    in_far = lax.ppermute(hand, "seq", [(1, 3), (2, 0)])
    in_side = lax.ppermute(outward, "seq", [(2, 3), (1, 0)])
    return (keep + in_end + in_far, in_side, turn, in_second), rows_far


def last_sums(pending):
    kept, in_side, turn, in_second = pending
    block = pl.BlockSpec((ROW, turn.shape[1]), lambda j: (j, 0))
    turn = pl.pallas_call(
        add_kernel,
        grid=(turn.shape[0] // ROW,),
        in_specs=[block] * 2,
        out_specs=block,
        out_shape=jax.ShapeDtypeStruct(turn.shape, turn.dtype),
        compiler_params=pltpu.CompilerParams(vmem_limit_bytes=8 * 1024 * 1024),
        cost_estimate=pl.CostEstimate(flops=1, bytes_accessed=1, transcendentals=0),
        name="add_terms",
    )(turn, in_second)
    return kept + in_side + lax.ppermute(turn, "seq", [(1, 2), (2, 1)])


def body(query_in, key_in, value_in, out_grad, document_rows, long_filter):
    seq_count = lax.axis_size("seq")
    tokens, channels = query_in.shape
    total_rows = tokens // ROW * seq_count
    wide = jnp.float32
    far = (MOST - 1 - OWN) * ROW

    def mixed(low, high):
        return key_in[low:high].astype(wide) * value_in[low:high].astype(wide)

    def upstream(low, high):
        return out_grad[low:high].astype(wide) * query_in[low:high].astype(wide)

    behind_tail = step(mixed(ROW, tokens), 1)
    ahead_head = step(upstream(0, far), -1)
    behind_head = step(mixed(0, ROW), 1)
    ahead_tail = step(upstream(far, tokens), -1)
    first_row = lax.axis_index("seq") * OWN
    table = scalars(document_rows, first_row, 4 if seq_count == 4 else 0)
    tables = dft_tables()

    narrow_tile, wide_tile = min(channels, 256), min(channels, 512)
    fixed = [pl.BlockSpec(memory_space=pltpu.SMEM)] + [
        pl.BlockSpec(t.shape, lambda j: (0, 0)) for t in tables
    ]

    def flat(rows, dtype=wide):
        return (
            lambda tile: pl.BlockSpec((rows, tile), lambda j: (0, j)),
            jax.ShapeDtypeStruct((rows, channels), dtype),
            None,
        )

    def spectra(rows):
        return (
            lambda tile: pl.BlockSpec((rows, 2 * ROW, tile), lambda j: (0, 0, j)),
            jax.ShapeDtypeStruct((rows, 2 * ROW, channels), wide),
            lambda tile: pltpu.VMEM((rows, 2 * ROW, tile), wide),
        )

    def call(kernel, cost, ins, outs, scratch, operands, tile=narrow_tile):
        return pl.pallas_call(
            kernel,
            grid=(channels // tile,),
            in_specs=fixed + [i[0](tile) for i in ins],
            out_specs=[o[0](tile) for o in outs],
            out_shape=[o[1] for o in outs],
            scratch_shapes=[x[2](tile) for x in scratch],
            compiler_params=pltpu.CompilerParams(vmem_limit_bytes=52 * 1024 * 1024),
            cost_estimate=pl.CostEstimate(
                flops=cost, bytes_accessed=1_000_000, transcendentals=0
            ),
        )(table, *tables, *operands)

    narrow = flat(tokens, jnp.bfloat16)
    share, row, rows = flat(2 * ROW), flat(ROW), flat(far)
    own, every = spectra(OWN), spectra(MOST)
    mixed_spec, grad_spec, filter_spec, first, second = call(
        own_kernel,
        C0,
        [narrow] * 4 + [flat(MOST * ROW)],
        [own, own, every, share, share],
        [own],
        (query_in, key_in, value_in, out_grad, long_filter),
    )
    half = flat(2 * ROW)
    upper = (
        lambda tile: pl.BlockSpec((OWN, 2 * ROW, tile), lambda j: (1, 0, j)),
        every[1],
        None,
    )
    right, left = call(
        forward_kernel,
        CP,
        [rows, rows, upper],
        [half, half],
        [],
        (behind_tail, ahead_head, filter_spec),
    )
    far_behind = step(right, 1, first=1)
    far_ahead = step(left, -1, first=1)
    roles = call(
        pair_kernel,
        C1,
        [rows, row, rows, row] + [narrow] * 4 + [share, share],
        [share] * 4,
        [every] * 2 + [spectra(2)],
        (behind_tail, behind_head, ahead_head, ahead_tail)
        + (query_in, key_in, value_in, out_grad, first, second),
        wide_tile,
    )
    if seq_count == 4:
        pending, (far_behind, far_ahead) = first_sums(
            (first, second), roles, (far_behind, far_ahead)
        )
    (query_grad,) = call(
        query_kernel,
        C2,
        [half, row, rows, own, every, narrow],
        [narrow],
        [spectra(FAR), own],
        (far_behind, behind_head, behind_tail, mixed_spec, filter_spec, out_grad),
    )
    if seq_count == 4:
        kept, in_side, turn, in_second = pending
        turn, query_grad = lax.optimization_barrier((turn, query_grad))
        kept, far_ahead = lax.optimization_barrier((kept, far_ahead))
        filter_grad = last_sums((kept, in_side, turn, in_second))
    else:
        filter_grad = lax.psum_scatter(
            jnp.concatenate(roles, axis=0), "seq", scatter_dimension=0, tiled=True
        )
    key_grad, value_grad = call(
        key_value_kernel,
        C3,
        [half, rows, row, own, every, narrow, narrow],
        [narrow, narrow],
        [spectra(FAR), own],
        (far_ahead, ahead_head, ahead_tail, grad_spec, filter_spec, key_in, value_in),
    )
    return query_grad, key_grad, value_grad, filter_grad * (1.0 / math.sqrt(total_rows * ROW))


def solution(mesh):
    tokens = P(("groups", "seq"), "chan")
    return jax.shard_map(
        body,
        mesh=mesh,
        in_specs=(tokens,) * 4 + (P("groups"), P(None, "chan")),
        out_specs=(tokens,) * 4,
        check_vma=False,
    )
```

```python
import functools
import math

import jax
import jax.numpy as jnp
import ml_dtypes
import numpy as np
from jax import lax
from jax.experimental import pallas as pl
from jax.experimental.pallas import tpu as pltpu
from jax.sharding import PartitionSpec as P

ROW = 128
MOST = 8
HALF = ROW // 2
OWN = 4
FAR = 2
CHUNK = 32
G = 20_000_000_000
CP, C0, C1, C2, C3 = 1, G, G // 2, G // 4, G // 4


def split_table(table):
    high = table.astype(ml_dtypes.bfloat16)
    low = (table - high.astype(np.float64)).astype(ml_dtypes.bfloat16)
    return high, low


def dft_tables():
    order = np.concatenate([np.arange(0, ROW, 2), np.arange(1, ROW, 2)])
    phase = np.outer(2 * order + 1, np.arange(ROW)) % (4 * ROW) * (math.pi / (2 * ROW))
    forward = np.concatenate([np.cos(phase), -np.sin(phase)], axis=0)
    high, low = split_table(forward)
    inv_high, inv_low = split_table(forward.T / ROW)
    return (
        np.concatenate([high, high], axis=1),
        low,
        np.concatenate([inv_high, inv_low], axis=0),
    )


def halves(value):
    high = value.astype(jnp.bfloat16)
    low = (value - high.astype(jnp.float32)).astype(jnp.bfloat16)
    return high, low


def matmul(one, two):
    return jnp.dot(one, two, preferred_element_type=jnp.float32)


def transform(signal, forward_ref, forward_low_ref):
    high, low = halves(signal)
    return matmul(forward_ref[...], jnp.concatenate([high, low], axis=0)) + matmul(
        forward_low_ref[...], high
    )


def untransform(spectrum, inverse_ref):
    high, low = halves(spectrum)
    both = matmul(inverse_ref[...], high)
    return both[:ROW] + (both[ROW:] + matmul(inverse_ref[pl.ds(0, ROW), :], low))


def turned(spectrum, sign):
    real, imag = spectrum[:ROW], spectrum[ROW:]
    plus = lambda part: jnp.concatenate([part[:HALF], -part[HALF:]], axis=0)
    minus = lambda part: jnp.concatenate([-part[:HALF], part[HALF:]], axis=0)
    if sign > 0:
        return jnp.concatenate([minus(imag), plus(real)], axis=0)
    return jnp.concatenate([plus(imag), minus(real)], axis=0)


def multiply_add(total, offset, one_ref, one, two_ref, two):
    for part in range(4):
        real = pl.ds(part * 32, 32)
        imag = pl.ds(ROW + part * 32, 32)
        one_re, one_im = one_ref[one, real, :], one_ref[one, imag, :]
        two_re, two_im = two_ref[two, real, :], two_ref[two, imag, :]
        total[offset, real, :] += one_re * two_re + one_im * two_im
        total[offset, imag, :] += one_re * two_im - one_im * two_re


def own_kernel(
    table_ref,
    forward_ref,
    forward_low_ref,
    inverse_ref,
    query_ref,
    key_ref,
    value_ref,
    out_grad_ref,
    filter_ref,
    mixed_spec,
    grad_spec,
    filter_spec,
    first_ref,
    second_ref,
    near,
):
    wide = jnp.float32
    for row in range(OWN):
        rows = pl.ds(row * ROW, ROW)
        mixed_spec[row] = transform(
            key_ref[rows, :].astype(wide) * value_ref[rows, :].astype(wide),
            forward_ref,
            forward_low_ref,
        )
        grad_spec[row] = transform(
            out_grad_ref[rows, :].astype(wide) * query_ref[rows, :].astype(wide),
            forward_ref,
            forward_low_ref,
        )
    near[...] = jnp.zeros_like(near)
    for source in range(OWN):
        stop = jnp.minimum(table_ref[3 * OWN + source], OWN - source)

        @pl.loop(0, stop)
        def _(offset):
            multiply_add(near, offset, mixed_spec, source, grad_spec, source + offset)

    for block in range(OWN):
        spectrum = near[block]
        if block + 1 < OWN:
            spectrum = spectrum + turned(near[block + 1], -1)
        out_ref = (first_ref, second_ref)[block // 2]
        out_ref[pl.ds(block % 2 * ROW, ROW), :] = untransform(
            spectrum, inverse_ref
        )
    before = None
    for offset in range(MOST):
        plain = transform(filter_ref[pl.ds(offset * ROW, ROW), :], forward_ref, forward_low_ref)
        filter_spec[offset] = plain if before is None else plain + turned(before, 1)
        before = plain


def fill(spec_ref, used, pieces, tables):
    @pl.when(used)
    def _():
        for row, (refs, place) in enumerate(pieces):
            rows = pl.ds(place * ROW, ROW)
            signal = refs[0][rows, :].astype(jnp.float32)
            for ref in refs[1:]:
                signal = signal * ref[rows, :].astype(jnp.float32)
            spec_ref[row] = transform(signal, *tables)


def behind_pieces(head_ref, tail_ref):
    return [((head_ref,), 0)] + [((tail_ref,), row) for row in range(OWN - 1)]


def ahead_pieces(head_ref, tail_ref):
    return [((head_ref,), row) for row in range(OWN - 1)] + [((tail_ref,), 0)]


def pair_sums(ranges, owner, mixed_spec, grad_spec, spectrum):
    width = spectrum.shape[2]
    zeros = (jnp.zeros((CHUNK, width), jnp.float32),) * 2

    def gathered(offset, real, imag):
        def one_step(row, totals):
            one_re = mixed_spec[row + OWN, real, :]
            one_im = mixed_spec[row + OWN, imag, :]
            two_re = grad_spec[row + offset, real, :]
            two_im = grad_spec[row + offset, imag, :]
            return (
                totals[0] + (one_re * two_re + one_im * two_im),
                totals[1] + (one_re * two_im - one_im * two_re),
            )

        total = zeros
        for low, high in ranges.get(offset, ()):
            total = lax.fori_loop(low, high, one_step, total)
        return total

    for part in range(ROW // CHUNK):
        real = pl.ds(part * CHUNK, CHUNK)
        imag = pl.ds(ROW + part * CHUNK, CHUNK)
        sign = 1.0 if part * CHUNK < HALF else -1.0
        now_re, now_im = gathered(2 * owner, real, imag)
        for place in range(2):
            next_re, next_im = gathered(2 * owner + place + 1, real, imag)
            spectrum[place, real, :] = now_re + sign * next_im
            spectrum[place, imag, :] = now_im - sign * next_re
            now_re, now_im = next_re, next_im


def pair_kernel(
    table_ref,
    forward_ref,
    forward_low_ref,
    inverse_ref,
    behind_tail_ref,
    behind_head_ref,
    ahead_head_ref,
    ahead_tail_ref,
    query_ref,
    key_ref,
    value_ref,
    out_grad_ref,
    first_ref,
    second_ref,
    hand_ref,
    turn_ref,
    outward_ref,
    keep_ref,
    mixed_spec,
    grad_spec,
    spectrum,
):
    before_own = jnp.minimum(table_ref[0] - 1, OWN)
    from_own = table_ref[3 * OWN - 1] - 1
    before_next = jnp.minimum(table_ref[4 * OWN + 2 * MOST] - 1, OWN)
    from_next = jnp.minimum(table_ref[2 * OWN - 1] - 1, OWN)

    tables = (forward_ref, forward_low_ref)
    own_mixed = [((key_ref, value_ref), row) for row in range(OWN)]
    own_grad = [((out_grad_ref, query_ref), row) for row in range(OWN)]
    behind = behind_pieces(behind_head_ref, behind_tail_ref)
    ahead = ahead_pieces(ahead_head_ref, ahead_tail_ref)
    own_part, ahead_part = pl.ds(OWN, OWN), pl.ds(OWN, OWN)
    fill(mixed_spec, before_own > 0, behind, tables)
    fill(grad_spec, before_own > 0, own_grad, tables)
    fill(mixed_spec.at[own_part], before_next > 0, own_mixed, tables)
    fill(grad_spec.at[ahead_part], before_next > 0, ahead, tables)

    for owner in range(MOST // 2):
        use_back = table_ref[4 * OWN + 2 * owner] > 0
        use_front = table_ref[4 * OWN + MOST + 2 * owner] > 0
        ranges = {}
        for offset in range(max(1, 2 * owner), min(MOST, 2 * owner + 3)):
            low = jnp.maximum(-before_own, jnp.where(use_back, -offset, OWN - offset))
            high = jnp.minimum(0, jnp.minimum(from_own, 2 * OWN) - offset)
            next_low = jnp.maximum(OWN - before_next, OWN - offset)
            next_high = jnp.where(use_front, jnp.minimum(OWN, OWN + from_next - offset), 0)
            ranges[offset] = ((low, high), (next_low, next_high))
        busy = functools.reduce(
            jnp.logical_or, [high > low for both in ranges.values() for low, high in both]
        )
        role = table_ref[4 * OWN + 2 * MOST + 1 + owner]
        outs = (hand_ref, turn_ref, outward_ref, keep_ref)
        own_ref = (first_ref, second_ref)[owner] if owner < 2 else None
        for kind, out_ref in enumerate(outs):

            @pl.when(jnp.logical_and(role == kind, jnp.logical_not(busy)))
            def _():
                out_ref[...] = jnp.zeros_like(out_ref) if own_ref is None else own_ref[...]

        @pl.when(busy)
        def _():
            pair_sums(ranges, owner, mixed_spec, grad_spec, spectrum)
            for place in range(2):
                rows = pl.ds(place * ROW, ROW)
                taps = untransform(spectrum[place], inverse_ref)
                if own_ref is not None:
                    taps = taps + own_ref[rows, :]
                for kind, out_ref in enumerate(outs):

                    @pl.when(role == kind)
                    def _():
                        out_ref[rows, :] = taps


def forward_kernel(
    table_ref,
    forward_ref,
    forward_low_ref,
    inverse_ref,
    behind_ref,
    ahead_ref,
    filter_spec,
    right_ref,
    left_ref,
):
    right_ref[...] = behind_ref[pl.ds(ROW, 2 * ROW), :]
    left_ref[...] = ahead_ref[pl.ds(0, 2 * ROW), :]

    def parts(spectrum):
        return spectrum[:ROW], spectrum[ROW:]

    @pl.when(table_ref[4 * OWN + 2 * MOST] == MOST)
    def _():
        total_re, total_im = 0.0, 0.0
        for row in range(3):
            signal = behind_ref[pl.ds(row * ROW, ROW), :]
            one_re, one_im = parts(transform(signal, forward_ref, forward_low_ref))
            two_re, two_im = parts(filter_spec[3 - row])
            total_re = total_re + (one_re * two_re - one_im * two_im)
            total_im = total_im + (one_re * two_im + one_im * two_re)
        right_ref[pl.ds(0, ROW), :] = untransform(
            jnp.concatenate([total_re, total_im], axis=0), inverse_ref
        )

    @pl.when(table_ref[3 * OWN - 1] == MOST)
    def _():
        total_re, total_im = 0.0, 0.0
        for row in range(3):
            signal = ahead_ref[pl.ds(row * ROW, ROW), :]
            one_re, one_im = parts(transform(signal, forward_ref, forward_low_ref))
            two_re, two_im = parts(filter_spec[1 + row])
            total_re = total_re + (two_re * one_re + two_im * one_im)
            total_im = total_im + (two_re * one_im - two_im * one_re)
        left_ref[pl.ds(0, ROW), :] = untransform(
            jnp.concatenate([total_re, total_im], axis=0), inverse_ref
        )


def summed(counts, direction, pieces, filter_spec, width):
    reals, imags = [], []
    for part in range(4):
        real = pl.ds(part * 32, 32)
        imag = pl.ds(ROW + part * 32, 32)
        total = (jnp.zeros((32, width), jnp.float32),) * 2
        for count, (ref, first, low, high) in zip(counts, pieces):

            def one_step(offset, totals):
                row = first + direction * offset
                one_re, one_im = ref[row, real, :], ref[row, imag, :]
                two_re, two_im = filter_spec[offset, real, :], filter_spec[offset, imag, :]
                if direction < 0:
                    return (
                        totals[0] + (one_re * two_re - one_im * two_im),
                        totals[1] + (one_re * two_im + one_im * two_re),
                    )
                return (
                    totals[0] + (two_re * one_re + two_im * one_im),
                    totals[1] + (two_re * one_im - two_im * one_re),
                )

            total = lax.fori_loop(low, jnp.minimum(count, high), one_step, total)
        reals.append(total[0])
        imags.append(total[1])
    return jnp.concatenate(reals + imags, axis=0)


def query_kernel(
    table_ref,
    forward_ref,
    forward_low_ref,
    inverse_ref,
    far_ref,
    head_ref,
    tail_ref,
    own_spec,
    filter_spec,
    out_grad_ref,
    query_grad_ref,
    far_spec,
    behind_spec,
):
    reach = table_ref[0] - 1
    tables = (forward_ref, forward_low_ref)
    fill(behind_spec, reach > 0, behind_pieces(head_ref, tail_ref), tables)
    used = jnp.logical_and(reach > OWN, reach < MOST - 1)
    fill(far_spec, used, [((far_ref,), row) for row in range(FAR)], tables)

    for row in range(OWN):
        rows = pl.ds(row * ROW, ROW)
        pieces = (
            (own_spec, row, 0, row + 1),
            (behind_spec, row + OWN, row + 1, row + 1 + OWN),
            (far_spec, row + OWN + FAR, row + 1 + OWN, min(MOST, row + 1 + OWN + FAR)),
        )
        count = jnp.minimum(table_ref[row], MOST)
        whole = count == MOST
        counts = (count, count, jnp.where(whole, 0, count) if row == 0 else count)
        total = summed(counts, -1, pieces, filter_spec, far_ref.shape[1])
        convolved = untransform(total, inverse_ref)
        if row == 0:
            convolved = convolved + jnp.where(whole, far_ref[pl.ds(0, ROW), :], 0.0)
        query_grad_ref[rows, :] = (
            out_grad_ref[rows, :].astype(jnp.float32) * convolved
        ).astype(jnp.bfloat16)


def key_value_kernel(
    table_ref,
    forward_ref,
    forward_low_ref,
    inverse_ref,
    far_ref,
    head_ref,
    tail_ref,
    own_spec,
    filter_spec,
    key_ref,
    value_ref,
    key_grad_ref,
    value_grad_ref,
    far_spec,
    ahead_spec,
):
    reach = table_ref[2 * OWN - 1] - 1
    tables = (forward_ref, forward_low_ref)
    fill(ahead_spec, reach > 0, ahead_pieces(head_ref, tail_ref), tables)
    used = jnp.logical_and(reach > OWN, reach < MOST - 1)
    fill(far_spec, used, [((far_ref,), row) for row in range(FAR)], tables)

    for row in range(OWN):
        rows = pl.ds(row * ROW, ROW)
        pieces = (
            (own_spec, row, 0, OWN - row),
            (ahead_spec, row - OWN, OWN - row, 2 * OWN - row),
            (far_spec, row - 2 * OWN, 2 * OWN - row, min(MOST, 2 * OWN + FAR - row)),
        )
        count = jnp.minimum(table_ref[OWN + row], MOST)
        last = row == OWN - 1
        whole = count == MOST
        counts = (count, count, jnp.where(whole, 0, count) if last else count)
        total = summed(counts, 1, pieces, filter_spec, far_ref.shape[1])
        mixed_grad = untransform(total, inverse_ref)
        if last:
            mixed_grad = mixed_grad + jnp.where(whole, far_ref[pl.ds(0, ROW), :], 0.0)
        key_grad_ref[rows, :] = (
            mixed_grad * value_ref[rows, :].astype(jnp.float32)
        ).astype(jnp.bfloat16)
        value_grad_ref[rows, :] = (
            mixed_grad * key_ref[rows, :].astype(jnp.float32)
        ).astype(jnp.bfloat16)


ROLES = np.array([[3, 0, 1, 2], [2, 3, 1, 0], [0, 1, 3, 2], [0, 1, 2, 3]], np.int32)


def scalars(document_rows, first_row, owner_split):
    count = document_rows.shape[0]
    index = jnp.arange(count, dtype=jnp.int32)
    ends = jnp.sum(
        jnp.where(index[None, :] <= index[:, None], document_rows[None, :], 0), axis=1
    )
    row = first_row + jnp.arange(-OWN, OWN + 1, dtype=jnp.int32)
    passed = ends[None, :] <= row[:, None]
    starts = jnp.max(jnp.where(passed, ends[None, :], 0), axis=1)
    stops = jnp.min(jnp.where(passed, jnp.int32(1 << 20), ends[None, :]), axis=1)
    ahead = jnp.where(row >= 0, stops - row, 0)
    behind = row + 1 - starts
    seq = first_row // OWN
    block = jnp.arange(MOST, dtype=jnp.int32)
    index4 = jnp.arange(4, dtype=jnp.int32)
    if owner_split:
        owner = block * owner_split // MOST
        use_back = (owner >= seq).astype(jnp.int32)
        use_front = (owner <= seq).astype(jnp.int32)
        roles = jnp.sum(jnp.where(index4[:, None] == seq, ROLES, 0), axis=0)
    else:
        use_back = jnp.ones_like(block)
        use_front = jnp.zeros_like(block)
        roles = index4
    ahead = ahead[: 2 * OWN]
    return jnp.concatenate(
        [behind[OWN : 2 * OWN], ahead[OWN:], ahead, use_back, use_front, behind[2 * OWN :], roles]
    )


def add_kernel(one_ref, two_ref, out_ref):
    out_ref[...] = one_ref[...] + two_ref[...]


def step(rows, by, first=0):
    length = lax.axis_size("seq")
    pairs = [(i, i + 1) for i in range(first, length - 1)]
    if by < 0:
        pairs = [(length - 1 - i, length - 1 - j) for i, j in pairs]
    return lax.ppermute(rows, "seq", pairs)


def first_sums(early, roles, rows_far):
    hand, turn, outward, keep = roles
    in_first = lax.ppermute(early[0], "seq", [(3, 2)])
    in_second = lax.ppermute(early[1], "seq", [(3, 2)])
    hand, turn, end, rows_far = lax.optimization_barrier(
        (hand + in_first, turn, early[1], rows_far)
    )
    in_far = lax.ppermute(hand, "seq", [(1, 3), (2, 0)])
    in_side = lax.ppermute(outward, "seq", [(2, 3), (1, 0)])
    in_end = lax.ppermute(end, "seq", [(0, 1)])
    return (keep + in_far, in_side + in_end, turn, in_second), rows_far


def last_sums(pending):
    kept, in_side, turn, in_second = pending
    block = pl.BlockSpec((ROW, turn.shape[1]), lambda j: (j, 0))
    turn = pl.pallas_call(
        add_kernel,
        grid=(turn.shape[0] // ROW,),
        in_specs=[block] * 2,
        out_specs=block,
        out_shape=jax.ShapeDtypeStruct(turn.shape, turn.dtype),
        compiler_params=pltpu.CompilerParams(vmem_limit_bytes=8 * 1024 * 1024),
        cost_estimate=pl.CostEstimate(flops=1, bytes_accessed=1, transcendentals=0),
        name="add_terms",
    )(turn, in_second)
    return kept + in_side + lax.ppermute(turn, "seq", [(1, 2), (2, 1)])


def body(query_in, key_in, value_in, out_grad, document_rows, long_filter):
    seq_count = lax.axis_size("seq")
    tokens, channels = query_in.shape
    total_rows = tokens // ROW * seq_count
    wide = jnp.float32
    far = (MOST - 1 - OWN) * ROW

    def mixed(low, high):
        return key_in[low:high].astype(wide) * value_in[low:high].astype(wide)

    def upstream(low, high):
        return out_grad[low:high].astype(wide) * query_in[low:high].astype(wide)

    behind_tail = step(mixed(ROW, tokens), 1)
    ahead_head = step(upstream(0, far), -1)
    behind_head = step(mixed(0, ROW), 1)
    ahead_tail = step(upstream(far, tokens), -1)
    first_row = lax.axis_index("seq") * OWN
    table = scalars(document_rows, first_row, 4 if seq_count == 4 else 0)
    tables = dft_tables()

    narrow_tile, wide_tile = min(channels, 256), min(channels, 512)
    fixed = [pl.BlockSpec(memory_space=pltpu.SMEM)] + [
        pl.BlockSpec(t.shape, lambda j: (0, 0)) for t in tables
    ]

    def flat(rows, dtype=wide):
        return (
            lambda tile: pl.BlockSpec((rows, tile), lambda j: (0, j)),
            jax.ShapeDtypeStruct((rows, channels), dtype),
            None,
        )

    def spectra(rows):
        return (
            lambda tile: pl.BlockSpec((rows, 2 * ROW, tile), lambda j: (0, 0, j)),
            jax.ShapeDtypeStruct((rows, 2 * ROW, channels), wide),
            lambda tile: pltpu.VMEM((rows, 2 * ROW, tile), wide),
        )

    def call(kernel, cost, ins, outs, scratch, operands, tile=narrow_tile):
        return pl.pallas_call(
            kernel,
            grid=(channels // tile,),
            in_specs=fixed + [i[0](tile) for i in ins],
            out_specs=[o[0](tile) for o in outs],
            out_shape=[o[1] for o in outs],
            scratch_shapes=[x[2](tile) for x in scratch],
            compiler_params=pltpu.CompilerParams(vmem_limit_bytes=52 * 1024 * 1024),
            cost_estimate=pl.CostEstimate(
                flops=cost, bytes_accessed=1_000_000, transcendentals=0
            ),
        )(table, *tables, *operands)

    narrow = flat(tokens, jnp.bfloat16)
    share, row, rows = flat(2 * ROW), flat(ROW), flat(far)
    own, every = spectra(OWN), spectra(MOST)
    mixed_spec, grad_spec, filter_spec, first, second = call(
        own_kernel,
        C0,
        [narrow] * 4 + [flat(MOST * ROW)],
        [own, own, every, share, share],
        [own],
        (query_in, key_in, value_in, out_grad, long_filter),
    )
    half = flat(2 * ROW)
    upper = (
        lambda tile: pl.BlockSpec((OWN, 2 * ROW, tile), lambda j: (1, 0, j)),
        every[1],
        None,
    )
    right, left = call(
        forward_kernel,
        CP,
        [rows, rows, upper],
        [half, half],
        [],
        (behind_tail, ahead_head, filter_spec),
    )
    far_behind = step(right, 1, first=1)
    far_ahead = step(left, -1, first=1)
    roles = call(
        pair_kernel,
        C1,
        [rows, row, rows, row] + [narrow] * 4 + [share, share],
        [share] * 4,
        [every] * 2 + [spectra(2)],
        (behind_tail, behind_head, ahead_head, ahead_tail)
        + (query_in, key_in, value_in, out_grad, first, second),
        wide_tile,
    )
    if seq_count == 4:
        pending, (far_behind, far_ahead) = first_sums(
            (first, second), roles, (far_behind, far_ahead)
        )
    (query_grad,) = call(
        query_kernel,
        C2,
        [half, row, rows, own, every, narrow],
        [narrow],
        [spectra(FAR), own],
        (far_behind, behind_head, behind_tail, mixed_spec, filter_spec, out_grad),
    )
    if seq_count == 4:
        kept, in_side, turn, in_second = pending
        turn, query_grad = lax.optimization_barrier((turn, query_grad))
        kept, far_ahead = lax.optimization_barrier((kept, far_ahead))
        filter_grad = last_sums((kept, in_side, turn, in_second))
    else:
        filter_grad = lax.psum_scatter(
            jnp.concatenate(roles, axis=0), "seq", scatter_dimension=0, tiled=True
        )
    key_grad, value_grad = call(
        key_value_kernel,
        C3,
        [half, rows, row, own, every, narrow, narrow],
        [narrow, narrow],
        [spectra(FAR), own],
        (far_ahead, ahead_head, ahead_tail, grad_spec, filter_spec, key_in, value_in),
    )
    return query_grad, key_grad, value_grad, filter_grad * (1.0 / math.sqrt(total_rows * ROW))


def solution(mesh):
    tokens = P(("groups", "seq"), "chan")
    return jax.shard_map(
        body,
        mesh=mesh,
        in_specs=(tokens,) * 4 + (P("groups"), P(None, "chan")),
        out_specs=(tokens,) * 4,
        check_vma=False,
    )
```
